32 devices in a mesh: groups: 2 (over y), ctx: 8 (over z, x), head: 2 (over core).
Axes of the slice: x: 2, y: 2, z: 4, core: 2. Of those that a mesh axis runs over, the one named last changes fastest.
Arguments:
- query_tensor: bfloat16 [2048, 4096], P(('groups', 'ctx'), 'head'), parts along dimension 0, may hold values from -110 to 110
- key_tensor: bfloat16 [2048, 1024], P(('groups', 'ctx'), 'head'), parts along dimension 0, may hold values from -6 to 6
- value_tensor: bfloat16 [2048, 1024], P(('groups', 'ctx'), 'head'), parts along dimension 0, may hold values from -6 to 6
- slash_offsets: int32 [16, 2], P(('groups', 'head')), parts along dimension 0, may hold values from 256 to 1023
- vertical_tiles: int32 [16, 2], P(('groups', 'head')), parts along dimension 0, may hold values from 0 to 7, as said below
- kept_rows: int32 [16, 32], P(('groups', 'ctx')), parts along dimension 0, may hold values from 0 to 127, as said below
- kept_count: int32 [16], P('groups'), parts along dimension 0, may hold values from 4 to 32, as said below
- out_weight: bfloat16 [2048, 4096], P('ctx', 'head'), may hold values from -0.09375 to 0.09375
Outputs:
- attended: bfloat16 [2048, 4096], P(('groups', 'ctx'), 'head'), parts along dimension 0
- projected: bfloat16 [256, 2048], P(('groups', 'ctx'), 'head'), parts along dimension 0
The draws below stay inside these ranges and needn't reach their ends.
There are 2 independent parts, one for each index of `groups`. The reference program is written for one: setup_inputs(seed, part) draws one part's arguments, and reference() takes and returns one part's arrays. A program takes and returns all parts, laid end to end along the dimension named above; an argument that names none is the same for every part. Nothing has to cross between parts.
Inputs may be any that keep to these rules, and one draw needn't show every extreme that they name: `vertical_tiles`: the tiles of one KV head differ. `kept_rows`: row c holds distinct local row indices of shard c; its first kept_count[c] entries are the kept rows in increasing order, the other entries are not kept. `kept_count`: each aligned block of 4 consecutive shards keeps exactly 64 rows in all.
All inputs are finite; a program needn't handle non-finite values.
Results may differ from the reference program's by a relative error of at most 0.0056.
Values may be sent and summed in bfloat16 or wider, within the bound.
No kernel may reach another device: no remote copies, remote signals or barrier semaphores. Data moves between devices by JAX's collectives and lax.ppermute only.
A program may use at most 64 MiB of HBM per device.

```python
import jax
import jax.numpy as jnp
from jax import lax

QUERY_HEAD_COUNT = 32
KEY_VALUE_HEADS = 8
HEAD_SIZE = 128
D_OUT = 2048
TOK_DEV = 128
SLASH_SPAN = 8
VTILES = 2
CONTEXT_SHARDS = 8
PROMPT_TOKENS = 1024
KEEP_DEV = 16
CAP = 32
KEPT = 128
LOCAL_BAND_KEYS = 256
SLASH_W = 128
VTILE = 128
SLASH_LIMIT = 1024


def paired_states(key):
    base = jax.random.fold_in(key, 7)
    random_key_one, random_key_two = jax.random.split(base, 2)
    key_sample = jnp.clip(jax.random.normal(random_key_one, (PROMPT_TOKENS, KEY_VALUE_HEADS * HEAD_SIZE), jnp.float32), -5.0, 5.0)
    query_draw = jnp.clip(jax.random.normal(random_key_two, (PROMPT_TOKENS, QUERY_HEAD_COUNT * HEAD_SIZE), jnp.float32), -5.0, 5.0)
    return (query_draw, key_sample)


def draw_query_tensor(key, part):
    return paired_states(key)[0].astype(jnp.bfloat16)


def draw_key_tensor(key, part):
    return paired_states(key)[1].astype(jnp.bfloat16)


def draw_slash_offsets(key, part):
    random_key_one, random_key_two = jax.random.split(jax.random.fold_in(key, 3))
    slash_shift_list = jax.random.randint(random_key_one, (KEY_VALUE_HEADS, 2), LOCAL_BAND_KEYS, SLASH_LIMIT, jnp.int32)
    picked_rows = jax.random.randint(random_key_two, (), 0, KEY_VALUE_HEADS * 2, jnp.int32)
    flag_value = jnp.arange(KEY_VALUE_HEADS * 2, dtype=jnp.int32).reshape(KEY_VALUE_HEADS, 2)
    return jnp.where(flag_value == picked_rows, SLASH_LIMIT - 1, slash_shift_list).astype(jnp.int32)


def draw_vertical_tiles(key, part):
    random_key_one, random_key_two = jax.random.split(jax.random.fold_in(key, 5))
    front_count = jax.random.randint(random_key_one, (KEY_VALUE_HEADS,), 0, CONTEXT_SHARDS, jnp.int32)
    gap_between = jax.random.randint(random_key_two, (KEY_VALUE_HEADS,), 1, CONTEXT_SHARDS, jnp.int32)
    return jnp.stack([front_count, (front_count + gap_between) % CONTEXT_SHARDS], 1).astype(jnp.int32)


def kept_plan(key):
    random_key_one, random_key_two, key_third, random_key_four = jax.random.split(jax.random.fold_in(key, 11), 4)
    blocks = CONTEXT_SHARDS // 4
    lower = KEEP_DEV // 4
    upper = 7 * KEEP_DEV // 8
    first_count = jax.random.randint(random_key_one, (blocks,), lower, upper + 1, jnp.int32)
    second_count = jax.random.randint(random_key_two, (blocks,), lower, upper + 1, jnp.int32)
    third_count = 2 * KEEP_DEV - first_count - second_count
    heavy = jnp.full((blocks,), 2 * KEEP_DEV, jnp.int32)
    stacked = jnp.stack([heavy, first_count, second_count, third_count], 1)
    order = jnp.argsort(jax.random.randint(key_third, (blocks, 4), 0, 1 << 20, jnp.int32) * 4 + jnp.arange(4, dtype=jnp.int32), axis=1)
    counts = jnp.take_along_axis(stacked, order, 1).reshape(CONTEXT_SHARDS).astype(jnp.int32)
    scores = jax.random.randint(random_key_four, (CONTEXT_SHARDS, TOK_DEV), 0, 1 << 20, jnp.int32) * TOK_DEV + jnp.arange(TOK_DEV, dtype=jnp.int32)
    picked = jnp.argsort(scores, axis=1)[:, :CAP].astype(jnp.int32)
    slot_ids = jnp.arange(CAP, dtype=jnp.int32)
    keyed = jnp.where(slot_ids[None, :] < counts[:, None], picked, picked + TOK_DEV)
    ordered = jnp.sort(keyed, axis=1)
    rows_out = jnp.where(ordered >= TOK_DEV, ordered - TOK_DEV, ordered)
    return (rows_out.astype(jnp.int32), counts)


def draw_kept_rows(key, part):
    return kept_plan(key)[0]


def draw_kept_count(key, part):
    return kept_plan(key)[1]


def block_levels(rng, shape, cuts, least, high):
    level, own = 1.0, jax.random.fold_in(rng, 6)
    for position, parts in cuts:
        draws = jnp.exp(jax.random.uniform(jax.random.fold_in(own, position), (parts,), jnp.float32, least / len(cuts), high / len(cuts)))
        level = level * jnp.repeat(draws, shape[position] // parts).reshape([-1 if axis == position else 1 for axis in range(len(shape))])
    return level


def noise(own_key, dims, deviation, most, cuts=(), held_as=jnp.bfloat16):
    gain = block_levels(own_key, dims, cuts, -0.22, 0.18) if cuts else 1.0
    values = jax.random.normal(own_key, dims, jnp.float32) * deviation * gain
    return jnp.minimum(jnp.maximum(values, -most), most).astype(held_as)


def setup_inputs(seed: int = 0, part: int = 0) -> dict:
    arg_keys = jax.random.split(jax.random.key(seed), 9)
    part_splits = jax.random.split(jax.random.fold_in(arg_keys[8], part), 9)
    return {
        "query_tensor": draw_query_tensor(jax.random.fold_in(jax.random.fold_in(arg_keys[8], part), 71), part),
        "key_tensor": draw_key_tensor(jax.random.fold_in(jax.random.fold_in(arg_keys[8], part), 71), part),
        "value_tensor": noise(part_splits[2], (PROMPT_TOKENS, KEY_VALUE_HEADS * HEAD_SIZE), 1.0, 6.0, ((0, 8), (1, 2))),
        "slash_offsets": draw_slash_offsets(jax.random.fold_in(jax.random.fold_in(arg_keys[8], part), 71), part),
        "vertical_tiles": draw_vertical_tiles(jax.random.fold_in(jax.random.fold_in(arg_keys[8], part), 71), part),
        "kept_rows": draw_kept_rows(jax.random.fold_in(jax.random.fold_in(arg_keys[8], part), 71), part),
        "kept_count": draw_kept_count(jax.random.fold_in(jax.random.fold_in(arg_keys[8], part), 71), part),
        "out_weight": noise(arg_keys[7], (D_OUT, QUERY_HEAD_COUNT * HEAD_SIZE), (QUERY_HEAD_COUNT * HEAD_SIZE) ** -0.5, 0.09375, ((0, 8), (1, 2))),
    }


def attend(query_rows, key_slab, value_slab, key_pos, query_pos, slash_shift_list, tile_list, column_kind, group_width):
    scores = jnp.dot(query_rows, key_slab.T, preferred_element_type=jnp.float32) * (key_slab.shape[-1] ** -0.5)
    distance = query_pos[:, None] - key_pos[None, :]
    key_tile = jnp.where(key_pos >= 0, key_pos // VTILE, -1)
    vertical = jnp.any(key_tile[:, None] == tile_list[None, :], axis=1)[None, :]
    in_band = (distance >= 0) & (distance < LOCAL_BAND_KEYS) & ~vertical
    first_slash = (distance >= slash_shift_list[0]) & (distance < slash_shift_list[0] + SLASH_W) & ~vertical
    second_slash = (distance >= slash_shift_list[1]) & (distance < slash_shift_list[1] + SLASH_W) & ~vertical
    earlier = in_band | first_slash
    kinds = column_kind[None, :]
    allowed = jnp.where(kinds == 0, in_band,
                        jnp.where(kinds == 1, first_slash & ~in_band,
                                  jnp.where(kinds == 2, second_slash & ~earlier,
                                            distance >= 0)))
    allowed = jnp.tile(allowed & (key_pos >= 0)[None, :], (group_width, 1))
    masked = jnp.where(allowed, scores, -jnp.inf)
    row_max = jnp.max(masked, axis=1, keepdims=True)
    weights = jnp.where(allowed, jnp.exp(masked - row_max), 0.0)
    row_sum = jnp.sum(weights, axis=1, keepdims=True)
    blended = jnp.dot(weights.astype(jnp.bfloat16), value_slab, preferred_element_type=jnp.float32)
    return (blended / row_sum).astype(jnp.bfloat16)


def reference(query_tensor, key_tensor, value_tensor, slash_offsets, vertical_tiles, kept_rows, kept_count, out_weight):
    shard_length = TOK_DEV
    group_width = QUERY_HEAD_COUNT // KEY_VALUE_HEADS
    pad_amount = (SLASH_SPAN + 2) * shard_length
    zero_index = jnp.zeros((), jnp.int32)
    empty_fill = jnp.zeros((pad_amount, KEY_VALUE_HEADS * HEAD_SIZE), jnp.bfloat16)
    key_lookup = jnp.concatenate([empty_fill, key_tensor], 0).reshape(pad_amount + PROMPT_TOKENS, KEY_VALUE_HEADS, HEAD_SIZE).transpose(1, 0, 2)
    value_lookup = jnp.concatenate([empty_fill, value_tensor], 0).reshape(pad_amount + PROMPT_TOKENS, KEY_VALUE_HEADS, HEAD_SIZE).transpose(1, 0, 2)
    query_lookup = query_tensor.reshape(CONTEXT_SHARDS, shard_length, KEY_VALUE_HEADS, group_width, HEAD_SIZE).transpose(0, 2, 3, 1, 4)
    slash_spans = (slash_offsets // shard_length).astype(jnp.int32)
    tile_window = jnp.arange(shard_length, dtype=jnp.int32)
    column_kind = jnp.concatenate([
        jnp.full((3 * shard_length,), 0, jnp.int32),
        jnp.full((3 * shard_length,), 1, jnp.int32),
        jnp.full((3 * shard_length,), 2, jnp.int32),
        jnp.full((VTILES * shard_length,), 3, jnp.int32)])

    def slab_from(source_table, head_number, first_key, length):
        return lax.dynamic_slice(source_table, (head_number.astype(jnp.int32), (first_key + pad_amount).astype(jnp.int32), zero_index), (1, length, HEAD_SIZE))[0]

    def single_block(flattened_index):
        row_of_block = (flattened_index // KEY_VALUE_HEADS).astype(jnp.int32)
        head_number = (flattened_index % KEY_VALUE_HEADS).astype(jnp.int32)
        first_pos = row_of_block * shard_length
        starts = [first_pos - 2 * shard_length]
        lengths = [3 * shard_length]
        for slash_index in range(2):
            starts.append(first_pos - (slash_spans[head_number, slash_index] + 2) * shard_length)
            lengths.append(3 * shard_length)
        for tile_index in range(VTILES):
            starts.append(vertical_tiles[head_number, tile_index] * shard_length)
            lengths.append(shard_length)
        key_slab = jnp.concatenate([slab_from(key_lookup, head_number, first_key, length) for first_key, length in zip(starts, lengths)], 0)
        value_slab = jnp.concatenate([slab_from(value_lookup, head_number, first_key, length) for first_key, length in zip(starts, lengths)], 0)
        key_pos = jnp.concatenate([(first_key + jnp.arange(length, dtype=jnp.int32)).astype(jnp.int32) for first_key, length in zip(starts, lengths)], 0)
        query_rows = lax.dynamic_slice(query_lookup, (row_of_block, head_number, zero_index, zero_index, zero_index), (1, 1, group_width, shard_length, HEAD_SIZE)).reshape(group_width * shard_length, HEAD_SIZE)
        query_pos = (first_pos + tile_window).astype(jnp.int32)
        return attend(query_rows, key_slab, value_slab, key_pos, query_pos, slash_offsets[head_number], vertical_tiles[head_number], column_kind, group_width)

    output_list = lax.map(single_block, jnp.arange(CONTEXT_SHARDS * KEY_VALUE_HEADS, dtype=jnp.int32))
    attended = output_list.reshape(CONTEXT_SHARDS, KEY_VALUE_HEADS, group_width, shard_length, HEAD_SIZE).transpose(0, 3, 1, 2, 4).reshape(PROMPT_TOKENS, QUERY_HEAD_COUNT * HEAD_SIZE)

    starts_all = (jnp.cumsum(kept_count) - kept_count).astype(jnp.int32)
    slot_ids = jnp.arange(CAP, dtype=jnp.int32)
    is_live = slot_ids[None, :] < kept_count[:, None]
    source_rows = (jnp.arange(CONTEXT_SHARDS, dtype=jnp.int32)[:, None] * shard_length + kept_rows).reshape(-1).astype(jnp.int32)
    target_rows = jnp.where(is_live, starts_all[:, None] + slot_ids[None, :], KEPT).reshape(-1).astype(jnp.int32)
    placed = jnp.zeros((KEPT, QUERY_HEAD_COUNT * HEAD_SIZE), jnp.bfloat16).at[target_rows].set(attended[source_rows], mode="drop")
    projected = jnp.dot(placed, out_weight.T, preferred_element_type=jnp.float32).astype(jnp.bfloat16)
    return attended, projected
```

```python
import math

import jax
import jax.numpy as jnp
from jax import lax
from jax.experimental import pallas as pl
from jax.experimental.pallas import tpu as pltpu
from jax.sharding import PartitionSpec as P

HEAD_SIZE = 128
SLASH_SPAN = 8
VTILES = 2
LOCAL_BAND_KEYS = 256
SLASH_W = 128
VTILE = 128
PAD_ROWS = 8
MASKED = -1e30

ANY = pl.BlockSpec(memory_space=pl.ANY)
SMEM = pl.BlockSpec(memory_space=pltpu.SMEM)
VMEM = pl.BlockSpec(memory_space=pltpu.VMEM)


def xor_pairs(size, k):
    return [(i, i ^ k) for i in range(size)]


def pack_heads(shard_index, query, key, value, kept_rows, heads):
    length = query.shape[0]
    width = query.shape[1] // heads
    hd = HEAD_SIZE
    capacity = kept_rows.shape[1]
    total = 2 * hd + width

    def body(c_ref, q_ref, k_ref, v_ref, kept_ref, *rest):
        out, (kept_buf, sems) = rest[:heads], rest[heads:]
        slot = c_ref[0] % heads
        copies = []
        for j in range(heads):
            head = slot ^ j
            q_at = pl.multiple_of(head * width, hd)
            k_at = pl.multiple_of(head * hd, hd)
            copies += [
                (k_ref.at[:, pl.ds(k_at, hd)], out[j].at[pl.ds(0, length), pl.ds(0, hd)]),
                (v_ref.at[:, pl.ds(k_at, hd)], out[j].at[pl.ds(0, length), pl.ds(hd, hd)]),
                (q_ref.at[:, pl.ds(q_at, width)], out[j].at[pl.ds(0, length), pl.ds(2 * hd, width)]),
            ]
        started = []
        for number, (source, target) in enumerate(copies):
            copy = pltpu.make_async_copy(source, target, sems.at[number])
            copy.start()
            started.append(copy)
        kept_buf[...] = jnp.zeros(kept_buf.shape, jnp.bfloat16)
        kept_buf[0:1, 0:capacity] = kept_ref[...].astype(jnp.float32).astype(jnp.bfloat16)
        for j in range(heads):
            copy = pltpu.make_async_copy(
                kept_buf, out[j].at[pl.ds(length, PAD_ROWS)], sems.at[len(copies) + j]
            )
            copy.start()
            started.append(copy)
        for copy in started:
            copy.wait()

    return pl.pallas_call(
        body,
        out_shape=[jax.ShapeDtypeStruct((length + PAD_ROWS, total), jnp.bfloat16)] * heads,
        in_specs=[SMEM, ANY, ANY, ANY, VMEM],
        out_specs=[ANY] * heads,
        scratch_shapes=[
            pltpu.VMEM((PAD_ROWS, total), jnp.bfloat16),
            pltpu.SemaphoreType.DMA((4 * heads,)),
        ],
        name="pack_heads",
    )(shard_index, query, key, value, kept_rows)


def pack_weight(shard_index, weight, heads):
    width = weight.shape[1] // heads

    def body(c_ref, w_ref, *rest):
        out, sems = rest[:heads], rest[heads]
        slot = c_ref[0] % heads
        copies = []
        for j in range(heads):
            at = pl.multiple_of((slot ^ j) * width, HEAD_SIZE)
            copies.append(pltpu.make_async_copy(w_ref.at[:, pl.ds(at, width)], out[j], sems.at[j]))
        for copy in copies:
            copy.start()
        for copy in copies:
            copy.wait()

    return pl.pallas_call(
        body,
        out_shape=[jax.ShapeDtypeStruct((weight.shape[0], width), jnp.bfloat16)] * heads,
        in_specs=[SMEM, ANY],
        out_specs=[ANY] * heads,
        scratch_shapes=[pltpu.SemaphoreType.DMA((heads,))],
        name="pack_weight",
    )(shard_index, weight)


def attention(shard_index, slash, tiles, counts, near, far, keep_rows):
    heads = len(near)
    pieces = heads + len(far)
    length = near[0].shape[0] - PAD_ROWS
    hd = HEAD_SIZE
    width = near[0].shape[1] - 2 * hd
    group = width // hd
    block_rows = heads * keep_rows
    factor = hd ** (-0.5) * math.log2(math.e)

    def body(c_ref, slash_ref, tile_ref, count_ref, *rest):
        near_refs, rest = rest[:heads], rest[heads:]
        far_refs, rest = rest[: len(far)], rest[len(far) :]
        out_refs, rows_ref = rest[:heads], rest[heads]
        k_all, v_all, bias = rest[heads + 1 :]
        c = c_ref[0]
        slot = c % heads
        first = c - slot
        for k in range(pieces):
            ref = near_refs[k] if k < heads else far_refs[k - heads]
            k_all[k * length : (k + 1) * length, :] = ref[0:length, 0:hd]
            v_all[k * length : (k + 1) * length, :] = ref[0:length, hd : 2 * hd]
        difference = lax.broadcasted_iota(jnp.int32, (length, length), 0) - lax.broadcasted_iota(
            jnp.int32, (length, length), 1
        )
        offsets = [slash_ref[slot, i] for i in range(slash_ref.shape[1])]
        verticals = [tile_ref[slot, i] for i in range(tile_ref.shape[1])]
        rows = jnp.zeros((block_rows, width), jnp.float32)
        for q in range(heads):
            q_shard = c ^ q
            for k in range(pieces):
                k_shard = c ^ k
                distance = difference + (q_shard - k_shard) * length
                reach = jnp.int32(LOCAL_BAND_KEYS)
                for tile in verticals:
                    reach = jnp.where(tile == k_shard, jnp.int32(1 << 30), reach)
                allowed = (distance >= 0) & (distance < reach)
                for offset in offsets:
                    allowed |= (distance >= offset) & (distance < offset + SLASH_W)
                bias[:, k * length : (k + 1) * length] = jnp.where(allowed, 0.0, MASKED)
            for g in range(group):
                at = 2 * hd + g * hd
                scores = lax.dot_general(
                    near_refs[q][0:length, at : at + hd],
                    k_all[...],
                    (((1,), (1,)), ((), ())),
                    preferred_element_type=jnp.float32,
                )
                scores = scores + bias[...]
                top = jnp.max(scores, axis=1, keepdims=True)
                weights = jnp.exp2((scores - top) * factor)
                total = jnp.sum(weights, axis=1, keepdims=True)
                mixed = jnp.dot(
                    weights.astype(jnp.bfloat16), v_all[...], preferred_element_type=jnp.float32
                )
                out_refs[q][:, g * hd : (g + 1) * hd] = (mixed / total).astype(jnp.bfloat16)
            q_slot = slot ^ q
            before = jnp.int32(0)
            for s in range(heads):
                before = before + jnp.where(s < q_slot, count_ref[first + s], 0)
            kept = near_refs[q][length : length + 1, 0:hd].astype(jnp.float32).astype(jnp.int32)
            token = lax.broadcasted_iota(jnp.int32, (length, hd), 0)
            is_token = (token == kept).astype(jnp.float32).astype(jnp.bfloat16)
            index = lax.broadcasted_iota(jnp.int32, (hd, block_rows), 0)
            place = lax.broadcasted_iota(jnp.int32, (hd, block_rows), 1)
            is_place = ((place - index == before) & (index < count_ref[q_shard])).astype(jnp.float32)
            chooser = jnp.dot(
                is_token, is_place.astype(jnp.bfloat16), preferred_element_type=jnp.float32
            ).astype(jnp.bfloat16)
            rows = rows + lax.dot_general(
                chooser,
                out_refs[q][...],
                (((0,), (0,)), ((), ())),
                preferred_element_type=jnp.float32,
            )
        rows_ref[...] = rows.astype(jnp.bfloat16)

    return pl.pallas_call(
        body,
        out_shape=[jax.ShapeDtypeStruct((length, width), jnp.bfloat16)] * heads
        + [jax.ShapeDtypeStruct((block_rows, width), jnp.bfloat16)],
        in_specs=[SMEM] * 4 + [VMEM] * pieces,
        out_specs=[VMEM] * (heads + 1),
        scratch_shapes=[
            pltpu.VMEM((pieces * length, hd), jnp.bfloat16),
            pltpu.VMEM((pieces * length, hd), jnp.bfloat16),
            pltpu.VMEM((length, pieces * length), jnp.float32),
        ],
        name="attention",
    )(shard_index, slash, tiles, counts, *near, *far)


def project(where, own_rows, other_rows, weights):
    heads = len(weights)
    count = own_rows.shape[0]
    outs = weights[0].shape[0]

    def body(where_ref, own_ref, other_ref, *rest):
        w_refs, (keep_ref, send_ref) = rest[:heads], rest[heads:]
        slot = where_ref[0] % heads
        keeps_own = where_ref[0] // heads == where_ref[1]
        own, other = own_ref[...], other_ref[...]
        both = jnp.concatenate(
            [jnp.where(keeps_own, own, other), jnp.where(keeps_own, other, own)], 0
        )
        for j in range(heads):
            at = pl.multiple_of((slot ^ j) * outs, HEAD_SIZE)
            share = lax.dot_general(
                both, w_refs[j][...], (((1,), (1,)), ((), ())), preferred_element_type=jnp.float32
            )
            keep_ref[:, pl.ds(at, outs)] = share[:count]
            send_ref[:, pl.ds(at, outs)] = share[count:]

    return pl.pallas_call(
        body,
        out_shape=[jax.ShapeDtypeStruct((count, heads * outs), jnp.float32)] * 2,
        in_specs=[SMEM] + [VMEM] * (2 + heads),
        out_specs=[VMEM] * 2,
        name="project",
    )(where, own_rows, other_rows, *weights)


def split_rows(shard_index, kept, received, heads):
    keep_rows = kept.shape[0] // heads

    def body(c_ref, a_ref, b_ref, *out):
        slot = c_ref[0] % heads
        for j in range(heads):
            at = pl.multiple_of((slot ^ j) * keep_rows, 8)
            out[j][...] = (a_ref[pl.ds(at, keep_rows), :] + b_ref[pl.ds(at, keep_rows), :]).astype(
                jnp.bfloat16
            )

    return pl.pallas_call(
        body,
        out_shape=[jax.ShapeDtypeStruct((keep_rows, kept.shape[1]), jnp.bfloat16)] * heads,
        in_specs=[SMEM, VMEM, VMEM],
        out_specs=[VMEM] * heads,
        name="split_rows",
    )(shard_index, kept, received)


def join_heads(shard_index, pieces):
    heads = len(pieces)
    length, width = pieces[0].shape

    def body(c_ref, *rest):
        ins, (out_ref, sems) = rest[:heads], rest[heads:]
        slot = c_ref[0] % heads
        copies = []
        for j in range(heads):
            at = pl.multiple_of((slot ^ j) * width, HEAD_SIZE)
            copies.append(
                pltpu.make_async_copy(ins[j], out_ref.at[:, pl.ds(at, width)], sems.at[j])
            )
        for copy in copies:
            copy.start()
        for copy in copies:
            copy.wait()

    return pl.pallas_call(
        body,
        out_shape=jax.ShapeDtypeStruct((length, heads * width), jnp.bfloat16),
        in_specs=[SMEM] + [ANY] * heads,
        out_specs=ANY,
        scratch_shapes=[pltpu.SemaphoreType.DMA((heads,))],
        name="join_heads",
    )(shard_index, *pieces)


def local_blocks(
    query_tensor,
    key_tensor,
    value_tensor,
    slash_offsets,
    vertical_tiles,
    kept_rows,
    kept_count,
    out_weight,
):
    size = lax.axis_size("ctx")
    cores = lax.axis_size("head")
    heads = key_tensor.shape[1] // HEAD_SIZE
    keep_rows = query_tensor.shape[0] // 8
    c = lax.axis_index("ctx").astype(jnp.int32)
    shard_index = c.reshape(1)

    def swap(x, k):
        return lax.ppermute(x, "ctx", xor_pairs(size, k))

    packed = pack_heads(shard_index, query_tensor, key_tensor, value_tensor, kept_rows, heads)
    near = [packed[0]] + [swap(packed[k], k) for k in range(1, heads)]
    key_values = [x[: query_tensor.shape[0], : 2 * HEAD_SIZE] for x in packed]
    far = [
        lax.ppermute(
            key_values[k % heads], "ctx", [(i, i ^ k) for i in range(size) if i // heads < (i ^ k) // heads]
        )
        for k in range(heads, size)
    ]
    packed_weight = pack_weight(shard_index, out_weight, heads)
    weights = [packed_weight[0]] + [swap(packed_weight[k], k) for k in range(1, heads)]
    *mixed, rows = attention(
        shard_index, slash_offsets, vertical_tiles, kept_count, near, far, keep_rows
    )
    other_rows = swap(rows, heads)
    returned = [mixed[0]] + [swap(mixed[k], k) for k in range(1, heads)]
    attended = join_heads(shard_index, returned)
    where = jnp.stack([c, lax.axis_index("head").astype(jnp.int32)])
    kept, sent = project(where, rows, other_rows, weights)
    received = lax.ppermute(sent, "head", [(i, cores - 1 - i) for i in range(cores)])
    shares = split_rows(shard_index, kept, received, heads)
    total = jnp.zeros(shares[0].shape, jnp.float32)
    for k in range(heads):
        pairs = []
        for i in range(size):
            for h in range(cores):
                target = heads * h + ((i % heads) ^ k)
                pairs.append((i * cores + h, target * cores + i // heads))
        total = total + lax.ppermute(shares[k], ("ctx", "head"), pairs).astype(jnp.float32)
    return (attended, total.astype(jnp.bfloat16))


def shifted_2(x, axis, by):
    size = lax.axis_size(axis)
    pairs = [(i, i + by) for i in range(size) if 0 <= i + by < size]
    return lax.ppermute(x, axis, pairs)


def broadcast(x, axis, root):
    mine = lax.axis_index(axis) == root
    return lax.psum(jnp.where(mine, x, jnp.zeros_like(x)), axis)


def attend(
    query_rows,
    key_slab,
    value_slab,
    key_pos,
    query_pos,
    slash_shift_list,
    tile_list,
    column_kind,
    group_width,
):
    scores = jnp.dot(query_rows, key_slab.T, preferred_element_type=jnp.float32) * key_slab.shape[
        -1
    ] ** (-0.5)
    distance = query_pos[:, None] - key_pos[None, :]
    key_tile = jnp.where(key_pos >= 0, key_pos // VTILE, -1)
    vertical = jnp.any(key_tile[:, None] == tile_list[None, :], axis=1)[None, :]
    in_band = (distance >= 0) & (distance < LOCAL_BAND_KEYS) & ~vertical
    first_slash = (
        (distance >= slash_shift_list[0]) & (distance < slash_shift_list[0] + SLASH_W) & ~vertical
    )
    second_slash = (
        (distance >= slash_shift_list[1]) & (distance < slash_shift_list[1] + SLASH_W) & ~vertical
    )
    earlier = in_band | first_slash
    kinds = column_kind[None, :]
    allowed = jnp.where(
        kinds == 0,
        in_band,
        jnp.where(
            kinds == 1,
            first_slash & ~in_band,
            jnp.where(kinds == 2, second_slash & ~earlier, distance >= 0),
        ),
    )
    allowed = jnp.tile(allowed & (key_pos >= 0)[None, :], (group_width, 1))
    masked = jnp.where(allowed, scores, -jnp.inf)
    row_max = jnp.max(masked, axis=1, keepdims=True)
    weights = jnp.where(allowed, jnp.exp(masked - row_max), 0.0)
    row_sum = jnp.sum(weights, axis=1, keepdims=True)
    blended = jnp.dot(weights.astype(jnp.bfloat16), value_slab, preferred_element_type=jnp.float32)
    return (blended / row_sum).astype(jnp.bfloat16)


def heads_first(stacked, local_heads, head_dim):
    reordered = jnp.moveaxis(stacked, -2, 0)
    return reordered.reshape(local_heads, -1, head_dim)


def move_near(row_block, is_live, offset, target_slot, keep_rows, sender):
    slot_grid = jnp.arange(keep_rows, dtype=jnp.int32)[:, None]
    gathered = jnp.zeros((keep_rows, row_block.shape[1]), jnp.float32)
    for travel in range(-3, 4):
        chooser = (
            (slot_grid == target_slot[None, :]) & (offset[None, :] == travel) & is_live[None, :]
        ).astype(jnp.bfloat16)
        parcel = jnp.dot(chooser, row_block, preferred_element_type=jnp.float32).astype(
            jnp.bfloat16
        )
        if travel != 0:
            parcel = sender(parcel, travel)
        gathered = gathered + parcel.astype(jnp.float32)
    return gathered.astype(jnp.bfloat16)


def local(
    query_tensor,
    key_tensor,
    value_tensor,
    slash_offsets,
    vertical_tiles,
    kept_rows,
    kept_count,
    out_weight,
):
    shard_length = query_tensor.shape[0]
    head_dim = HEAD_SIZE
    local_heads = key_tensor.shape[1] // head_dim
    group_width = query_tensor.shape[1] // key_tensor.shape[1]
    shard_index = lax.axis_index("ctx")
    first_pos = shard_index * shard_length
    key_heads = key_tensor.reshape(shard_length, local_heads, head_dim)
    value_heads = value_tensor.reshape(shard_length, local_heads, head_dim)
    slash_spans = slash_offsets // shard_length
    own_pair = jnp.stack([key_heads, value_heads])
    moving = jnp.concatenate([own_pair, own_pair], 0)
    member_spans = jnp.stack(
        [slash_spans[:, 0], slash_spans[:, 0], slash_spans[:, 1], slash_spans[:, 1]]
    )
    for bit_number in range((SLASH_SPAN - 1).bit_length()):
        shifted = shifted_2(moving, "ctx", 1 << bit_number)
        head_flags = (member_spans >> bit_number & 1 == 1)[:, None, :, None]
        moving = jnp.where(head_flags, shifted, moving)
    nearby = jnp.concatenate([moving, own_pair], 0)
    distances = [nearby]
    for repeat_factor in range(2):
        nearby = shifted_2(nearby, "ctx", 1)
        distances.append(nearby)
    ordered = jnp.stack([distances[2], distances[1], distances[0]])
    band_pieces = ordered[:, 4:6]
    slash_pieces = jnp.stack([ordered[:, 0:2], ordered[:, 2:4]])
    tile_keys = []
    tile_values = []
    for head_number in range(local_heads):
        for tile_index in range(VTILES):
            fetched = broadcast(
                jnp.stack([key_heads[:, head_number], value_heads[:, head_number]]),
                "ctx",
                vertical_tiles[head_number, tile_index],
            )
            tile_keys.append(fetched[0])
            tile_values.append(fetched[1])
    all_keys = jnp.concatenate(
        [
            heads_first(band_pieces[:, 0], local_heads, head_dim),
            heads_first(slash_pieces[:, :, 0], local_heads, head_dim),
            jnp.stack(tile_keys).reshape(local_heads, VTILES * shard_length, head_dim),
        ],
        1,
    )
    all_values = jnp.concatenate(
        [
            heads_first(band_pieces[:, 1], local_heads, head_dim),
            heads_first(slash_pieces[:, :, 1], local_heads, head_dim),
            jnp.stack(tile_values).reshape(local_heads, VTILES * shard_length, head_dim),
        ],
        1,
    )
    window = jnp.arange(3 * shard_length, dtype=jnp.int32)
    band_pos = jnp.broadcast_to(
        first_pos - 2 * shard_length + window, (local_heads, 3 * shard_length)
    )
    slash_pos = first_pos - (slash_spans[:, :, None] + 2) * shard_length + window[None, None, :]
    tile_pos = (
        vertical_tiles[:, :, None] * shard_length
        + jnp.arange(shard_length, dtype=jnp.int32)[None, None, :]
    )
    key_pos = jnp.concatenate(
        [band_pos, slash_pos.reshape(local_heads, -1), tile_pos.reshape(local_heads, -1)], 1
    )
    column_kind = jnp.concatenate(
        [
            jnp.full((3 * shard_length,), 0, jnp.int32),
            jnp.full((3 * shard_length,), 1, jnp.int32),
            jnp.full((3 * shard_length,), 2, jnp.int32),
            jnp.full((VTILES * shard_length,), 3, jnp.int32),
        ]
    )
    query_pos = first_pos + jnp.arange(shard_length, dtype=jnp.int32)
    query_heads = (
        query_tensor.reshape(shard_length, local_heads, group_width, head_dim)
        .transpose(1, 2, 0, 3)
        .reshape(local_heads, group_width * shard_length, head_dim)
    )

    def attend_head(packed):
        return attend(
            packed[0],
            packed[1],
            packed[2],
            packed[3],
            query_pos,
            packed[4],
            packed[5],
            column_kind,
            group_width,
        )

    mixed_heads = lax.map(
        attend_head, (query_heads, all_keys, all_values, key_pos, slash_offsets, vertical_tiles)
    )
    attended = (
        mixed_heads.reshape(local_heads, group_width, shard_length, head_dim)
        .transpose(2, 0, 1, 3)
        .reshape(shard_length, -1)
    )
    keep_rows = shard_length // 8
    capacity = kept_rows.shape[1]
    starts = jnp.cumsum(kept_count) - kept_count
    slot_ids = jnp.arange(capacity, dtype=jnp.int32)
    is_live = slot_ids < kept_count[shard_index]
    placed_at = starts[shard_index] + slot_ids
    target_shard = placed_at // keep_rows
    target_slot = placed_at % keep_rows
    offset = target_shard - shard_index
    selected = jnp.take(attended, kept_rows[0], axis=0)
    rounded = lax.psum_scatter(
        lax.dot_general(
            selected,
            lax.all_gather(out_weight, "ctx", axis=0, tiled=True),
            (((1,), (1,)), ((), ())),
            preferred_element_type=jnp.float32,
        ),
        "head",
        scatter_dimension=1,
        tiled=True,
    ).astype(jnp.bfloat16)

    def send_output(parcel, travel):
        return shifted_2(parcel, "ctx", travel)

    projected = move_near(rounded, is_live, offset, target_slot, keep_rows, send_output)
    return (attended, projected)


def solution(mesh):
    placed = (
        P(("groups", "ctx"), "head"),
        P(("groups", "ctx"), "head"),
        P(("groups", "ctx"), "head"),
        P(("groups", "head"), None),
        P(("groups", "head"), None),
        P(("groups", "ctx"), None),
        P("groups"),
        P("ctx", "head"),
    )
    def program(*args):
        heads = args[1].shape[1] // HEAD_SIZE
        size = lax.axis_size("ctx")
        power = size & (size - 1) == 0 and heads & (heads - 1) == 0
        whole_tiles = args[0].shape[0] == VTILE and args[5].shape[1] <= HEAD_SIZE
        cores = lax.axis_size("head")
        if power and whole_tiles and cores == 2 and size == heads * cores:
            return local_blocks(*args)
        return local(*args)

    return jax.shard_map(
        program,
        mesh=mesh,
        in_specs=placed,
        out_specs=(P(("groups", "ctx"), "head"), P(("groups", "ctx"), "head")),
        check_vma=False,
    )
```

```python
import math

import jax
import jax.numpy as jnp
from jax import lax
from jax.experimental import pallas as pl
from jax.experimental.pallas import tpu as pltpu
from jax.sharding import PartitionSpec as P

HEAD_SIZE = 128
SLASH_SPAN = 8
VTILES = 2
LOCAL_BAND_KEYS = 256
SLASH_W = 128
VTILE = 128
PAD_ROWS = 8
MASKED = -1e30

SMEM = pl.BlockSpec(memory_space=pltpu.SMEM)
VMEM = pl.BlockSpec(memory_space=pltpu.VMEM)


def xor_pairs(size, k):
    return [(i, i ^ k) for i in range(size)]


def in_vmem(x):
    return pltpu.with_memory_space_constraint(x, pltpu.VMEM)


def pack_heads(meta, query, key, value, kept_rows, heads):
    length = query.shape[0]
    width = query.shape[1] // heads
    hd = HEAD_SIZE
    capacity = kept_rows.shape[1]
    total = 2 * hd + width

    def body(meta_ref, q_ref, k_ref, v_ref, kept_ref, *out):
        slot = meta_ref[0] % heads
        kept = jnp.zeros((PAD_ROWS, total), jnp.bfloat16)
        for j in range(heads):
            head = slot ^ j
            q_at = pl.multiple_of(head * width, hd)
            k_at = pl.multiple_of(head * hd, hd)
            k, v = k_ref[:, pl.ds(k_at, hd)], v_ref[:, pl.ds(k_at, hd)]
            out[j][0:length, 0:hd] = k
            out[j][0:length, hd : 2 * hd] = v
            out[j][0:length, 2 * hd :] = q_ref[:, pl.ds(q_at, width)]
            out[j][length:, :] = kept
            out[j][length : length + 1, 0:capacity] = (
                kept_ref[...].astype(jnp.float32).astype(jnp.bfloat16)
            )
            out[heads + j][:, 0:hd] = k
            out[heads + j][:, hd:] = v

    return pl.pallas_call(
        body,
        out_shape=[pltpu.VMEM((length + PAD_ROWS, total), jnp.bfloat16)] * heads
        + [pltpu.VMEM((length, 2 * hd), jnp.bfloat16)] * heads,
        in_specs=[SMEM] + [VMEM] * 4,
        out_specs=[VMEM] * (2 * heads),
        name="pack_heads",
    )(meta, query, key, value, kept_rows)


def pack_weight(meta, weight, heads):
    width = weight.shape[1] // heads

    def body(meta_ref, w_ref, *out):
        slot = meta_ref[0] % heads
        for j in range(heads):
            at = pl.multiple_of((slot ^ j) * width, HEAD_SIZE)
            out[j][...] = w_ref[:, pl.ds(at, width)]

    return pl.pallas_call(
        body,
        out_shape=[pltpu.VMEM((weight.shape[0], width), jnp.bfloat16)] * heads,
        in_specs=[SMEM, VMEM],
        out_specs=[VMEM] * heads,
        name="pack_weight",
    )(meta, weight)


def attention(meta, offsets_at, tiles_at, counts_at, near, far, keep_rows):
    heads = len(near)
    pieces = heads + len(far)
    length = near[0].shape[0] - PAD_ROWS
    hd = HEAD_SIZE
    width = near[0].shape[1] - 2 * hd
    group = width // hd
    block_rows = heads * keep_rows
    factor = hd ** (-0.5) * math.log2(math.e)

    def body(meta_ref, *rest):
        near_refs, rest = rest[:heads], rest[heads:]
        far_refs, rest = rest[: len(far)], rest[len(far) :]
        out_refs, rows_ref = rest[:heads], rest[heads]
        k_all, v_all, bias = rest[heads + 1 :]
        c = meta_ref[0]
        slot = c % heads
        first = counts_at + c - slot
        for k in range(pieces):
            ref = near_refs[k] if k < heads else far_refs[k - heads]
            k_all[k * length : (k + 1) * length, :] = ref[0:length, 0:hd]
            v_all[k * length : (k + 1) * length, :] = ref[0:length, hd : 2 * hd]
        difference = lax.broadcasted_iota(jnp.int32, (length, length), 0) - lax.broadcasted_iota(
            jnp.int32, (length, length), 1
        )
        offsets = [meta_ref[offsets_at + i * heads + slot] for i in range(2)]
        verticals = [meta_ref[tiles_at + i * heads + slot] for i in range(VTILES)]
        rows = jnp.zeros((block_rows, width), jnp.float32)
        for q in range(heads):
            q_shard = c ^ q
            for k in range(pieces):
                k_shard = c ^ k
                distance = difference + (q_shard - k_shard) * length
                reach = jnp.int32(LOCAL_BAND_KEYS)
                for tile in verticals:
                    reach = jnp.where(tile == k_shard, jnp.int32(1 << 30), reach)
                allowed = (distance >= 0) & (distance < reach)
                for offset in offsets:
                    allowed |= (distance >= offset) & (distance < offset + SLASH_W)
                bias[:, k * length : (k + 1) * length] = jnp.where(allowed, 0.0, MASKED)
            for g in range(group):
                at = 2 * hd + g * hd
                scores = lax.dot_general(
                    near_refs[q][0:length, at : at + hd],
                    k_all[...],
                    (((1,), (1,)), ((), ())),
                    preferred_element_type=jnp.float32,
                )
                scores = scores + bias[...]
                top = jnp.max(scores, axis=1, keepdims=True)
                weights = jnp.exp2((scores - top) * factor)
                total = jnp.sum(weights, axis=1, keepdims=True)
                mixed = jnp.dot(
                    weights.astype(jnp.bfloat16), v_all[...], preferred_element_type=jnp.float32
                )
                out_refs[q][:, g * hd : (g + 1) * hd] = (mixed / total).astype(jnp.bfloat16)
            q_slot = slot ^ q
            before = jnp.int32(0)
            for s in range(heads):
                before = before + jnp.where(s < q_slot, meta_ref[first + s], 0)
            kept = near_refs[q][length : length + 1, 0:hd].astype(jnp.float32).astype(jnp.int32)
            token = lax.broadcasted_iota(jnp.int32, (length, hd), 0)
            is_token = (token == kept).astype(jnp.float32).astype(jnp.bfloat16)
            index = lax.broadcasted_iota(jnp.int32, (hd, block_rows), 0)
            place = lax.broadcasted_iota(jnp.int32, (hd, block_rows), 1)
            is_place = ((place - index == before) & (index < meta_ref[counts_at + q_shard])).astype(jnp.float32)
            chooser = jnp.dot(
                is_token, is_place.astype(jnp.bfloat16), preferred_element_type=jnp.float32
            ).astype(jnp.bfloat16)
            rows = rows + lax.dot_general(
                chooser,
                out_refs[q][...],
                (((0,), (0,)), ((), ())),
                preferred_element_type=jnp.float32,
            )
        rows_ref[...] = rows.astype(jnp.bfloat16)

    return pl.pallas_call(
        body,
        out_shape=[pltpu.VMEM((length, width), jnp.bfloat16)] * heads
        + [pltpu.VMEM((block_rows, width), jnp.bfloat16)],
        in_specs=[SMEM] + [VMEM] * pieces,
        out_specs=[VMEM] * (heads + 1),
        scratch_shapes=[
            pltpu.VMEM((pieces * length, hd), jnp.bfloat16),
            pltpu.VMEM((pieces * length, hd), jnp.bfloat16),
            pltpu.VMEM((length, pieces * length), jnp.float32),
        ],
        name="attention",
    )(meta, *near, *far)


def project(meta, own_rows, other_rows, weights):
    heads = len(weights)
    count = own_rows.shape[0]
    outs = weights[0].shape[0]

    def body(meta_ref, own_ref, other_ref, *rest):
        w_refs, (keep_ref, send_ref) = rest[:heads], rest[heads:]
        slot = meta_ref[0] % heads
        keeps_own = meta_ref[0] // heads == meta_ref[1]
        own, other = own_ref[...], other_ref[...]
        both = jnp.concatenate(
            [jnp.where(keeps_own, own, other), jnp.where(keeps_own, other, own)], 0
        )
        for j in range(heads):
            at = pl.multiple_of((slot ^ j) * outs, HEAD_SIZE)
            share = lax.dot_general(
                both, w_refs[j][...], (((1,), (1,)), ((), ())), preferred_element_type=jnp.float32
            )
            keep_ref[:, pl.ds(at, outs)] = share[:count]
            send_ref[:, pl.ds(at, outs)] = share[count:]

    return pl.pallas_call(
        body,
        out_shape=[pltpu.VMEM((count, heads * outs), jnp.float32)] * 2,
        in_specs=[SMEM] + [VMEM] * (2 + heads),
        out_specs=[VMEM] * 2,
        name="project",
    )(meta, own_rows, other_rows, *weights)


def split_rows(meta, kept, received, heads):
    keep_rows = kept.shape[0] // heads

    def body(meta_ref, a_ref, b_ref, *out):
        slot = meta_ref[0] % heads
        for j in range(heads):
            at = pl.multiple_of((slot ^ j) * keep_rows, 8)
            out[j][...] = (a_ref[pl.ds(at, keep_rows), :] + b_ref[pl.ds(at, keep_rows), :]).astype(
                jnp.bfloat16
            )

    return pl.pallas_call(
        body,
        out_shape=[pltpu.VMEM((keep_rows, kept.shape[1]), jnp.bfloat16)] * heads,
        in_specs=[SMEM, VMEM, VMEM],
        out_specs=[VMEM] * heads,
        name="split_rows",
    )(meta, kept, received)


def join_heads(meta, pieces):
    heads = len(pieces)
    length, width = pieces[0].shape

    def body(meta_ref, *rest):
        slot = meta_ref[0] % heads
        for j in range(heads):
            at = pl.multiple_of((slot ^ j) * width, HEAD_SIZE)
            rest[heads][:, pl.ds(at, width)] = rest[j][...]

    return pl.pallas_call(
        body,
        out_shape=jax.ShapeDtypeStruct((length, heads * width), jnp.bfloat16),
        in_specs=[SMEM] + [VMEM] * heads,
        out_specs=VMEM,
        name="join_heads",
    )(meta, *pieces)


def local_blocks(
    query_tensor,
    key_tensor,
    value_tensor,
    slash_offsets,
    vertical_tiles,
    kept_rows,
    kept_count,
    out_weight,
):
    size = lax.axis_size("ctx")
    cores = lax.axis_size("head")
    heads = key_tensor.shape[1] // HEAD_SIZE
    keep_rows = query_tensor.shape[0] // 8
    c = lax.axis_index("ctx").astype(jnp.int32)
    h = lax.axis_index("head").astype(jnp.int32)
    tables = [jnp.stack([c, h]), slash_offsets.T.reshape(-1), vertical_tiles.T.reshape(-1), kept_count]
    meta = jnp.concatenate(tables)
    offsets_at = 2
    tiles_at = offsets_at + slash_offsets.size
    counts_at = tiles_at + vertical_tiles.size

    def swap(x, k):
        return in_vmem(lax.ppermute(x, "ctx", xor_pairs(size, k)))

    packed = pack_heads(c.reshape(1), query_tensor, key_tensor, value_tensor, kept_rows, heads)
    near = [in_vmem(packed[0])] + [swap(packed[k], k) for k in range(1, heads)]
    far = [
        in_vmem(
            lax.ppermute(
                packed[heads + k % heads],
                "ctx",
                [(i, i ^ k) for i in range(size) if i // heads < (i ^ k) // heads],
            )
        )
        for k in range(heads, size)
    ]
    packed_weight = pack_weight(c.reshape(1), out_weight, heads)
    weights = [in_vmem(packed_weight[0])] + [swap(packed_weight[k], k) for k in range(1, heads)]
    *mixed, rows = attention(meta, offsets_at, tiles_at, counts_at, near, far, keep_rows)
    other_rows = swap(rows, heads)
    returned = [in_vmem(mixed[0])] + [swap(mixed[k], k) for k in range(1, heads)]
    attended = join_heads(meta, returned)
    kept, sent = project(meta, in_vmem(rows), other_rows, weights)
    received = in_vmem(lax.ppermute(sent, "head", [(i, cores - 1 - i) for i in range(cores)]))
    shares = split_rows(meta, in_vmem(kept), received, heads)
    total = jnp.zeros(shares[0].shape, jnp.float32)
    for k in range(heads):
        pairs = []
        for i in range(size):
            for h in range(cores):
                target = heads * h + ((i % heads) ^ k)
                pairs.append((i * cores + h, target * cores + i // heads))
        total = total + lax.ppermute(shares[k], ("ctx", "head"), pairs).astype(jnp.float32)
    return (attended, total.astype(jnp.bfloat16))


def shifted_2(x, axis, by):
    size = lax.axis_size(axis)
    pairs = [(i, i + by) for i in range(size) if 0 <= i + by < size]
    return lax.ppermute(x, axis, pairs)


def broadcast(x, axis, root):
    mine = lax.axis_index(axis) == root
    return lax.psum(jnp.where(mine, x, jnp.zeros_like(x)), axis)


def attend(
    query_rows,
    key_slab,
    value_slab,
    key_pos,
    query_pos,
    slash_shift_list,
    tile_list,
    column_kind,
    group_width,
):
    scores = jnp.dot(query_rows, key_slab.T, preferred_element_type=jnp.float32) * key_slab.shape[
        -1
    ] ** (-0.5)
    distance = query_pos[:, None] - key_pos[None, :]
    key_tile = jnp.where(key_pos >= 0, key_pos // VTILE, -1)
    vertical = jnp.any(key_tile[:, None] == tile_list[None, :], axis=1)[None, :]
    in_band = (distance >= 0) & (distance < LOCAL_BAND_KEYS) & ~vertical
    first_slash = (
        (distance >= slash_shift_list[0]) & (distance < slash_shift_list[0] + SLASH_W) & ~vertical
    )
    second_slash = (
        (distance >= slash_shift_list[1]) & (distance < slash_shift_list[1] + SLASH_W) & ~vertical
    )
    earlier = in_band | first_slash
    kinds = column_kind[None, :]
    allowed = jnp.where(
        kinds == 0,
        in_band,
        jnp.where(
            kinds == 1,
            first_slash & ~in_band,
            jnp.where(kinds == 2, second_slash & ~earlier, distance >= 0),
        ),
    )
    allowed = jnp.tile(allowed & (key_pos >= 0)[None, :], (group_width, 1))
    masked = jnp.where(allowed, scores, -jnp.inf)
    row_max = jnp.max(masked, axis=1, keepdims=True)
    weights = jnp.where(allowed, jnp.exp(masked - row_max), 0.0)
    row_sum = jnp.sum(weights, axis=1, keepdims=True)
    blended = jnp.dot(weights.astype(jnp.bfloat16), value_slab, preferred_element_type=jnp.float32)
    return (blended / row_sum).astype(jnp.bfloat16)


def heads_first(stacked, local_heads, head_dim):
    reordered = jnp.moveaxis(stacked, -2, 0)
    return reordered.reshape(local_heads, -1, head_dim)


def move_near(row_block, is_live, offset, target_slot, keep_rows, sender):
    slot_grid = jnp.arange(keep_rows, dtype=jnp.int32)[:, None]
    gathered = jnp.zeros((keep_rows, row_block.shape[1]), jnp.float32)
    for travel in range(-3, 4):
        chooser = (
            (slot_grid == target_slot[None, :]) & (offset[None, :] == travel) & is_live[None, :]
        ).astype(jnp.bfloat16)
        parcel = jnp.dot(chooser, row_block, preferred_element_type=jnp.float32).astype(
            jnp.bfloat16
        )
        if travel != 0:
            parcel = sender(parcel, travel)
        gathered = gathered + parcel.astype(jnp.float32)
    return gathered.astype(jnp.bfloat16)


def local(
    query_tensor,
    key_tensor,
    value_tensor,
    slash_offsets,
    vertical_tiles,
    kept_rows,
    kept_count,
    out_weight,
):
    shard_length = query_tensor.shape[0]
    head_dim = HEAD_SIZE
    local_heads = key_tensor.shape[1] // head_dim
    group_width = query_tensor.shape[1] // key_tensor.shape[1]
    shard_index = lax.axis_index("ctx")
    first_pos = shard_index * shard_length
    key_heads = key_tensor.reshape(shard_length, local_heads, head_dim)
    value_heads = value_tensor.reshape(shard_length, local_heads, head_dim)
    slash_spans = slash_offsets // shard_length
    own_pair = jnp.stack([key_heads, value_heads])
    moving = jnp.concatenate([own_pair, own_pair], 0)
    member_spans = jnp.stack(
        [slash_spans[:, 0], slash_spans[:, 0], slash_spans[:, 1], slash_spans[:, 1]]
    )
    for bit_number in range((SLASH_SPAN - 1).bit_length()):
        shifted = shifted_2(moving, "ctx", 1 << bit_number)
        head_flags = (member_spans >> bit_number & 1 == 1)[:, None, :, None]
        moving = jnp.where(head_flags, shifted, moving)
    nearby = jnp.concatenate([moving, own_pair], 0)
    distances = [nearby]
    for repeat_factor in range(2):
        nearby = shifted_2(nearby, "ctx", 1)
        distances.append(nearby)
    ordered = jnp.stack([distances[2], distances[1], distances[0]])
    band_pieces = ordered[:, 4:6]
    slash_pieces = jnp.stack([ordered[:, 0:2], ordered[:, 2:4]])
    tile_keys = []
    tile_values = []
    for head_number in range(local_heads):
        for tile_index in range(VTILES):
            fetched = broadcast(
                jnp.stack([key_heads[:, head_number], value_heads[:, head_number]]),
                "ctx",
                vertical_tiles[head_number, tile_index],
            )
            tile_keys.append(fetched[0])
            tile_values.append(fetched[1])
    all_keys = jnp.concatenate(
        [
            heads_first(band_pieces[:, 0], local_heads, head_dim),
            heads_first(slash_pieces[:, :, 0], local_heads, head_dim),
            jnp.stack(tile_keys).reshape(local_heads, VTILES * shard_length, head_dim),
        ],
        1,
    )
    all_values = jnp.concatenate(
        [
            heads_first(band_pieces[:, 1], local_heads, head_dim),
            heads_first(slash_pieces[:, :, 1], local_heads, head_dim),
            jnp.stack(tile_values).reshape(local_heads, VTILES * shard_length, head_dim),
        ],
        1,
    )
    window = jnp.arange(3 * shard_length, dtype=jnp.int32)
    band_pos = jnp.broadcast_to(
        first_pos - 2 * shard_length + window, (local_heads, 3 * shard_length)
    )
    slash_pos = first_pos - (slash_spans[:, :, None] + 2) * shard_length + window[None, None, :]
    tile_pos = (
        vertical_tiles[:, :, None] * shard_length
        + jnp.arange(shard_length, dtype=jnp.int32)[None, None, :]
    )
    key_pos = jnp.concatenate(
        [band_pos, slash_pos.reshape(local_heads, -1), tile_pos.reshape(local_heads, -1)], 1
    )
    column_kind = jnp.concatenate(
        [
            jnp.full((3 * shard_length,), 0, jnp.int32),
            jnp.full((3 * shard_length,), 1, jnp.int32),
            jnp.full((3 * shard_length,), 2, jnp.int32),
            jnp.full((VTILES * shard_length,), 3, jnp.int32),
        ]
    )
    query_pos = first_pos + jnp.arange(shard_length, dtype=jnp.int32)
    query_heads = (
        query_tensor.reshape(shard_length, local_heads, group_width, head_dim)
        .transpose(1, 2, 0, 3)
        .reshape(local_heads, group_width * shard_length, head_dim)
    )

    def attend_head(packed):
        return attend(
            packed[0],
            packed[1],
            packed[2],
            packed[3],
            query_pos,
            packed[4],
            packed[5],
            column_kind,
            group_width,
        )

    mixed_heads = lax.map(
        attend_head, (query_heads, all_keys, all_values, key_pos, slash_offsets, vertical_tiles)
    )
    attended = (
        mixed_heads.reshape(local_heads, group_width, shard_length, head_dim)
        .transpose(2, 0, 1, 3)
        .reshape(shard_length, -1)
    )
    keep_rows = shard_length // 8
    capacity = kept_rows.shape[1]
    starts = jnp.cumsum(kept_count) - kept_count
    slot_ids = jnp.arange(capacity, dtype=jnp.int32)
    is_live = slot_ids < kept_count[shard_index]
    placed_at = starts[shard_index] + slot_ids
    target_shard = placed_at // keep_rows
    target_slot = placed_at % keep_rows
    offset = target_shard - shard_index
    selected = jnp.take(attended, kept_rows[0], axis=0)
    rounded = lax.psum_scatter(
        lax.dot_general(
            selected,
            lax.all_gather(out_weight, "ctx", axis=0, tiled=True),
            (((1,), (1,)), ((), ())),
            preferred_element_type=jnp.float32,
        ),
        "head",
        scatter_dimension=1,
        tiled=True,
    ).astype(jnp.bfloat16)

    def send_output(parcel, travel):
        return shifted_2(parcel, "ctx", travel)

    projected = move_near(rounded, is_live, offset, target_slot, keep_rows, send_output)
    return (attended, projected)


def solution(mesh):
    placed = (
        P(("groups", "ctx"), "head"),
        P(("groups", "ctx"), "head"),
        P(("groups", "ctx"), "head"),
        P(("groups", "head"), None),
        P(("groups", "head"), None),
        P(("groups", "ctx"), None),
        P("groups"),
        P("ctx", "head"),
    )
    def program(*args):
        heads = args[1].shape[1] // HEAD_SIZE
        size = lax.axis_size("ctx")
        power = size & (size - 1) == 0 and heads & (heads - 1) == 0
        whole_tiles = args[0].shape[0] == VTILE and args[5].shape[1] <= HEAD_SIZE
        cores = lax.axis_size("head")
        if power and whole_tiles and cores == 2 and size == heads * cores:
            return local_blocks(*args)
        return local(*args)

    return jax.shard_map(
        program,
        mesh=mesh,
        in_specs=placed,
        out_specs=(P(("groups", "ctx"), "head"), P(("groups", "ctx"), "head")),
        check_vma=False,
    )
```

```python
import math

import jax
import jax.numpy as jnp
from jax import lax
from jax.experimental import pallas as pl
from jax.experimental.pallas import tpu as pltpu
from jax.sharding import PartitionSpec as P


HEAD_SIZE = 128
SLASH_SPAN = 8
VTILES = 2
LOCAL_BAND_KEYS = 256
SLASH_W = 128
VTILE = 128
PAD_ROWS = 8
MASKED = -1e30


SMEM = pl.BlockSpec(memory_space=pltpu.SMEM)
VMEM = pl.BlockSpec(memory_space=pltpu.VMEM)


def xor_pairs(size, k):
    return [(i, i ^ k) for i in range(size)]


def in_vmem(x):
    return pltpu.with_memory_space_constraint(x, pltpu.VMEM)


def pack_heads(shard_index, query, key, value, kept_rows, heads):
    length = query.shape[0]
    width = query.shape[1] // heads
    hd = HEAD_SIZE
    capacity = kept_rows.shape[1]
    total = 2 * hd + width

    def body(c_ref, q_ref, k_ref, v_ref, kept_ref, *out):
        slot = c_ref[0] % heads
        kept = jnp.zeros((PAD_ROWS, total), jnp.bfloat16)
        for j in range(heads):
            head = slot ^ j
            q_at = pl.multiple_of(head * width, hd)
            k_at = pl.multiple_of(head * hd, hd)
            k, v = k_ref[:, pl.ds(k_at, hd)], v_ref[:, pl.ds(k_at, hd)]
            out[j][0:length, 0:hd] = k
            out[j][0:length, hd : 2 * hd] = v
            out[j][0:length, 2 * hd :] = q_ref[:, pl.ds(q_at, width)]
            out[j][length:, :] = kept
            out[j][length : length + 1, 0:capacity] = (
                kept_ref[...].astype(jnp.float32).astype(jnp.bfloat16)
            )
            out[heads + j][:, 0:hd] = k
            out[heads + j][:, hd:] = v

    return pl.pallas_call(
        body,
        out_shape=[pltpu.VMEM((length + PAD_ROWS, total), jnp.bfloat16)] * heads
        + [pltpu.VMEM((length, 2 * hd), jnp.bfloat16)] * heads,
        in_specs=[SMEM] + [VMEM] * 4,
        out_specs=[VMEM] * (2 * heads),
        name="pack_heads",
    )(shard_index, query, key, value, kept_rows)


def pack_weight(shard_index, weight, heads):
    width = weight.shape[1] // heads

    def body(c_ref, w_ref, *out):
        slot = c_ref[0] % heads
        for j in range(heads):
            at = pl.multiple_of((slot ^ j) * width, HEAD_SIZE)
            out[j][...] = w_ref[:, pl.ds(at, width)]

    return pl.pallas_call(
        body,
        out_shape=[pltpu.VMEM((weight.shape[0], width), jnp.bfloat16)] * heads,
        in_specs=[SMEM, VMEM],
        out_specs=[VMEM] * heads,
        name="pack_weight",
    )(shard_index, weight)


def attention(shard_index, slash, tiles, counts, near, far, keep_rows):
    heads = len(near)
    length = near[0].shape[0] - PAD_ROWS
    hd = HEAD_SIZE
    width = near[0].shape[1] - 2 * hd
    group = width // hd
    far_keys = len(far) * length
    keys = far_keys + heads * length
    block_rows = heads * keep_rows
    factor = hd ** (-0.5) * math.log2(math.e)

    def body(c_ref, slash_ref, tile_ref, count_ref, *rest):
        near_refs, rest = rest[:heads], rest[heads:]
        far_refs, rest = rest[: len(far)], rest[len(far) :]
        out_refs, rows_ref = rest[:heads], rest[heads]
        q_all, k_all, v_all, kept_all, mixed_all = rest[heads + 1 :]
        c = c_ref[0]
        slot = c % heads
        first = c - slot
        for k in range(len(far)):
            k_all[k * length : (k + 1) * length, :] = far_refs[k][:, 0:hd]
            v_all[k * length : (k + 1) * length, :] = far_refs[k][:, hd:]
        for k in range(heads):
            to = slot ^ k
            at = pl.ds(pl.multiple_of(far_keys + to * length, length), length)
            k_all[at, :] = near_refs[k][0:length, 0:hd]
            v_all[at, :] = near_refs[k][0:length, hd : 2 * hd]
            for g in range(group):
                q_at = pl.multiple_of((to * group + g) * length, length)
                q_all[pl.ds(q_at, length), :] = near_refs[k][
                    0:length, (2 + g) * hd : (3 + g) * hd
                ]
            kept_at = pl.ds(pl.multiple_of(to * PAD_ROWS, PAD_ROWS), PAD_ROWS)
            kept_all[kept_at, :] = near_refs[k][length:, 0:hd].astype(jnp.float32)
        difference = lax.broadcasted_iota(jnp.int32, (length, length), 0) - lax.broadcasted_iota(
            jnp.int32, (length, length), 1
        )
        offsets = [slash_ref[i, slot] for i in range(2)]
        verticals = [tile_ref[i, slot] for i in range(VTILES)]

        def bias_of(q_shard, k_shard):
            distance = difference + (q_shard - k_shard) * length
            reach = jnp.int32(LOCAL_BAND_KEYS)
            for tile in verticals:
                reach = jnp.where(tile == k_shard, jnp.int32(1 << 30), reach)
            allowed = (distance >= 0) & (distance < reach)
            for offset in offsets:
                allowed |= (distance >= offset) & (distance < offset + SLASH_W)
            return jnp.where(allowed, 0.0, MASKED)

        rows = jnp.zeros((block_rows, width), jnp.float32)
        before = jnp.int32(0)
        for s in range(heads):
            q_shard = first + s
            shards = [c ^ (heads + k) for k in range(len(far))] + [first + t for t in range(s + 1)]
            bias = jnp.concatenate([bias_of(q_shard, shard) for shard in shards], 1)
            seen = len(shards) * length
            rows_at = s * group * length
            scores = lax.dot_general(
                q_all[rows_at : rows_at + group * length, :],
                k_all[0:seen, :],
                (((1,), (1,)), ((), ())),
                preferred_element_type=jnp.float32,
            )
            scores = (scores.reshape(group, length, seen) + bias[None]).reshape(group * length, seen)
            top = jnp.max(scores, axis=1, keepdims=True)
            weights = jnp.exp2((scores - top) * factor)
            total = jnp.sum(weights, axis=1, keepdims=True)
            mixed = jnp.dot(
                weights.astype(jnp.bfloat16), v_all[0:seen, :], preferred_element_type=jnp.float32
            )
            mixed = (mixed / total).astype(jnp.bfloat16)
            for g in range(group):
                mixed_all[s * length : (s + 1) * length, g * hd : (g + 1) * hd] = mixed[
                    g * length : (g + 1) * length
                ]
            count = count_ref[q_shard]
            kept = kept_all[s * PAD_ROWS : s * PAD_ROWS + 1, :].astype(jnp.int32)
            token = lax.broadcasted_iota(jnp.int32, (length, hd), 0)
            is_token = (token == kept).astype(jnp.float32).astype(jnp.bfloat16)
            index = lax.broadcasted_iota(jnp.int32, (hd, block_rows), 0)
            place = lax.broadcasted_iota(jnp.int32, (hd, block_rows), 1)
            is_place = ((place - index == before) & (index < count)).astype(jnp.float32)
            chooser = jnp.dot(
                is_token, is_place.astype(jnp.bfloat16), preferred_element_type=jnp.float32
            ).astype(jnp.bfloat16)
            rows = rows + lax.dot_general(
                chooser,
                mixed_all[s * length : (s + 1) * length, :],
                (((0,), (0,)), ((), ())),
                preferred_element_type=jnp.float32,
            )
            before = before + count
        rows_ref[...] = rows.astype(jnp.bfloat16)
        for k in range(heads):
            at = pl.multiple_of((slot ^ k) * length, length)
            out_refs[k][...] = mixed_all[pl.ds(at, length), :]

    return pl.pallas_call(
        body,
        out_shape=[pltpu.VMEM((length, width), jnp.bfloat16)] * heads
        + [pltpu.VMEM((block_rows, width), jnp.bfloat16)],
        in_specs=[SMEM] * 4 + [VMEM] * (heads + len(far)),
        out_specs=[VMEM] * (heads + 1),
        scratch_shapes=[
            pltpu.VMEM((heads * group * length, hd), jnp.bfloat16),
            pltpu.VMEM((keys, hd), jnp.bfloat16),
            pltpu.VMEM((keys, hd), jnp.bfloat16),
            pltpu.VMEM((heads * PAD_ROWS, hd), jnp.float32),
            pltpu.VMEM((heads * length, width), jnp.bfloat16),
        ],
        name="attention",
    )(shard_index, slash, tiles, counts, *near, *far)


def project(shard_index, core_index, own_rows, other_rows, weights):
    heads = len(weights)
    count = own_rows.shape[0]
    outs = weights[0].shape[0]

    def body(c_ref, h_ref, own_ref, other_ref, *rest):
        w_refs, (keep_ref, send_ref) = rest[:heads], rest[heads:]
        slot = c_ref[0] % heads
        keeps_own = c_ref[0] // heads == h_ref[0]
        own, other = own_ref[...], other_ref[...]
        both = jnp.concatenate(
            [jnp.where(keeps_own, own, other), jnp.where(keeps_own, other, own)], 0
        )
        for j in range(heads):
            at = pl.multiple_of((slot ^ j) * outs, HEAD_SIZE)
            share = lax.dot_general(
                both, w_refs[j][...], (((1,), (1,)), ((), ())), preferred_element_type=jnp.float32
            )
            keep_ref[:, pl.ds(at, outs)] = share[:count]
            send_ref[:, pl.ds(at, outs)] = share[count:]

    return pl.pallas_call(
        body,
        out_shape=[pltpu.VMEM((count, heads * outs), jnp.float32)] * 2,
        in_specs=[SMEM] * 2 + [VMEM] * (2 + heads),
        out_specs=[VMEM] * 2,
        name="project",
    )(shard_index, core_index, own_rows, other_rows, *weights)


def split_rows(shard_index, kept, received, heads):
    keep_rows = kept.shape[0] // heads

    def body(c_ref, a_ref, b_ref, *out):
        slot = c_ref[0] % heads
        for j in range(heads):
            at = pl.multiple_of((slot ^ j) * keep_rows, 8)
            out[j][...] = (a_ref[pl.ds(at, keep_rows), :] + b_ref[pl.ds(at, keep_rows), :]).astype(
                jnp.bfloat16
            )

    return pl.pallas_call(
        body,
        out_shape=[pltpu.VMEM((keep_rows, kept.shape[1]), jnp.bfloat16)] * heads,
        in_specs=[SMEM, VMEM, VMEM],
        out_specs=[VMEM] * heads,
        name="split_rows",
    )(shard_index, kept, received)


def join_heads(shard_index, pieces):
    heads = len(pieces)
    length, width = pieces[0].shape

    def body(c_ref, *rest):
        slot = c_ref[0] % heads
        for j in range(heads):
            at = pl.multiple_of((slot ^ j) * width, HEAD_SIZE)
            rest[heads][:, pl.ds(at, width)] = rest[j][...]

    return pl.pallas_call(
        body,
        out_shape=jax.ShapeDtypeStruct((length, heads * width), jnp.bfloat16),
        in_specs=[SMEM] + [VMEM] * heads,
        out_specs=VMEM,
        name="join_heads",
    )(shard_index, *pieces)


def local_blocks(
    query_tensor,
    key_tensor,
    value_tensor,
    slash_offsets,
    vertical_tiles,
    kept_rows,
    kept_count,
    out_weight,
):
    size = lax.axis_size("ctx")
    cores = lax.axis_size("head")
    heads = key_tensor.shape[1] // HEAD_SIZE
    keep_rows = query_tensor.shape[0] // 8
    c = lax.axis_index("ctx").astype(jnp.int32)
    shard_index = c.reshape(1)
    core_index = lax.axis_index("head").astype(jnp.int32).reshape(1)

    def move(x, axis, pairs):
        return in_vmem(lax.ppermute(x, axis, pairs))

    def swap(x, k):
        return move(x, "ctx", xor_pairs(size, k))

    packed = pack_heads(shard_index, query_tensor, key_tensor, value_tensor, kept_rows, heads)
    near = [in_vmem(packed[0])] + [swap(packed[k], k) for k in range(1, heads)]
    far = []
    for k in range(heads, size):
        pairs = [(i, i ^ k) for i in range(size) if i // heads < (i ^ k) // heads]
        far.append(move(packed[heads + k % heads], "ctx", pairs))
    packed_weight = pack_weight(shard_index, out_weight, heads)
    weights = [in_vmem(packed_weight[0])]
    weights += [swap(packed_weight[k], k) for k in range(1, heads)]
    *mixed, rows = attention(
        shard_index, slash_offsets.T, vertical_tiles.T, kept_count, near, far, keep_rows
    )
    other_rows = move(rows, "ctx", xor_pairs(size, heads))
    returned = [in_vmem(mixed[0])] + [swap(mixed[k], k) for k in range(1, heads)]
    attended = join_heads(shard_index, returned)
    kept, sent = project(shard_index, core_index, in_vmem(rows), other_rows, weights)
    received = move(sent, "head", [(i, cores - 1 - i) for i in range(cores)])
    shares = split_rows(shard_index, in_vmem(kept), received, heads)
    total = jnp.zeros(shares[0].shape, jnp.float32)
    for k in range(heads):
        pairs = []
        for i in range(size):
            for h in range(cores):
                target = heads * h + ((i % heads) ^ k)
                pairs.append((i * cores + h, target * cores + i // heads))
        share = lax.ppermute(shares[k], ("ctx", "head"), pairs)
        total = total + share.astype(jnp.float32)
    return (attended, total.astype(jnp.bfloat16))


def shifted_2(x, axis, by):
    size = lax.axis_size(axis)
    pairs = [(i, i + by) for i in range(size) if 0 <= i + by < size]
    return lax.ppermute(x, axis, pairs)


def broadcast(x, axis, root):
    mine = lax.axis_index(axis) == root
    return lax.psum(jnp.where(mine, x, jnp.zeros_like(x)), axis)


def attend(
    query_rows,
    key_slab,
    value_slab,
    key_pos,
    query_pos,
    slash_shift_list,
    tile_list,
    column_kind,
    group_width,
):
    scores = jnp.dot(query_rows, key_slab.T, preferred_element_type=jnp.float32) * key_slab.shape[
        -1
    ] ** (-0.5)
    distance = query_pos[:, None] - key_pos[None, :]
    key_tile = jnp.where(key_pos >= 0, key_pos // VTILE, -1)
    vertical = jnp.any(key_tile[:, None] == tile_list[None, :], axis=1)[None, :]
    in_band = (distance >= 0) & (distance < LOCAL_BAND_KEYS) & ~vertical
    first_slash = (
        (distance >= slash_shift_list[0]) & (distance < slash_shift_list[0] + SLASH_W) & ~vertical
    )
    second_slash = (
        (distance >= slash_shift_list[1]) & (distance < slash_shift_list[1] + SLASH_W) & ~vertical
    )
    earlier = in_band | first_slash
    kinds = column_kind[None, :]
    allowed = jnp.where(
        kinds == 0,
        in_band,
        jnp.where(
            kinds == 1,
            first_slash & ~in_band,
            jnp.where(kinds == 2, second_slash & ~earlier, distance >= 0),
        ),
    )
    allowed = jnp.tile(allowed & (key_pos >= 0)[None, :], (group_width, 1))
    masked = jnp.where(allowed, scores, -jnp.inf)
    row_max = jnp.max(masked, axis=1, keepdims=True)
    weights = jnp.where(allowed, jnp.exp(masked - row_max), 0.0)
    row_sum = jnp.sum(weights, axis=1, keepdims=True)
    blended = jnp.dot(weights.astype(jnp.bfloat16), value_slab, preferred_element_type=jnp.float32)
    return (blended / row_sum).astype(jnp.bfloat16)


def heads_first(stacked, local_heads, head_dim):
    reordered = jnp.moveaxis(stacked, -2, 0)
    return reordered.reshape(local_heads, -1, head_dim)


def move_near(row_block, is_live, offset, target_slot, keep_rows, sender):
    slot_grid = jnp.arange(keep_rows, dtype=jnp.int32)[:, None]
    gathered = jnp.zeros((keep_rows, row_block.shape[1]), jnp.float32)
    for travel in range(-3, 4):
        chooser = (
            (slot_grid == target_slot[None, :]) & (offset[None, :] == travel) & is_live[None, :]
        ).astype(jnp.bfloat16)
        parcel = jnp.dot(chooser, row_block, preferred_element_type=jnp.float32).astype(
            jnp.bfloat16
        )
        if travel != 0:
            parcel = sender(parcel, travel)
        gathered = gathered + parcel.astype(jnp.float32)
    return gathered.astype(jnp.bfloat16)


def local(
    query_tensor,
    key_tensor,
    value_tensor,
    slash_offsets,
    vertical_tiles,
    kept_rows,
    kept_count,
    out_weight,
):
    shard_length = query_tensor.shape[0]
    head_dim = HEAD_SIZE
    local_heads = key_tensor.shape[1] // head_dim
    group_width = query_tensor.shape[1] // key_tensor.shape[1]
    shard_index = lax.axis_index("ctx")
    first_pos = shard_index * shard_length
    key_heads = key_tensor.reshape(shard_length, local_heads, head_dim)
    value_heads = value_tensor.reshape(shard_length, local_heads, head_dim)
    slash_spans = slash_offsets // shard_length
    own_pair = jnp.stack([key_heads, value_heads])
    moving = jnp.concatenate([own_pair, own_pair], 0)
    member_spans = jnp.stack(
        [slash_spans[:, 0], slash_spans[:, 0], slash_spans[:, 1], slash_spans[:, 1]]
    )
    for bit_number in range((SLASH_SPAN - 1).bit_length()):
        shifted = shifted_2(moving, "ctx", 1 << bit_number)
        head_flags = (member_spans >> bit_number & 1 == 1)[:, None, :, None]
        moving = jnp.where(head_flags, shifted, moving)
    nearby = jnp.concatenate([moving, own_pair], 0)
    distances = [nearby]
    for _ in range(2):
        nearby = shifted_2(nearby, "ctx", 1)
        distances.append(nearby)
    ordered = jnp.stack([distances[2], distances[1], distances[0]])
    band_pieces = ordered[:, 4:6]
    slash_pieces = jnp.stack([ordered[:, 0:2], ordered[:, 2:4]])
    tile_keys = []
    tile_values = []
    for head_number in range(local_heads):
        for tile_index in range(VTILES):
            fetched = broadcast(
                jnp.stack([key_heads[:, head_number], value_heads[:, head_number]]),
                "ctx",
                vertical_tiles[head_number, tile_index],
            )
            tile_keys.append(fetched[0])
            tile_values.append(fetched[1])
    all_keys = jnp.concatenate(
        [
            heads_first(band_pieces[:, 0], local_heads, head_dim),
            heads_first(slash_pieces[:, :, 0], local_heads, head_dim),
            jnp.stack(tile_keys).reshape(local_heads, VTILES * shard_length, head_dim),
        ],
        1,
    )
    all_values = jnp.concatenate(
        [
            heads_first(band_pieces[:, 1], local_heads, head_dim),
            heads_first(slash_pieces[:, :, 1], local_heads, head_dim),
            jnp.stack(tile_values).reshape(local_heads, VTILES * shard_length, head_dim),
        ],
        1,
    )
    window = jnp.arange(3 * shard_length, dtype=jnp.int32)
    band_pos = jnp.broadcast_to(
        first_pos - 2 * shard_length + window, (local_heads, 3 * shard_length)
    )
    slash_pos = first_pos - (slash_spans[:, :, None] + 2) * shard_length + window[None, None, :]
    tile_pos = (
        vertical_tiles[:, :, None] * shard_length
        + jnp.arange(shard_length, dtype=jnp.int32)[None, None, :]
    )
    key_pos = jnp.concatenate(
        [band_pos, slash_pos.reshape(local_heads, -1), tile_pos.reshape(local_heads, -1)], 1
    )
    column_kind = jnp.concatenate(
        [
            jnp.full((3 * shard_length,), 0, jnp.int32),
            jnp.full((3 * shard_length,), 1, jnp.int32),
            jnp.full((3 * shard_length,), 2, jnp.int32),
            jnp.full((VTILES * shard_length,), 3, jnp.int32),
        ]
    )
    query_pos = first_pos + jnp.arange(shard_length, dtype=jnp.int32)
    query_heads = (
        query_tensor.reshape(shard_length, local_heads, group_width, head_dim)
        .transpose(1, 2, 0, 3)
        .reshape(local_heads, group_width * shard_length, head_dim)
    )

    def attend_head(packed):
        return attend(
            packed[0],
            packed[1],
            packed[2],
            packed[3],
            query_pos,
            packed[4],
            packed[5],
            column_kind,
            group_width,
        )

    mixed_heads = lax.map(
        attend_head, (query_heads, all_keys, all_values, key_pos, slash_offsets, vertical_tiles)
    )
    attended = (
        mixed_heads.reshape(local_heads, group_width, shard_length, head_dim)
        .transpose(2, 0, 1, 3)
        .reshape(shard_length, -1)
    )
    keep_rows = shard_length // 8
    capacity = kept_rows.shape[1]
    starts = jnp.cumsum(kept_count) - kept_count
    slot_ids = jnp.arange(capacity, dtype=jnp.int32)
    is_live = slot_ids < kept_count[shard_index]
    placed_at = starts[shard_index] + slot_ids
    target_shard = placed_at // keep_rows
    target_slot = placed_at % keep_rows
    offset = target_shard - shard_index
    selected = jnp.take(attended, kept_rows[0], axis=0)
    rounded = lax.psum_scatter(
        lax.dot_general(
            selected,
            lax.all_gather(out_weight, "ctx", axis=0, tiled=True),
            (((1,), (1,)), ((), ())),
            preferred_element_type=jnp.float32,
        ),
        "head",
        scatter_dimension=1,
        tiled=True,
    ).astype(jnp.bfloat16)

    def send_output(parcel, travel):
        return shifted_2(parcel, "ctx", travel)

    projected = move_near(rounded, is_live, offset, target_slot, keep_rows, send_output)
    return (attended, projected)


def solution(mesh):
    placed = (
        P(("groups", "ctx"), "head"),
        P(("groups", "ctx"), "head"),
        P(("groups", "ctx"), "head"),
        P(("groups", "head"), None),
        P(("groups", "head"), None),
        P(("groups", "ctx"), None),
        P("groups"),
        P("ctx", "head"),
    )
    size, cores = mesh.shape["ctx"], mesh.shape["head"]

    def blocks_fit(args):
        heads = args[1].shape[1] // cores // HEAD_SIZE
        length = args[0].shape[0] // size // mesh.shape["groups"]
        power = size & (size - 1) == 0 and heads & (heads - 1) == 0
        whole_tiles = length == VTILE and args[5].shape[1] <= HEAD_SIZE
        return power and whole_tiles and cores == 2 and size == heads * cores

    def sharded(body):
        return jax.shard_map(
            body,
            mesh=mesh,
            in_specs=placed,
            out_specs=(P(("groups", "ctx"), "head"), P(("groups", "ctx"), "head")),
            check_vma=False,
        )

    def program(*args):
        if not blocks_fit(args):
            return sharded(local)(*args)
        return sharded(local_blocks)(*args)

    return program
```

```python
import math

import jax
import jax.numpy as jnp
from jax import lax
from jax.experimental import pallas as pl
from jax.experimental.pallas import tpu as pltpu
from jax.sharding import PartitionSpec as P


HEAD_SIZE = 128
SLASH_SPAN = 8
VTILES = 2
LOCAL_BAND_KEYS = 256
SLASH_W = 128
VTILE = 128
PAD_ROWS = 8
MASKED = -1e30


SMEM = pl.BlockSpec(memory_space=pltpu.SMEM)
VMEM = pl.BlockSpec(memory_space=pltpu.VMEM)


def xor_pairs(size, k):
    return [(i, i ^ k) for i in range(size)]


def in_vmem(x):
    return pltpu.with_memory_space_constraint(x, pltpu.VMEM)


def pack_heads(shard_index, query, key, value, kept_rows, heads):
    length = query.shape[0]
    width = query.shape[1] // heads
    hd = HEAD_SIZE
    capacity = kept_rows.shape[1]
    total = 2 * hd + width

    def body(c_ref, q_ref, k_ref, v_ref, kept_ref, *out):
        slot = c_ref[0] % heads
        kept = jnp.zeros((PAD_ROWS, total), jnp.bfloat16)
        for j in range(heads):
            head = slot ^ j
            q_at = pl.multiple_of(head * width, hd)
            k_at = pl.multiple_of(head * hd, hd)
            k, v = k_ref[:, pl.ds(k_at, hd)], v_ref[:, pl.ds(k_at, hd)]
            out[j][0:length, 0:hd] = k
            out[j][0:length, hd : 2 * hd] = v
            out[j][0:length, 2 * hd :] = q_ref[:, pl.ds(q_at, width)]
            out[j][length:, :] = kept
            out[j][length : length + 1, 0:capacity] = (
                kept_ref[...].astype(jnp.float32).astype(jnp.bfloat16)
            )
            out[heads + j][:, 0:hd] = k
            out[heads + j][:, hd:] = v

    return pl.pallas_call(
        body,
        out_shape=[pltpu.VMEM((length + PAD_ROWS, total), jnp.bfloat16)] * heads
        + [pltpu.VMEM((length, 2 * hd), jnp.bfloat16)] * heads,
        in_specs=[SMEM] + [VMEM] * 4,
        out_specs=[VMEM] * (2 * heads),
        name="pack_heads",
    )(shard_index, query, key, value, kept_rows)


def pack_weight(shard_index, weight, heads):
    width = weight.shape[1] // heads

    def body(c_ref, w_ref, *out):
        slot = c_ref[0] % heads
        for j in range(heads):
            at = pl.multiple_of((slot ^ j) * width, HEAD_SIZE)
            out[j][...] = w_ref[:, pl.ds(at, width)]

    return pl.pallas_call(
        body,
        out_shape=[pltpu.VMEM((weight.shape[0], width), jnp.bfloat16)] * heads,
        in_specs=[SMEM, VMEM],
        out_specs=[VMEM] * heads,
        name="pack_weight",
    )(shard_index, weight)


def mask_tiles(shard_index, slash, shards, length):
    def body(c_ref, slash_ref, out_ref):
        slot = c_ref[0] % slash_ref.shape[1]
        difference = lax.broadcasted_iota(jnp.int32, (length, length), 0) - lax.broadcasted_iota(
            jnp.int32, (length, length), 1
        )
        for d in range(shards):
            distance = difference + d * length
            allowed = (distance >= 0) & (distance < LOCAL_BAND_KEYS)
            for i in range(slash_ref.shape[0]):
                offset = slash_ref[i, slot]
                allowed |= (distance >= offset) & (distance < offset + SLASH_W)
            out_ref[d * length : (d + 1) * length, :] = jnp.where(allowed, 0.0, MASKED)
        out_ref[shards * length : (shards + 1) * length, :] = jnp.where(difference >= 0, 0.0, MASKED)
        rest = lax.broadcasted_iota(jnp.int32, (2 * length, length), 0)
        out_ref[(shards + 1) * length :, :] = jnp.where(rest < length, 0.0, MASKED)

    return pl.pallas_call(
        body,
        out_shape=pltpu.VMEM(((shards + 3) * length, length), jnp.float32),
        in_specs=[SMEM, SMEM],
        out_specs=VMEM,
        name="mask_tiles",
    )(shard_index, slash)


def attention(shard_index, tiles, counts, masks, near, far, keep_rows):
    heads = len(near)
    length = near[0].shape[0] - PAD_ROWS
    hd = HEAD_SIZE
    width = near[0].shape[1] - 2 * hd
    group = width // hd
    size = heads + len(far)
    far_keys = len(far) * length
    keys = far_keys + heads * length
    block_rows = heads * keep_rows
    factor = hd ** (-0.5) * math.log2(math.e)

    def body(c_ref, tile_ref, count_ref, mask_ref, *rest):
        near_refs, rest = rest[:heads], rest[heads:]
        far_refs, rest = rest[: len(far)], rest[len(far) :]
        out_refs, rows_ref = rest[:heads], rest[heads]
        q_all, k_all, v_all, kept_all, mixed_all = rest[heads + 1 :]
        c = c_ref[0]
        slot = c % heads
        first = c - slot
        for k in range(len(far)):
            k_all[k * length : (k + 1) * length, :] = far_refs[k][:, 0:hd]
            v_all[k * length : (k + 1) * length, 0:hd] = far_refs[k][:, hd:]
        v_all[:, hd:] = jnp.ones((keys, hd), jnp.bfloat16)
        for k in range(heads):
            to = slot ^ k
            at = pl.ds(pl.multiple_of(far_keys + to * length, length), length)
            k_all[at, :] = near_refs[k][0:length, 0:hd]
            v_all[at, 0:hd] = near_refs[k][0:length, hd : 2 * hd]
            for g in range(group):
                q_at = pl.multiple_of((to * group + g) * length, length)
                q_all[pl.ds(q_at, length), :] = near_refs[k][
                    0:length, (2 + g) * hd : (3 + g) * hd
                ]
            kept_at = pl.ds(pl.multiple_of(to * PAD_ROWS, PAD_ROWS), PAD_ROWS)
            kept_all[kept_at, :] = near_refs[k][length:, 0:hd].astype(jnp.float32)
        verticals = [tile_ref[i, slot] for i in range(VTILES)]

        def mask_of(q_shard, k_shard):
            back = q_shard - k_shard
            entry = back
            for tile in verticals:
                vertical = size + jnp.where(back == 0, 0, 1)
                entry = jnp.where(tile == k_shard, vertical, entry)
            entry = jnp.where(back < 0, size + 2, entry)
            return mask_ref[pl.ds(pl.multiple_of(entry * length, length), length), :]

        rows = jnp.zeros((block_rows, width), jnp.float32)
        before = jnp.int32(0)
        for s in range(heads):
            q_shard = first + s
            shards = [c ^ (heads + k) for k in range(len(far))] + [first + t for t in range(s + 1)]
            mask = jnp.concatenate([mask_of(q_shard, shard) for shard in shards], 1)
            seen = len(shards) * length
            rows_at = s * group * length
            scores = lax.dot_general(
                q_all[rows_at : rows_at + group * length, :],
                k_all[0:seen, :],
                (((1,), (1,)), ((), ())),
                preferred_element_type=jnp.float32,
            )
            scores = scores.reshape(group, length, seen) * factor + mask[None]
            scores = scores.reshape(group * length, seen)
            weights = jnp.exp2(scores - jnp.max(scores, axis=1, keepdims=True))
            mixed = jnp.dot(
                weights.astype(jnp.bfloat16), v_all[0:seen, :], preferred_element_type=jnp.float32
            )
            mixed = (mixed[:, :hd] / mixed[:, hd:]).astype(jnp.bfloat16)
            for g in range(group):
                mixed_all[s * length : (s + 1) * length, g * hd : (g + 1) * hd] = mixed[
                    g * length : (g + 1) * length
                ]
            count = count_ref[q_shard]
            kept = kept_all[s * PAD_ROWS : s * PAD_ROWS + 1, :].astype(jnp.int32)
            token = lax.broadcasted_iota(jnp.int32, (length, hd), 0)
            is_token = (token == kept).astype(jnp.float32).astype(jnp.bfloat16)
            index = lax.broadcasted_iota(jnp.int32, (hd, block_rows), 0)
            place = lax.broadcasted_iota(jnp.int32, (hd, block_rows), 1)
            is_place = ((place - index == before) & (index < count)).astype(jnp.float32)
            chooser = jnp.dot(
                is_token, is_place.astype(jnp.bfloat16), preferred_element_type=jnp.float32
            ).astype(jnp.bfloat16)
            rows = rows + lax.dot_general(
                chooser,
                mixed_all[s * length : (s + 1) * length, :],
                (((0,), (0,)), ((), ())),
                preferred_element_type=jnp.float32,
            )
            before = before + count
        rows_ref[...] = rows.astype(jnp.bfloat16)
        for k in range(heads):
            at = pl.multiple_of((slot ^ k) * length, length)
            out_refs[k][...] = mixed_all[pl.ds(at, length), :]

    return pl.pallas_call(
        body,
        out_shape=[pltpu.VMEM((length, width), jnp.bfloat16)] * heads
        + [pltpu.VMEM((block_rows, width), jnp.bfloat16)],
        in_specs=[SMEM] * 3 + [VMEM] * (1 + heads + len(far)),
        out_specs=[VMEM] * (heads + 1),
        scratch_shapes=[
            pltpu.VMEM((heads * group * length, hd), jnp.bfloat16),
            pltpu.VMEM((keys, hd), jnp.bfloat16),
            pltpu.VMEM((keys, 2 * hd), jnp.bfloat16),
            pltpu.VMEM((heads * PAD_ROWS, hd), jnp.float32),
            pltpu.VMEM((heads * length, width), jnp.bfloat16),
        ],
        name="attention",
    )(shard_index, tiles, counts, masks, *near, *far)


def project(shard_index, core_index, own_rows, other_rows, weights):
    heads = len(weights)
    count = own_rows.shape[0]
    outs = weights[0].shape[0]

    def body(c_ref, h_ref, own_ref, other_ref, *rest):
        w_refs, (keep_ref, send_ref) = rest[:heads], rest[heads:]
        slot = c_ref[0] % heads
        keeps_own = c_ref[0] // heads == h_ref[0]
        own, other = own_ref[...], other_ref[...]
        both = jnp.concatenate(
            [jnp.where(keeps_own, own, other), jnp.where(keeps_own, other, own)], 0
        )
        for j in range(heads):
            at = pl.multiple_of((slot ^ j) * outs, HEAD_SIZE)
            share = lax.dot_general(
                both, w_refs[j][...], (((1,), (1,)), ((), ())), preferred_element_type=jnp.float32
            )
            keep_ref[:, pl.ds(at, outs)] = share[:count]
            send_ref[:, pl.ds(at, outs)] = share[count:]

    return pl.pallas_call(
        body,
        out_shape=[pltpu.VMEM((count, heads * outs), jnp.float32)] * 2,
        in_specs=[SMEM] * 2 + [VMEM] * (2 + heads),
        out_specs=[VMEM] * 2,
        name="project",
    )(shard_index, core_index, own_rows, other_rows, *weights)


def split_rows(shard_index, kept, received, heads):
    keep_rows = kept.shape[0] // heads

    def body(c_ref, a_ref, b_ref, *out):
        slot = c_ref[0] % heads
        for j in range(heads):
            at = pl.multiple_of((slot ^ j) * keep_rows, 8)
            out[j][...] = (a_ref[pl.ds(at, keep_rows), :] + b_ref[pl.ds(at, keep_rows), :]).astype(
                jnp.bfloat16
            )

    return pl.pallas_call(
        body,
        out_shape=[pltpu.VMEM((keep_rows, kept.shape[1]), jnp.bfloat16)] * heads,
        in_specs=[SMEM, VMEM, VMEM],
        out_specs=[VMEM] * heads,
        name="split_rows",
    )(shard_index, kept, received)


def join_heads(shard_index, pieces):
    heads = len(pieces)
    length, width = pieces[0].shape

    def body(c_ref, *rest):
        slot = c_ref[0] % heads
        for j in range(heads):
            at = pl.multiple_of((slot ^ j) * width, HEAD_SIZE)
            rest[heads][:, pl.ds(at, width)] = rest[j][...]

    return pl.pallas_call(
        body,
        out_shape=jax.ShapeDtypeStruct((length, heads * width), jnp.bfloat16),
        in_specs=[SMEM] + [VMEM] * heads,
        out_specs=VMEM,
        name="join_heads",
    )(shard_index, *pieces)


def local_blocks(
    query_tensor,
    key_tensor,
    value_tensor,
    slash_offsets,
    vertical_tiles,
    kept_rows,
    kept_count,
    out_weight,
):
    size = lax.axis_size("ctx")
    cores = lax.axis_size("head")
    heads = key_tensor.shape[1] // HEAD_SIZE
    keep_rows = query_tensor.shape[0] // 8
    c = lax.axis_index("ctx").astype(jnp.int32)
    shard_index = c.reshape(1)
    core_index = lax.axis_index("head").astype(jnp.int32).reshape(1)

    def move(x, axis, pairs):
        return in_vmem(lax.ppermute(x, axis, pairs))

    def swap(x, k):
        return move(x, "ctx", xor_pairs(size, k))

    packed = pack_heads(shard_index, query_tensor, key_tensor, value_tensor, kept_rows, heads)
    near = [in_vmem(packed[0])] + [swap(packed[k], k) for k in range(1, heads)]
    far = []
    for k in range(heads, size):
        pairs = [(i, i ^ k) for i in range(size) if i // heads < (i ^ k) // heads]
        far.append(move(packed[heads + k % heads], "ctx", pairs))
    packed_weight = pack_weight(shard_index, out_weight, heads)
    weights = [in_vmem(packed_weight[0])]
    weights += [swap(packed_weight[k], k) for k in range(1, heads)]
    masks = in_vmem(mask_tiles(shard_index, slash_offsets.T, size, query_tensor.shape[0]))
    *mixed, rows = attention(
        shard_index, vertical_tiles.T, kept_count, masks, near, far, keep_rows
    )
    other_rows = move(rows, "ctx", xor_pairs(size, heads))
    returned = [in_vmem(mixed[0])] + [swap(mixed[k], k) for k in range(1, heads)]
    attended = join_heads(shard_index, returned)
    kept, sent = project(shard_index, core_index, in_vmem(rows), other_rows, weights)
    received = move(sent, "head", [(i, cores - 1 - i) for i in range(cores)])
    shares = split_rows(shard_index, in_vmem(kept), received, heads)
    total = jnp.zeros(shares[0].shape, jnp.float32)
    for k in range(heads):
        pairs = []
        for i in range(size):
            for h in range(cores):
                target = heads * h + ((i % heads) ^ k)
                pairs.append((i * cores + h, target * cores + i // heads))
        share = lax.ppermute(shares[k], ("ctx", "head"), pairs)
        total = total + share.astype(jnp.float32)
    return (attended, total.astype(jnp.bfloat16))


def shifted_2(x, axis, by):
    size = lax.axis_size(axis)
    pairs = [(i, i + by) for i in range(size) if 0 <= i + by < size]
    return lax.ppermute(x, axis, pairs)


def broadcast(x, axis, root):
    mine = lax.axis_index(axis) == root
    return lax.psum(jnp.where(mine, x, jnp.zeros_like(x)), axis)


def attend(
    query_rows,
    key_slab,
    value_slab,
    key_pos,
    query_pos,
    slash_shift_list,
    tile_list,
    column_kind,
    group_width,
):
    scores = jnp.dot(query_rows, key_slab.T, preferred_element_type=jnp.float32) * key_slab.shape[
        -1
    ] ** (-0.5)
    distance = query_pos[:, None] - key_pos[None, :]
    key_tile = jnp.where(key_pos >= 0, key_pos // VTILE, -1)
    vertical = jnp.any(key_tile[:, None] == tile_list[None, :], axis=1)[None, :]
    in_band = (distance >= 0) & (distance < LOCAL_BAND_KEYS) & ~vertical
    first_slash = (
        (distance >= slash_shift_list[0]) & (distance < slash_shift_list[0] + SLASH_W) & ~vertical
    )
    second_slash = (
        (distance >= slash_shift_list[1]) & (distance < slash_shift_list[1] + SLASH_W) & ~vertical
    )
    earlier = in_band | first_slash
    kinds = column_kind[None, :]
    allowed = jnp.where(
        kinds == 0,
        in_band,
        jnp.where(
            kinds == 1,
            first_slash & ~in_band,
            jnp.where(kinds == 2, second_slash & ~earlier, distance >= 0),
        ),
    )
    allowed = jnp.tile(allowed & (key_pos >= 0)[None, :], (group_width, 1))
    masked = jnp.where(allowed, scores, -jnp.inf)
    row_max = jnp.max(masked, axis=1, keepdims=True)
    weights = jnp.where(allowed, jnp.exp(masked - row_max), 0.0)
    row_sum = jnp.sum(weights, axis=1, keepdims=True)
    blended = jnp.dot(weights.astype(jnp.bfloat16), value_slab, preferred_element_type=jnp.float32)
    return (blended / row_sum).astype(jnp.bfloat16)


def heads_first(stacked, local_heads, head_dim):
    reordered = jnp.moveaxis(stacked, -2, 0)
    return reordered.reshape(local_heads, -1, head_dim)


def move_near(row_block, is_live, offset, target_slot, keep_rows, sender):
    slot_grid = jnp.arange(keep_rows, dtype=jnp.int32)[:, None]
    gathered = jnp.zeros((keep_rows, row_block.shape[1]), jnp.float32)
    for travel in range(-3, 4):
        chooser = (
            (slot_grid == target_slot[None, :]) & (offset[None, :] == travel) & is_live[None, :]
        ).astype(jnp.bfloat16)
        parcel = jnp.dot(chooser, row_block, preferred_element_type=jnp.float32).astype(
            jnp.bfloat16
        )
        if travel != 0:
            parcel = sender(parcel, travel)
        gathered = gathered + parcel.astype(jnp.float32)
    return gathered.astype(jnp.bfloat16)


def local(
    query_tensor,
    key_tensor,
    value_tensor,
    slash_offsets,
    vertical_tiles,
    kept_rows,
    kept_count,
    out_weight,
):
    shard_length = query_tensor.shape[0]
    head_dim = HEAD_SIZE
    local_heads = key_tensor.shape[1] // head_dim
    group_width = query_tensor.shape[1] // key_tensor.shape[1]
    shard_index = lax.axis_index("ctx")
    first_pos = shard_index * shard_length
    key_heads = key_tensor.reshape(shard_length, local_heads, head_dim)
    value_heads = value_tensor.reshape(shard_length, local_heads, head_dim)
    slash_spans = slash_offsets // shard_length
    own_pair = jnp.stack([key_heads, value_heads])
    moving = jnp.concatenate([own_pair, own_pair], 0)
    member_spans = jnp.stack(
        [slash_spans[:, 0], slash_spans[:, 0], slash_spans[:, 1], slash_spans[:, 1]]
    )
    for bit_number in range((SLASH_SPAN - 1).bit_length()):
        shifted = shifted_2(moving, "ctx", 1 << bit_number)
        head_flags = (member_spans >> bit_number & 1 == 1)[:, None, :, None]
        moving = jnp.where(head_flags, shifted, moving)
    nearby = jnp.concatenate([moving, own_pair], 0)
    distances = [nearby]
    for _ in range(2):
        nearby = shifted_2(nearby, "ctx", 1)
        distances.append(nearby)
    ordered = jnp.stack([distances[2], distances[1], distances[0]])
    band_pieces = ordered[:, 4:6]
    slash_pieces = jnp.stack([ordered[:, 0:2], ordered[:, 2:4]])
    tile_keys = []
    tile_values = []
    for head_number in range(local_heads):
        for tile_index in range(VTILES):
            fetched = broadcast(
                jnp.stack([key_heads[:, head_number], value_heads[:, head_number]]),
                "ctx",
                vertical_tiles[head_number, tile_index],
            )
            tile_keys.append(fetched[0])
            tile_values.append(fetched[1])
    all_keys = jnp.concatenate(
        [
            heads_first(band_pieces[:, 0], local_heads, head_dim),
            heads_first(slash_pieces[:, :, 0], local_heads, head_dim),
            jnp.stack(tile_keys).reshape(local_heads, VTILES * shard_length, head_dim),
        ],
        1,
    )
    all_values = jnp.concatenate(
        [
            heads_first(band_pieces[:, 1], local_heads, head_dim),
            heads_first(slash_pieces[:, :, 1], local_heads, head_dim),
            jnp.stack(tile_values).reshape(local_heads, VTILES * shard_length, head_dim),
        ],
        1,
    )
    window = jnp.arange(3 * shard_length, dtype=jnp.int32)
    band_pos = jnp.broadcast_to(
        first_pos - 2 * shard_length + window, (local_heads, 3 * shard_length)
    )
    slash_pos = first_pos - (slash_spans[:, :, None] + 2) * shard_length + window[None, None, :]
    tile_pos = (
        vertical_tiles[:, :, None] * shard_length
        + jnp.arange(shard_length, dtype=jnp.int32)[None, None, :]
    )
    key_pos = jnp.concatenate(
        [band_pos, slash_pos.reshape(local_heads, -1), tile_pos.reshape(local_heads, -1)], 1
    )
    column_kind = jnp.concatenate(
        [
            jnp.full((3 * shard_length,), 0, jnp.int32),
            jnp.full((3 * shard_length,), 1, jnp.int32),
            jnp.full((3 * shard_length,), 2, jnp.int32),
            jnp.full((VTILES * shard_length,), 3, jnp.int32),
        ]
    )
    query_pos = first_pos + jnp.arange(shard_length, dtype=jnp.int32)
    query_heads = (
        query_tensor.reshape(shard_length, local_heads, group_width, head_dim)
        .transpose(1, 2, 0, 3)
        .reshape(local_heads, group_width * shard_length, head_dim)
    )

    def attend_head(packed):
        return attend(
            packed[0],
            packed[1],
            packed[2],
            packed[3],
            query_pos,
            packed[4],
            packed[5],
            column_kind,
            group_width,
        )

    mixed_heads = lax.map(
        attend_head, (query_heads, all_keys, all_values, key_pos, slash_offsets, vertical_tiles)
    )
    attended = (
        mixed_heads.reshape(local_heads, group_width, shard_length, head_dim)
        .transpose(2, 0, 1, 3)
        .reshape(shard_length, -1)
    )
    keep_rows = shard_length // 8
    capacity = kept_rows.shape[1]
    starts = jnp.cumsum(kept_count) - kept_count
    slot_ids = jnp.arange(capacity, dtype=jnp.int32)
    is_live = slot_ids < kept_count[shard_index]
    placed_at = starts[shard_index] + slot_ids
    target_shard = placed_at // keep_rows
    target_slot = placed_at % keep_rows
    offset = target_shard - shard_index
    selected = jnp.take(attended, kept_rows[0], axis=0)
    rounded = lax.psum_scatter(
        lax.dot_general(
            selected,
            lax.all_gather(out_weight, "ctx", axis=0, tiled=True),
            (((1,), (1,)), ((), ())),
            preferred_element_type=jnp.float32,
        ),
        "head",
        scatter_dimension=1,
        tiled=True,
    ).astype(jnp.bfloat16)

    def send_output(parcel, travel):
        return shifted_2(parcel, "ctx", travel)

    projected = move_near(rounded, is_live, offset, target_slot, keep_rows, send_output)
    return (attended, projected)


def solution(mesh):
    placed = (
        P(("groups", "ctx"), "head"),
        P(("groups", "ctx"), "head"),
        P(("groups", "ctx"), "head"),
        P(("groups", "head"), None),
        P(("groups", "head"), None),
        P(("groups", "ctx"), None),
        P("groups"),
        P("ctx", "head"),
    )
    size, cores = mesh.shape["ctx"], mesh.shape["head"]

    def blocks_fit(args):
        heads = args[1].shape[1] // cores // HEAD_SIZE
        length = args[0].shape[0] // size // mesh.shape["groups"]
        power = size & (size - 1) == 0 and heads & (heads - 1) == 0
        whole_tiles = length == VTILE and args[5].shape[1] <= HEAD_SIZE
        return power and whole_tiles and cores == 2 and size == heads * cores

    def sharded(body):
        return jax.shard_map(
            body,
            mesh=mesh,
            in_specs=placed,
            out_specs=(P(("groups", "ctx"), "head"), P(("groups", "ctx"), "head")),
            check_vma=False,
        )

    def program(*args):
        if not blocks_fit(args):
            return sharded(local)(*args)
        return sharded(local_blocks)(*args)

    return program
```

```python
import math

import jax
import jax.numpy as jnp
from jax import lax
from jax.experimental import pallas as pl
from jax.experimental.pallas import tpu as pltpu
from jax.sharding import PartitionSpec as P


HEAD_SIZE = 128
SLASH_SPAN = 8
VTILES = 2
LOCAL_BAND_KEYS = 256
SLASH_W = 128
VTILE = 128
PAD_ROWS = 8
MASKED = -1e30


ANY = pl.BlockSpec(memory_space=pl.ANY)
SMEM = pl.BlockSpec(memory_space=pltpu.SMEM)
VMEM = pl.BlockSpec(memory_space=pltpu.VMEM)
GRANT = pltpu.CompilerParams(vmem_limit_bytes=16 << 20)


def xor_pairs(size, k):
    return [(i, i ^ k) for i in range(size)]


def in_vmem(x):
    return pltpu.with_memory_space_constraint(x, pltpu.VMEM)


def in_hbm(x):
    return pltpu.with_memory_space_constraint(x, pltpu.HBM)


def start_all(copies, sems):
    started = [
        pltpu.make_async_copy(source, target, sems.at[number])
        for number, (source, target) in enumerate(copies)
    ]
    for copy in started:
        copy.start()
    return started


def pack_heads(shard_index, query, key, value, kept_rows, heads):
    length = query.shape[0]
    width = query.shape[1] // heads
    hd = HEAD_SIZE
    capacity = kept_rows.shape[1]
    total = 2 * hd + width

    def body(c_ref, q_ref, k_ref, v_ref, kept_ref, *rest):
        out, (kept_buf, sems) = rest[: 2 * heads], rest[2 * heads :]
        slot = c_ref[0] % heads
        copies = [(kept_ref, kept_buf)]
        for j in range(heads):
            head = slot ^ j
            q_from = q_ref.at[:, pl.ds(pl.multiple_of(head * width, hd), width)]
            k_from = k_ref.at[:, pl.ds(pl.multiple_of(head * hd, hd), hd)]
            v_from = v_ref.at[:, pl.ds(pl.multiple_of(head * hd, hd), hd)]
            rows = pl.ds(0, length)
            copies += [
                (q_from, out[j].at[rows, pl.ds(2 * hd, width)]),
                (k_from, out[j].at[rows, pl.ds(0, hd)]),
                (v_from, out[j].at[rows, pl.ds(hd, hd)]),
                (k_from, out[heads + j].at[:, pl.ds(0, hd)]),
                (v_from, out[heads + j].at[:, pl.ds(hd, hd)]),
            ]
        started = start_all(copies, sems)
        for j in range(heads):
            out[j][length:, :] = jnp.zeros((PAD_ROWS, total), jnp.bfloat16)
        started[0].wait()
        kept = kept_buf[...].astype(jnp.float32).astype(jnp.bfloat16)
        for j in range(heads):
            out[j][length : length + 1, 0:capacity] = kept
        for copy in started[1:]:
            copy.wait()

    return pl.pallas_call(
        body,
        out_shape=[pltpu.VMEM((length + PAD_ROWS, total), jnp.bfloat16)] * heads
        + [pltpu.VMEM((length, 2 * hd), jnp.bfloat16)] * heads,
        in_specs=[SMEM] + [ANY] * 4,
        out_specs=[VMEM] * (2 * heads),
        scratch_shapes=[
            pltpu.VMEM((1, capacity), jnp.int32),
            pltpu.SemaphoreType.DMA((1 + 5 * heads,)),
        ],
        compiler_params=GRANT,
        name="pack_heads",
    )(shard_index, in_hbm(query), in_hbm(key), in_hbm(value), in_hbm(kept_rows))


def pack_weight(shard_index, group_index, weight, heads):
    width = weight.shape[1] // heads
    outs = weight.shape[0]
    counts = [outs] * (heads - 1) + [outs // 2]

    def body(c_ref, g_ref, w_ref, *rest):
        out, sems = rest[:heads], rest[heads]
        slot = c_ref[0] % heads
        copies = []
        for j in range(heads):
            at = pl.multiple_of((slot ^ j) * width, HEAD_SIZE)
            first = pl.multiple_of(g_ref[0] * counts[j], counts[j]) if counts[j] < outs else 0
            copies.append((w_ref.at[pl.ds(first, counts[j]), pl.ds(at, width)], out[j]))
        for copy in start_all(copies, sems):
            copy.wait()

    return pl.pallas_call(
        body,
        out_shape=[pltpu.VMEM((count, width), jnp.bfloat16) for count in counts],
        in_specs=[SMEM, SMEM, ANY],
        out_specs=[VMEM] * heads,
        scratch_shapes=[pltpu.SemaphoreType.DMA((heads,))],
        compiler_params=GRANT,
        name="pack_weight",
    )(shard_index, group_index, in_hbm(weight))


def mask_tiles(shard_index, slash, tiles, counts, length):
    heads = slash.shape[1]
    size = counts.shape[0]
    lanes = HEAD_SIZE

    def body(c_ref, slash_ref, tile_ref, count_ref, out_ref, table_ref, tile_buf):
        c = c_ref[0]
        slot = c % heads
        first = c - slot
        difference = lax.broadcasted_iota(jnp.int32, (length, length), 0) - lax.broadcasted_iota(
            jnp.int32, (length, length), 1
        )
        for d in range(size):
            distance = difference + d * length
            allowed = (distance >= 0) & (distance < LOCAL_BAND_KEYS)
            for i in range(slash_ref.shape[0]):
                offset = slash_ref[i, slot]
                allowed |= (distance >= offset) & (distance < offset + SLASH_W)
            tile_buf[d] = jnp.where(allowed, 0.0, MASKED)
        tile_buf[size] = jnp.where(difference >= 0, 0.0, MASKED)
        tile_buf[size + 1] = jnp.zeros((length, length), jnp.float32)
        tile_buf[size + 2] = jnp.full((length, length), MASKED, jnp.float32)
        before = jnp.int32(0)
        for s in range(heads):
            shards = [c ^ k for k in range(heads, size)] + [first + t for t in range(s + 1)]
            for number, k_shard in enumerate(shards):
                back = first + s - k_shard
                entry = back
                for i in range(tile_ref.shape[0]):
                    vertical = size + jnp.where(back == 0, 0, 1)
                    entry = jnp.where(tile_ref[i, slot] == k_shard, vertical, entry)
                entry = jnp.where(back < 0, size + 2, entry)
                out_ref[s, :, number * length : (number + 1) * length] = tile_buf[entry]
            count = count_ref[first + s]
            table_ref[s, 0:1, :] = jnp.full((1, lanes), count, jnp.int32)
            table_ref[s, 1:2, :] = jnp.full((1, lanes), before, jnp.int32)
            before = before + count

    return pl.pallas_call(
        body,
        out_shape=[
            pltpu.VMEM((heads, length, size * length), jnp.float32),
            pltpu.VMEM((heads, 8, lanes), jnp.int32),
        ],
        in_specs=[SMEM] * 4,
        out_specs=[VMEM] * 2,
        scratch_shapes=[pltpu.VMEM((size + 3, length, length), jnp.float32)],
        compiler_params=GRANT,
        name="mask_tiles",
    )(shard_index, in_hbm(slash), in_hbm(tiles), in_hbm(counts))


def attention(shard_index, masks, table, near, far, keep_rows):
    heads = len(near)
    length = near[0].shape[0] - PAD_ROWS
    hd = HEAD_SIZE
    width = near[0].shape[1] - 2 * hd
    group = width // hd
    far_keys = len(far) * length
    keys = far_keys + heads * length
    block_rows = heads * keep_rows
    factor = hd ** (-0.5) * math.log2(math.e)

    def body(c_ref, mask_ref, table_ref, *rest):
        near_refs, rest = rest[:heads], rest[heads:]
        far_refs, rest = rest[: len(far)], rest[len(far) :]
        out_refs, rows_ref = rest[:heads], rest[heads]
        q_all, k_all, v_all, kept_all, mixed_all = rest[heads + 1 :]
        slot = c_ref[0] % heads
        for k in range(len(far)):
            k_all[k * length : (k + 1) * length, :] = far_refs[k][:, 0:hd]
            v_all[k * length : (k + 1) * length, 0:hd] = far_refs[k][:, hd:]
        v_all[:, hd:] = jnp.ones((keys, hd), jnp.bfloat16)
        for k in range(heads):
            to = slot ^ k
            at = pl.ds(pl.multiple_of(far_keys + to * length, length), length)
            k_all[at, :] = near_refs[k][0:length, 0:hd]
            v_all[at, 0:hd] = near_refs[k][0:length, hd : 2 * hd]
            for g in range(group):
                q_at = pl.multiple_of((to * group + g) * length, length)
                q_all[pl.ds(q_at, length), :] = near_refs[k][
                    0:length, (2 + g) * hd : (3 + g) * hd
                ]
            kept_at = pl.ds(pl.multiple_of(to * PAD_ROWS, PAD_ROWS), PAD_ROWS)
            kept_all[kept_at, :] = near_refs[k][length:, 0:hd].astype(jnp.float32)
        rows = jnp.zeros((block_rows, width), jnp.float32)
        for s in range(heads):
            seen = far_keys + (s + 1) * length
            rows_at = s * group * length
            scores = lax.dot_general(
                q_all[rows_at : rows_at + group * length, :],
                k_all[0:seen, :],
                (((1,), (1,)), ((), ())),
                preferred_element_type=jnp.float32,
            )
            scores = scores.reshape(group, length, seen) * factor + mask_ref[s, :, 0:seen][None]
            scores = scores.reshape(group * length, seen)
            weights = jnp.exp2(scores - jnp.max(scores, axis=1, keepdims=True))
            mixed = jnp.dot(
                weights.astype(jnp.bfloat16), v_all[0:seen, :], preferred_element_type=jnp.float32
            )
            mixed = (mixed[:, :hd] / mixed[:, hd:]).astype(jnp.bfloat16)
            for g in range(group):
                mixed_all[s * length : (s + 1) * length, g * hd : (g + 1) * hd] = mixed[
                    g * length : (g + 1) * length
                ]
            kept = kept_all[s * PAD_ROWS : s * PAD_ROWS + 1, :].astype(jnp.int32)
            token = lax.broadcasted_iota(jnp.int32, (length, hd), 0)
            is_token = (token == kept).astype(jnp.float32).astype(jnp.bfloat16)
            index = lax.broadcasted_iota(jnp.int32, (hd, block_rows), 0)
            place = lax.broadcasted_iota(jnp.int32, (hd, block_rows), 1)
            count, before = table_ref[s, 0:1, 0:block_rows], table_ref[s, 1:2, 0:block_rows]
            is_place = ((place - index == before) & (index < count)).astype(jnp.float32)
            chooser = jnp.dot(
                is_token, is_place.astype(jnp.bfloat16), preferred_element_type=jnp.float32
            ).astype(jnp.bfloat16)
            rows = rows + lax.dot_general(
                chooser,
                mixed_all[s * length : (s + 1) * length, :],
                (((0,), (0,)), ((), ())),
                preferred_element_type=jnp.float32,
            )
        rows_ref[...] = rows.astype(jnp.bfloat16)
        for k in range(heads):
            at = pl.multiple_of((slot ^ k) * length, length)
            out_refs[k][...] = mixed_all[pl.ds(at, length), :]

    return pl.pallas_call(
        body,
        out_shape=[pltpu.VMEM((length, width), jnp.bfloat16)] * heads
        + [pltpu.VMEM((block_rows, width), jnp.bfloat16)],
        in_specs=[SMEM] + [VMEM] * (2 + heads + len(far)),
        out_specs=[VMEM] * (heads + 1),
        scratch_shapes=[
            pltpu.VMEM((heads * group * length, hd), jnp.bfloat16),
            pltpu.VMEM((keys, hd), jnp.bfloat16),
            pltpu.VMEM((keys, 2 * hd), jnp.bfloat16),
            pltpu.VMEM((heads * PAD_ROWS, hd), jnp.float32),
            pltpu.VMEM((heads * length, width), jnp.bfloat16),
        ],
        compiler_params=GRANT,
        name="attention",
    )(shard_index, masks, table, *near, *far)


def project(shard_index, core_index, group_index, own_rows, other_rows, weights):
    heads = len(weights) - 1
    count = own_rows.shape[0]
    outs = weights[0].shape[0]

    def body(c_ref, h_ref, g_ref, own_ref, other_ref, *rest):
        w_refs, (keep_ref, send_ref) = rest[: heads + 1], rest[heads + 1 :]
        slot = c_ref[0] % heads
        keeps_own = c_ref[0] // heads == h_ref[0]
        own, other = own_ref[...], other_ref[...]
        both = jnp.concatenate(
            [jnp.where(keeps_own, own, other), jnp.where(keeps_own, other, own)], 0
        )
        half = outs // 2
        last = (slot ^ (heads - 1)) * outs
        starts = [(slot ^ j) * outs for j in range(heads - 1)]
        starts += [last + g_ref[0] * half, last + (1 - g_ref[0]) * half]
        for w_ref, start in zip(w_refs, starts):
            at = pl.ds(pl.multiple_of(start, HEAD_SIZE), w_ref.shape[0])
            share = lax.dot_general(
                both, w_ref[...], (((1,), (1,)), ((), ())), preferred_element_type=jnp.float32
            )
            keep_ref[:, at] = share[:count]
            send_ref[:, at] = share[count:]

    return pl.pallas_call(
        body,
        out_shape=[pltpu.VMEM((count, heads * outs), jnp.float32)] * 2,
        in_specs=[SMEM] * 3 + [VMEM] * (3 + heads),
        out_specs=[VMEM] * 2,
        compiler_params=GRANT,
        name="project",
    )(shard_index, core_index, group_index, own_rows, other_rows, *weights)


def split_rows(shard_index, kept, received, heads):
    keep_rows = kept.shape[0] // heads

    def body(c_ref, a_ref, b_ref, *out):
        slot = c_ref[0] % heads
        for j in range(heads):
            at = pl.multiple_of((slot ^ j) * keep_rows, 8)
            out[j][...] = (a_ref[pl.ds(at, keep_rows), :] + b_ref[pl.ds(at, keep_rows), :]).astype(
                jnp.bfloat16
            )

    return pl.pallas_call(
        body,
        out_shape=[pltpu.VMEM((keep_rows, kept.shape[1]), jnp.bfloat16)] * heads,
        in_specs=[SMEM, VMEM, VMEM],
        out_specs=[VMEM] * heads,
        compiler_params=GRANT,
        name="split_rows",
    )(shard_index, kept, received)


def add_shares(shares):
    def body(*rest):
        total = rest[0][...].astype(jnp.float32)
        for share in rest[1:-1]:
            total = total + share[...].astype(jnp.float32)
        rest[-1][...] = total.astype(jnp.bfloat16)

    return pl.pallas_call(
        body,
        out_shape=pltpu.VMEM(shares[0].shape, jnp.bfloat16),
        in_specs=[VMEM] * len(shares),
        out_specs=VMEM,
        compiler_params=GRANT,
        name="add_shares",
    )(*shares)


def join_heads(shard_index, pieces):
    heads = len(pieces)
    length, width = pieces[0].shape

    def body(c_ref, *rest):
        ins, (out_ref, sems) = rest[:heads], rest[heads:]
        slot = c_ref[0] % heads
        copies = []
        for j in range(heads):
            at = pl.multiple_of((slot ^ j) * width, HEAD_SIZE)
            copies.append((ins[j], out_ref.at[:, pl.ds(at, width)]))
        for copy in start_all(copies, sems):
            copy.wait()

    return pl.pallas_call(
        body,
        out_shape=pltpu.HBM((length, heads * width), jnp.bfloat16),
        in_specs=[SMEM] + [VMEM] * heads,
        out_specs=ANY,
        scratch_shapes=[pltpu.SemaphoreType.DMA((heads,))],
        compiler_params=GRANT,
        name="join_heads",
    )(shard_index, *pieces)


def local_blocks(
    query_tensor,
    key_tensor,
    value_tensor,
    slash_offsets,
    vertical_tiles,
    kept_rows,
    kept_count,
    out_weight,
):
    size = lax.axis_size("ctx")
    cores = lax.axis_size("head")
    heads = key_tensor.shape[1] // HEAD_SIZE
    keep_rows = query_tensor.shape[0] // 8
    c = lax.axis_index("ctx").astype(jnp.int32)
    shard_index = c.reshape(1)
    group_index = lax.axis_index("groups").astype(jnp.int32).reshape(1)
    core_index = lax.axis_index("head").astype(jnp.int32).reshape(1)

    def move(x, axis, pairs):
        return in_vmem(lax.ppermute(x, axis, pairs))

    def swap(x, k):
        return move(x, "ctx", xor_pairs(size, k))

    packed = pack_heads(shard_index, query_tensor, key_tensor, value_tensor, kept_rows, heads)
    near = [in_vmem(packed[0])] + [swap(packed[k], k) for k in range(1, heads)]
    far = []
    for k in range(heads, size):
        pairs = [(i, i ^ k) for i in range(size) if i // heads < (i ^ k) // heads]
        far.append(move(packed[heads + k % heads], "ctx", pairs))
    packed_weight = pack_weight(shard_index, group_index, out_weight, heads)
    weights = [in_vmem(packed_weight[0])]
    weights += [swap(packed_weight[k], k) for k in range(1, heads)]
    weights.append(move(weights[-1], "groups", [(0, 1), (1, 0)]))
    masks, table = mask_tiles(
        shard_index, slash_offsets.T, vertical_tiles.T, kept_count, query_tensor.shape[0]
    )
    *mixed, rows = attention(shard_index, in_vmem(masks), in_vmem(table), near, far, keep_rows)
    other_rows = move(rows, "ctx", xor_pairs(size, heads))
    returned = [in_vmem(mixed[0])] + [swap(mixed[k], k) for k in range(1, heads)]
    kept, sent = project(shard_index, core_index, group_index, in_vmem(rows), other_rows, weights)
    received = move(sent, "head", [(i, cores - 1 - i) for i in range(cores)])
    shares = split_rows(shard_index, in_vmem(kept), received, heads)
    parts = [in_vmem(shares[0])] + [swap(shares[k], k) for k in range(1, heads)]
    summed = add_shares(parts)
    pairs = []
    for i in range(size):
        for h in range(cores):
            pairs.append((i * cores + h, (heads * h + i % heads) * cores + i // heads))
    projected = in_hbm(lax.ppermute(summed, ("ctx", "head"), pairs))
    return (join_heads(shard_index, returned), projected)


def shifted_2(x, axis, by):
    size = lax.axis_size(axis)
    pairs = [(i, i + by) for i in range(size) if 0 <= i + by < size]
    return lax.ppermute(x, axis, pairs)


def broadcast(x, axis, root):
    mine = lax.axis_index(axis) == root
    return lax.psum(jnp.where(mine, x, jnp.zeros_like(x)), axis)


def attend(
    query_rows,
    key_slab,
    value_slab,
    key_pos,
    query_pos,
    slash_shift_list,
    tile_list,
    column_kind,
    group_width,
):
    scores = jnp.dot(query_rows, key_slab.T, preferred_element_type=jnp.float32) * key_slab.shape[
        -1
    ] ** (-0.5)
    distance = query_pos[:, None] - key_pos[None, :]
    key_tile = jnp.where(key_pos >= 0, key_pos // VTILE, -1)
    vertical = jnp.any(key_tile[:, None] == tile_list[None, :], axis=1)[None, :]
    in_band = (distance >= 0) & (distance < LOCAL_BAND_KEYS) & ~vertical
    first_slash = (
        (distance >= slash_shift_list[0]) & (distance < slash_shift_list[0] + SLASH_W) & ~vertical
    )
    second_slash = (
        (distance >= slash_shift_list[1]) & (distance < slash_shift_list[1] + SLASH_W) & ~vertical
    )
    earlier = in_band | first_slash
    kinds = column_kind[None, :]
    allowed = jnp.where(
        kinds == 0,
        in_band,
        jnp.where(
            kinds == 1,
            first_slash & ~in_band,
            jnp.where(kinds == 2, second_slash & ~earlier, distance >= 0),
        ),
    )
    allowed = jnp.tile(allowed & (key_pos >= 0)[None, :], (group_width, 1))
    masked = jnp.where(allowed, scores, -jnp.inf)
    row_max = jnp.max(masked, axis=1, keepdims=True)
    weights = jnp.where(allowed, jnp.exp(masked - row_max), 0.0)
    row_sum = jnp.sum(weights, axis=1, keepdims=True)
    blended = jnp.dot(weights.astype(jnp.bfloat16), value_slab, preferred_element_type=jnp.float32)
    return (blended / row_sum).astype(jnp.bfloat16)


def heads_first(stacked, local_heads, head_dim):
    reordered = jnp.moveaxis(stacked, -2, 0)
    return reordered.reshape(local_heads, -1, head_dim)


def move_near(row_block, is_live, offset, target_slot, keep_rows, sender):
    slot_grid = jnp.arange(keep_rows, dtype=jnp.int32)[:, None]
    gathered = jnp.zeros((keep_rows, row_block.shape[1]), jnp.float32)
    for travel in range(-3, 4):
        chooser = (
            (slot_grid == target_slot[None, :]) & (offset[None, :] == travel) & is_live[None, :]
        ).astype(jnp.bfloat16)
        parcel = jnp.dot(chooser, row_block, preferred_element_type=jnp.float32).astype(
            jnp.bfloat16
        )
        if travel != 0:
            parcel = sender(parcel, travel)
        gathered = gathered + parcel.astype(jnp.float32)
    return gathered.astype(jnp.bfloat16)


def local(
    query_tensor,
    key_tensor,
    value_tensor,
    slash_offsets,
    vertical_tiles,
    kept_rows,
    kept_count,
    out_weight,
):
    shard_length = query_tensor.shape[0]
    head_dim = HEAD_SIZE
    local_heads = key_tensor.shape[1] // head_dim
    group_width = query_tensor.shape[1] // key_tensor.shape[1]
    shard_index = lax.axis_index("ctx")
    first_pos = shard_index * shard_length
    key_heads = key_tensor.reshape(shard_length, local_heads, head_dim)
    value_heads = value_tensor.reshape(shard_length, local_heads, head_dim)
    slash_spans = slash_offsets // shard_length
    own_pair = jnp.stack([key_heads, value_heads])
    moving = jnp.concatenate([own_pair, own_pair], 0)
    member_spans = jnp.stack(
        [slash_spans[:, 0], slash_spans[:, 0], slash_spans[:, 1], slash_spans[:, 1]]
    )
    for bit_number in range((SLASH_SPAN - 1).bit_length()):
        shifted = shifted_2(moving, "ctx", 1 << bit_number)
        head_flags = (member_spans >> bit_number & 1 == 1)[:, None, :, None]
        moving = jnp.where(head_flags, shifted, moving)
    nearby = jnp.concatenate([moving, own_pair], 0)
    distances = [nearby]
    for _ in range(2):
        nearby = shifted_2(nearby, "ctx", 1)
        distances.append(nearby)
    ordered = jnp.stack([distances[2], distances[1], distances[0]])
    band_pieces = ordered[:, 4:6]
    slash_pieces = jnp.stack([ordered[:, 0:2], ordered[:, 2:4]])
    tile_keys = []
    tile_values = []
    for head_number in range(local_heads):
        for tile_index in range(VTILES):
            fetched = broadcast(
                jnp.stack([key_heads[:, head_number], value_heads[:, head_number]]),
                "ctx",
                vertical_tiles[head_number, tile_index],
            )
            tile_keys.append(fetched[0])
            tile_values.append(fetched[1])
    all_keys = jnp.concatenate(
        [
            heads_first(band_pieces[:, 0], local_heads, head_dim),
            heads_first(slash_pieces[:, :, 0], local_heads, head_dim),
            jnp.stack(tile_keys).reshape(local_heads, VTILES * shard_length, head_dim),
        ],
        1,
    )
    all_values = jnp.concatenate(
        [
            heads_first(band_pieces[:, 1], local_heads, head_dim),
            heads_first(slash_pieces[:, :, 1], local_heads, head_dim),
            jnp.stack(tile_values).reshape(local_heads, VTILES * shard_length, head_dim),
        ],
        1,
    )
    window = jnp.arange(3 * shard_length, dtype=jnp.int32)
    band_pos = jnp.broadcast_to(
        first_pos - 2 * shard_length + window, (local_heads, 3 * shard_length)
    )
    slash_pos = first_pos - (slash_spans[:, :, None] + 2) * shard_length + window[None, None, :]
    tile_pos = (
        vertical_tiles[:, :, None] * shard_length
        + jnp.arange(shard_length, dtype=jnp.int32)[None, None, :]
    )
    key_pos = jnp.concatenate(
        [band_pos, slash_pos.reshape(local_heads, -1), tile_pos.reshape(local_heads, -1)], 1
    )
    column_kind = jnp.concatenate(
        [
            jnp.full((3 * shard_length,), 0, jnp.int32),
            jnp.full((3 * shard_length,), 1, jnp.int32),
            jnp.full((3 * shard_length,), 2, jnp.int32),
            jnp.full((VTILES * shard_length,), 3, jnp.int32),
        ]
    )
    query_pos = first_pos + jnp.arange(shard_length, dtype=jnp.int32)
    query_heads = (
        query_tensor.reshape(shard_length, local_heads, group_width, head_dim)
        .transpose(1, 2, 0, 3)
        .reshape(local_heads, group_width * shard_length, head_dim)
    )

    def attend_head(packed):
        return attend(
            packed[0],
            packed[1],
            packed[2],
            packed[3],
            query_pos,
            packed[4],
            packed[5],
            column_kind,
            group_width,
        )

    mixed_heads = lax.map(
        attend_head, (query_heads, all_keys, all_values, key_pos, slash_offsets, vertical_tiles)
    )
    attended = (
        mixed_heads.reshape(local_heads, group_width, shard_length, head_dim)
        .transpose(2, 0, 1, 3)
        .reshape(shard_length, -1)
    )
    keep_rows = shard_length // 8
    capacity = kept_rows.shape[1]
    starts = jnp.cumsum(kept_count) - kept_count
    slot_ids = jnp.arange(capacity, dtype=jnp.int32)
    is_live = slot_ids < kept_count[shard_index]
    placed_at = starts[shard_index] + slot_ids
    target_shard = placed_at // keep_rows
    target_slot = placed_at % keep_rows
    offset = target_shard - shard_index
    selected = jnp.take(attended, kept_rows[0], axis=0)
    rounded = lax.psum_scatter(
        lax.dot_general(
            selected,
            lax.all_gather(out_weight, "ctx", axis=0, tiled=True),
            (((1,), (1,)), ((), ())),
            preferred_element_type=jnp.float32,
        ),
        "head",
        scatter_dimension=1,
        tiled=True,
    ).astype(jnp.bfloat16)

    def send_output(parcel, travel):
        return shifted_2(parcel, "ctx", travel)

    projected = move_near(rounded, is_live, offset, target_slot, keep_rows, send_output)
    return (attended, projected)


def solution(mesh):
    placed = (
        P(("groups", "ctx"), "head"),
        P(("groups", "ctx"), "head"),
        P(("groups", "ctx"), "head"),
        P(("groups", "head"), None),
        P(("groups", "head"), None),
        P(("groups", "ctx"), None),
        P("groups"),
        P("ctx", "head"),
    )
    size, cores = mesh.shape["ctx"], mesh.shape["head"]

    def blocks_fit(args):
        heads = args[1].shape[1] // cores // HEAD_SIZE
        length = args[0].shape[0] // size // mesh.shape["groups"]
        power = size & (size - 1) == 0 and heads & (heads - 1) == 0
        whole_tiles = length == VTILE and args[5].shape[1] <= HEAD_SIZE
        pairs = cores == 2 and mesh.shape["groups"] == 2 and args[7].shape[0] // size % 256 == 0
        return power and whole_tiles and pairs and size == heads * cores

    def sharded(body):
        return jax.shard_map(
            body,
            mesh=mesh,
            in_specs=placed,
            out_specs=(P(("groups", "ctx"), "head"), P(("groups", "ctx"), "head")),
            check_vma=False,
        )

    def program(*args):
        if not blocks_fit(args):
            return sharded(local)(*args)
        return sharded(local_blocks)(*args)

    return program
```

```python
import math

import jax
import jax.numpy as jnp
from jax import lax
from jax.experimental import pallas as pl
from jax.experimental.pallas import tpu as pltpu
from jax.sharding import PartitionSpec as P


HEAD_SIZE = 128
SLASH_SPAN = 8
VTILES = 2
LOCAL_BAND_KEYS = 256
SLASH_W = 128
VTILE = 128
PAD_ROWS = 8
MASKED = -1e30


ANY = pl.BlockSpec(memory_space=pl.ANY)
SMEM = pl.BlockSpec(memory_space=pltpu.SMEM)
VMEM = pl.BlockSpec(memory_space=pltpu.VMEM)
GRANT = pltpu.CompilerParams(vmem_limit_bytes=16 << 20)


def xor_pairs(size, k):
    return [(i, i ^ k) for i in range(size)]


def in_vmem(x):
    return pltpu.with_memory_space_constraint(x, pltpu.VMEM)


def in_hbm(x):
    return pltpu.with_memory_space_constraint(x, pltpu.HBM)


def start_all(copies, sems):
    started = [
        pltpu.make_async_copy(source, target, sems.at[number])
        for number, (source, target) in enumerate(copies)
    ]
    for copy in started:
        copy.start()
    return started


def pack_heads(shard_index, query, key, value, kept_rows, heads):
    length = query.shape[0]
    width = query.shape[1] // heads
    hd = HEAD_SIZE
    capacity = kept_rows.shape[1]
    total = 2 * hd + width

    def body(c_ref, q_ref, k_ref, v_ref, kept_ref, *rest):
        out, (kept_buf, sems) = rest[: 2 * heads], rest[2 * heads :]
        slot = c_ref[0] % heads
        copies = [(kept_ref, kept_buf)]
        for j in range(heads):
            head = slot ^ j
            q_from = q_ref.at[:, pl.ds(pl.multiple_of(head * width, hd), width)]
            k_from = k_ref.at[:, pl.ds(pl.multiple_of(head * hd, hd), hd)]
            v_from = v_ref.at[:, pl.ds(pl.multiple_of(head * hd, hd), hd)]
            rows = pl.ds(0, length)
            copies += [
                (q_from, out[j].at[rows, pl.ds(2 * hd, width)]),
                (k_from, out[j].at[rows, pl.ds(0, hd)]),
                (v_from, out[j].at[rows, pl.ds(hd, hd)]),
                (k_from, out[heads + j].at[:, pl.ds(0, hd)]),
                (v_from, out[heads + j].at[:, pl.ds(hd, hd)]),
            ]
        started = start_all(copies, sems)
        for j in range(heads):
            out[j][length:, :] = jnp.zeros((PAD_ROWS, total), jnp.bfloat16)
        started[0].wait()
        kept = kept_buf[...].astype(jnp.float32).astype(jnp.bfloat16)
        for j in range(heads):
            out[j][length : length + 1, 0:capacity] = kept
        for copy in started[1:]:
            copy.wait()

    return pl.pallas_call(
        body,
        out_shape=[pltpu.VMEM((length + PAD_ROWS, total), jnp.bfloat16)] * heads
        + [pltpu.VMEM((length, 2 * hd), jnp.bfloat16)] * heads,
        in_specs=[SMEM] + [ANY] * 4,
        out_specs=[VMEM] * (2 * heads),
        scratch_shapes=[
            pltpu.VMEM((1, capacity), jnp.int32),
            pltpu.SemaphoreType.DMA((1 + 5 * heads,)),
        ],
        compiler_params=GRANT,
        name="pack_heads",
    )(shard_index, in_hbm(query), in_hbm(key), in_hbm(value), in_hbm(kept_rows))


def pack_weight(shard_index, group_index, slash, tiles, counts, weight, length):
    heads = slash.shape[1]
    size = counts.shape[0]
    lanes = HEAD_SIZE
    width = weight.shape[1] // heads
    outs = weight.shape[0]
    sent = [outs] * (heads - 1) + [outs // 2]

    def body(c_ref, g_ref, slash_ref, tile_ref, count_ref, w_ref, *rest):
        out, (mask_ref, table_ref, tile_buf, sems) = rest[:heads], rest[heads:]
        c = c_ref[0]
        slot = c % heads
        first = c - slot
        copies = []
        for j in range(heads):
            at = pl.multiple_of((slot ^ j) * width, HEAD_SIZE)
            row = pl.multiple_of(g_ref[0] * sent[j], sent[j]) if sent[j] < outs else 0
            copies.append((w_ref.at[pl.ds(row, sent[j]), pl.ds(at, width)], out[j]))
        started = start_all(copies, sems)
        difference = lax.broadcasted_iota(jnp.int32, (length, length), 0) - lax.broadcasted_iota(
            jnp.int32, (length, length), 1
        )
        for d in range(size):
            distance = difference + d * length
            allowed = (distance >= 0) & (distance < LOCAL_BAND_KEYS)
            for i in range(slash_ref.shape[0]):
                offset = slash_ref[i, slot]
                allowed |= (distance >= offset) & (distance < offset + SLASH_W)
            tile_buf[d] = jnp.where(allowed, 0.0, MASKED)
        tile_buf[size] = jnp.where(difference >= 0, 0.0, MASKED)
        tile_buf[size + 1] = jnp.zeros((length, length), jnp.float32)
        tile_buf[size + 2] = jnp.full((length, length), MASKED, jnp.float32)
        before = jnp.int32(0)
        for s in range(heads):
            shards = [c ^ k for k in range(heads, size)] + [first + t for t in range(s + 1)]
            for number, k_shard in enumerate(shards):
                back = first + s - k_shard
                entry = back
                for i in range(tile_ref.shape[0]):
                    vertical = size + jnp.where(back == 0, 0, 1)
                    entry = jnp.where(tile_ref[i, slot] == k_shard, vertical, entry)
                entry = jnp.where(back < 0, size + 2, entry)
                mask_ref[s, :, number * length : (number + 1) * length] = tile_buf[entry]
            count = count_ref[first + s]
            table_ref[s, 0:1, :] = jnp.full((1, lanes), count, jnp.int32)
            table_ref[s, 1:2, :] = jnp.full((1, lanes), before, jnp.int32)
            before = before + count
        for copy in started:
            copy.wait()

    return pl.pallas_call(
        body,
        out_shape=[pltpu.VMEM((count, width), jnp.bfloat16) for count in sent]
        + [
            pltpu.VMEM((heads, length, size * length), jnp.float32),
            pltpu.VMEM((heads, 8, lanes), jnp.int32),
        ],
        in_specs=[SMEM] * 5 + [ANY],
        out_specs=[VMEM] * (heads + 2),
        scratch_shapes=[
            pltpu.VMEM((size + 3, length, length), jnp.float32),
            pltpu.SemaphoreType.DMA((heads,)),
        ],
        compiler_params=GRANT,
        name="pack_weight",
    )(shard_index, group_index, in_hbm(slash), in_hbm(tiles), in_hbm(counts), in_hbm(weight))


def attention(shard_index, masks, table, near, far, keep_rows):
    heads = len(near)
    length = near[0].shape[0] - PAD_ROWS
    hd = HEAD_SIZE
    width = near[0].shape[1] - 2 * hd
    group = width // hd
    far_keys = len(far) * length
    keys = far_keys + heads * length
    block_rows = heads * keep_rows
    factor = hd ** (-0.5) * math.log2(math.e)

    def body(c_ref, mask_ref, table_ref, *rest):
        near_refs, rest = rest[:heads], rest[heads:]
        far_refs, rest = rest[: len(far)], rest[len(far) :]
        out_refs, rows_ref = rest[:heads], rest[heads]
        q_all, k_all, v_all, kept_all, mixed_all = rest[heads + 1 :]
        slot = c_ref[0] % heads
        for k in range(len(far)):
            k_all[k * length : (k + 1) * length, :] = far_refs[k][:, 0:hd]
            v_all[k * length : (k + 1) * length, 0:hd] = far_refs[k][:, hd:]
        v_all[:, hd:] = jnp.ones((keys, hd), jnp.bfloat16)
        for k in range(heads):
            to = slot ^ k
            at = pl.ds(pl.multiple_of(far_keys + to * length, length), length)
            k_all[at, :] = near_refs[k][0:length, 0:hd]
            v_all[at, 0:hd] = near_refs[k][0:length, hd : 2 * hd]
            for g in range(group):
                q_at = pl.multiple_of((to * group + g) * length, length)
                q_all[pl.ds(q_at, length), :] = near_refs[k][
                    0:length, (2 + g) * hd : (3 + g) * hd
                ]
            kept_at = pl.ds(pl.multiple_of(to * PAD_ROWS, PAD_ROWS), PAD_ROWS)
            kept_all[kept_at, :] = near_refs[k][length:, 0:hd].astype(jnp.float32)
        rows = jnp.zeros((block_rows, width), jnp.float32)

        def scores_of(step):
            s, part = step
            rows_at = (s * group + part * 2) * length
            return lax.dot_general(
                q_all[rows_at : rows_at + 2 * length, :],
                k_all[0 : far_keys + (s + 1) * length, :],
                (((1,), (1,)), ((), ())),
                preferred_element_type=jnp.float32,
            )

        steps = [(s, part) for s in range(heads) for part in range(group // 2)]
        ready = [scores_of(step) for step in steps[:1]]
        for number, (s, part) in enumerate(steps):
            if number + 1 < len(steps):
                ready.append(scores_of(steps[number + 1]))
            seen = far_keys + (s + 1) * length
            scores = ready.pop(0).reshape(2, length, seen) * factor + mask_ref[s, :, 0:seen][None]
            scores = scores.reshape(2 * length, seen)
            weights = jnp.exp2(scores - jnp.max(scores, axis=1, keepdims=True))
            mixed = jnp.dot(
                weights.astype(jnp.bfloat16), v_all[0:seen, :], preferred_element_type=jnp.float32
            )
            mixed = (mixed[:, :hd] / mixed[:, hd:]).astype(jnp.bfloat16)
            for g in range(2):
                at = (part * 2 + g) * hd
                mixed_all[s * length : (s + 1) * length, at : at + hd] = mixed[
                    g * length : (g + 1) * length
                ]
        for s in range(heads):
            kept = kept_all[s * PAD_ROWS : s * PAD_ROWS + 1, :].astype(jnp.int32)
            token = lax.broadcasted_iota(jnp.int32, (length, hd), 0)
            is_token = (token == kept).astype(jnp.float32).astype(jnp.bfloat16)
            index = lax.broadcasted_iota(jnp.int32, (hd, block_rows), 0)
            place = lax.broadcasted_iota(jnp.int32, (hd, block_rows), 1)
            count, before = table_ref[s, 0:1, 0:block_rows], table_ref[s, 1:2, 0:block_rows]
            is_place = ((place - index == before) & (index < count)).astype(jnp.float32)
            chooser = jnp.dot(
                is_token, is_place.astype(jnp.bfloat16), preferred_element_type=jnp.float32
            ).astype(jnp.bfloat16)
            rows = rows + lax.dot_general(
                chooser,
                mixed_all[s * length : (s + 1) * length, :],
                (((0,), (0,)), ((), ())),
                preferred_element_type=jnp.float32,
            )
        rows_ref[...] = rows.astype(jnp.bfloat16)
        for k in range(heads):
            at = pl.multiple_of((slot ^ k) * length, length)
            out_refs[k][...] = mixed_all[pl.ds(at, length), :]

    return pl.pallas_call(
        body,
        out_shape=[pltpu.VMEM((length, width), jnp.bfloat16)] * heads
        + [pltpu.VMEM((block_rows, width), jnp.bfloat16)],
        in_specs=[SMEM] + [VMEM] * (2 + heads + len(far)),
        out_specs=[VMEM] * (heads + 1),
        scratch_shapes=[
            pltpu.VMEM((heads * group * length, hd), jnp.bfloat16),
            pltpu.VMEM((keys, hd), jnp.bfloat16),
            pltpu.VMEM((keys, 2 * hd), jnp.bfloat16),
            pltpu.VMEM((heads * PAD_ROWS, hd), jnp.float32),
            pltpu.VMEM((heads * length, width), jnp.bfloat16),
        ],
        compiler_params=GRANT,
        name="attention",
    )(shard_index, masks, table, *near, *far)


def project(shard_index, core_index, group_index, own_rows, other_rows, weights):
    heads = len(weights) - 1
    count = own_rows.shape[0]
    outs = weights[0].shape[0]

    def body(c_ref, h_ref, g_ref, own_ref, other_ref, *rest):
        w_refs, (keep_ref, send_ref) = rest[: heads + 1], rest[heads + 1 :]
        slot = c_ref[0] % heads
        keeps_own = c_ref[0] // heads == h_ref[0]
        own, other = own_ref[...], other_ref[...]
        both = jnp.concatenate(
            [jnp.where(keeps_own, own, other), jnp.where(keeps_own, other, own)], 0
        )
        half = outs // 2
        last = (slot ^ (heads - 1)) * outs
        starts = [(slot ^ j) * outs for j in range(heads - 1)]
        starts += [last + g_ref[0] * half, last + (1 - g_ref[0]) * half]
        for w_ref, start in zip(w_refs, starts):
            at = pl.ds(pl.multiple_of(start, HEAD_SIZE), w_ref.shape[0])
            share = lax.dot_general(
                both, w_ref[...], (((1,), (1,)), ((), ())), preferred_element_type=jnp.float32
            )
            keep_ref[:, at] = share[:count]
            send_ref[:, at] = share[count:]

    return pl.pallas_call(
        body,
        out_shape=[pltpu.VMEM((count, heads * outs), jnp.float32)] * 2,
        in_specs=[SMEM] * 3 + [VMEM] * (3 + heads),
        out_specs=[VMEM] * 2,
        compiler_params=GRANT,
        name="project",
    )(shard_index, core_index, group_index, own_rows, other_rows, *weights)


def split_rows(shard_index, kept, received, heads):
    keep_rows = kept.shape[0] // heads

    def body(c_ref, a_ref, b_ref, *out):
        slot = c_ref[0] % heads
        for j in range(heads):
            at = pl.multiple_of((slot ^ j) * keep_rows, 8)
            out[j][...] = (a_ref[pl.ds(at, keep_rows), :] + b_ref[pl.ds(at, keep_rows), :]).astype(
                jnp.bfloat16
            )

    return pl.pallas_call(
        body,
        out_shape=[pltpu.VMEM((keep_rows, kept.shape[1]), jnp.bfloat16)] * heads,
        in_specs=[SMEM, VMEM, VMEM],
        out_specs=[VMEM] * heads,
        compiler_params=GRANT,
        name="split_rows",
    )(shard_index, kept, received)


def add_shares(shares):
    def body(*rest):
        total = rest[0][...].astype(jnp.float32)
        for share in rest[1:-1]:
            total = total + share[...].astype(jnp.float32)
        rest[-1][...] = total.astype(jnp.bfloat16)

    return pl.pallas_call(
        body,
        out_shape=pltpu.VMEM(shares[0].shape, jnp.bfloat16),
        in_specs=[VMEM] * len(shares),
        out_specs=VMEM,
        compiler_params=GRANT,
        name="add_shares",
    )(*shares)


def join_heads(shard_index, pieces):
    heads = len(pieces)
    length, width = pieces[0].shape

    def body(c_ref, *rest):
        ins, (out_ref, sems) = rest[:heads], rest[heads:]
        slot = c_ref[0] % heads
        copies = []
        for j in range(heads):
            at = pl.multiple_of((slot ^ j) * width, HEAD_SIZE)
            copies.append((ins[j], out_ref.at[:, pl.ds(at, width)]))
        for copy in start_all(copies, sems):
            copy.wait()

    return pl.pallas_call(
        body,
        out_shape=pltpu.HBM((length, heads * width), jnp.bfloat16),
        in_specs=[SMEM] + [VMEM] * heads,
        out_specs=ANY,
        scratch_shapes=[pltpu.SemaphoreType.DMA((heads,))],
        compiler_params=GRANT,
        name="join_heads",
    )(shard_index, *pieces)


def local_blocks(
    query_tensor,
    key_tensor,
    value_tensor,
    slash_offsets,
    vertical_tiles,
    kept_rows,
    kept_count,
    out_weight,
):
    size = lax.axis_size("ctx")
    cores = lax.axis_size("head")
    heads = key_tensor.shape[1] // HEAD_SIZE
    keep_rows = query_tensor.shape[0] // 8
    c = lax.axis_index("ctx").astype(jnp.int32)
    shard_index = c.reshape(1)
    group_index = lax.axis_index("groups").astype(jnp.int32).reshape(1)
    core_index = lax.axis_index("head").astype(jnp.int32).reshape(1)

    def move(x, axis, pairs):
        return in_vmem(lax.ppermute(x, axis, pairs))

    def swap(x, k):
        return move(x, "ctx", xor_pairs(size, k))

    packed = pack_heads(shard_index, query_tensor, key_tensor, value_tensor, kept_rows, heads)
    near = [in_vmem(packed[0])] + [swap(packed[k], k) for k in range(1, heads)]
    far = []
    for k in range(heads, size):
        pairs = [(i, i ^ k) for i in range(size) if i // heads < (i ^ k) // heads]
        far.append(move(packed[heads + k % heads], "ctx", pairs))
    *packed_weight, masks, table = pack_weight(
        shard_index,
        group_index,
        slash_offsets.T,
        vertical_tiles.T,
        kept_count,
        out_weight,
        query_tensor.shape[0],
    )
    weights = [in_vmem(packed_weight[0])]
    weights += [swap(packed_weight[k], k) for k in range(1, heads)]
    weights.append(move(weights[-1], "groups", [(0, 1), (1, 0)]))
    *mixed, rows = attention(shard_index, in_vmem(masks), in_vmem(table), near, far, keep_rows)
    other_rows = move(rows, "ctx", xor_pairs(size, heads))
    returned = [in_vmem(mixed[0])] + [swap(mixed[k], k) for k in range(1, heads)]
    kept, sent = project(shard_index, core_index, group_index, in_vmem(rows), other_rows, weights)
    received = move(sent, "head", [(i, cores - 1 - i) for i in range(cores)])
    shares = split_rows(shard_index, in_vmem(kept), received, heads)
    parts = [in_vmem(shares[0])] + [swap(shares[k], k) for k in range(1, heads)]
    summed = add_shares(parts)
    pairs = []
    for i in range(size):
        for h in range(cores):
            pairs.append((i * cores + h, (heads * h + i % heads) * cores + i // heads))
    projected = in_hbm(lax.ppermute(summed, ("ctx", "head"), pairs))
    return (join_heads(shard_index, returned), projected)


def shifted_2(x, axis, by):
    size = lax.axis_size(axis)
    pairs = [(i, i + by) for i in range(size) if 0 <= i + by < size]
    return lax.ppermute(x, axis, pairs)


def broadcast(x, axis, root):
    mine = lax.axis_index(axis) == root
    return lax.psum(jnp.where(mine, x, jnp.zeros_like(x)), axis)


def attend(
    query_rows,
    key_slab,
    value_slab,
    key_pos,
    query_pos,
    slash_shift_list,
    tile_list,
    column_kind,
    group_width,
):
    scores = jnp.dot(query_rows, key_slab.T, preferred_element_type=jnp.float32) * key_slab.shape[
        -1
    ] ** (-0.5)
    distance = query_pos[:, None] - key_pos[None, :]
    key_tile = jnp.where(key_pos >= 0, key_pos // VTILE, -1)
    vertical = jnp.any(key_tile[:, None] == tile_list[None, :], axis=1)[None, :]
    in_band = (distance >= 0) & (distance < LOCAL_BAND_KEYS) & ~vertical
    first_slash = (
        (distance >= slash_shift_list[0]) & (distance < slash_shift_list[0] + SLASH_W) & ~vertical
    )
    second_slash = (
        (distance >= slash_shift_list[1]) & (distance < slash_shift_list[1] + SLASH_W) & ~vertical
    )
    earlier = in_band | first_slash
    kinds = column_kind[None, :]
    allowed = jnp.where(
        kinds == 0,
        in_band,
        jnp.where(
            kinds == 1,
            first_slash & ~in_band,
            jnp.where(kinds == 2, second_slash & ~earlier, distance >= 0),
        ),
    )
    allowed = jnp.tile(allowed & (key_pos >= 0)[None, :], (group_width, 1))
    masked = jnp.where(allowed, scores, -jnp.inf)
    row_max = jnp.max(masked, axis=1, keepdims=True)
    weights = jnp.where(allowed, jnp.exp(masked - row_max), 0.0)
    row_sum = jnp.sum(weights, axis=1, keepdims=True)
    blended = jnp.dot(weights.astype(jnp.bfloat16), value_slab, preferred_element_type=jnp.float32)
    return (blended / row_sum).astype(jnp.bfloat16)


def heads_first(stacked, local_heads, head_dim):
    reordered = jnp.moveaxis(stacked, -2, 0)
    return reordered.reshape(local_heads, -1, head_dim)


def move_near(row_block, is_live, offset, target_slot, keep_rows, sender):
    slot_grid = jnp.arange(keep_rows, dtype=jnp.int32)[:, None]
    gathered = jnp.zeros((keep_rows, row_block.shape[1]), jnp.float32)
    for travel in range(-3, 4):
        chooser = (
            (slot_grid == target_slot[None, :]) & (offset[None, :] == travel) & is_live[None, :]
        ).astype(jnp.bfloat16)
        parcel = jnp.dot(chooser, row_block, preferred_element_type=jnp.float32).astype(
            jnp.bfloat16
        )
        if travel != 0:
            parcel = sender(parcel, travel)
        gathered = gathered + parcel.astype(jnp.float32)
    return gathered.astype(jnp.bfloat16)


def local(
    query_tensor,
    key_tensor,
    value_tensor,
    slash_offsets,
    vertical_tiles,
    kept_rows,
    kept_count,
    out_weight,
):
    shard_length = query_tensor.shape[0]
    head_dim = HEAD_SIZE
    local_heads = key_tensor.shape[1] // head_dim
    group_width = query_tensor.shape[1] // key_tensor.shape[1]
    shard_index = lax.axis_index("ctx")
    first_pos = shard_index * shard_length
    key_heads = key_tensor.reshape(shard_length, local_heads, head_dim)
    value_heads = value_tensor.reshape(shard_length, local_heads, head_dim)
    slash_spans = slash_offsets // shard_length
    own_pair = jnp.stack([key_heads, value_heads])
    moving = jnp.concatenate([own_pair, own_pair], 0)
    member_spans = jnp.stack(
        [slash_spans[:, 0], slash_spans[:, 0], slash_spans[:, 1], slash_spans[:, 1]]
    )
    for bit_number in range((SLASH_SPAN - 1).bit_length()):
        shifted = shifted_2(moving, "ctx", 1 << bit_number)
        head_flags = (member_spans >> bit_number & 1 == 1)[:, None, :, None]
        moving = jnp.where(head_flags, shifted, moving)
    nearby = jnp.concatenate([moving, own_pair], 0)
    distances = [nearby]
    for _ in range(2):
        nearby = shifted_2(nearby, "ctx", 1)
        distances.append(nearby)
    ordered = jnp.stack([distances[2], distances[1], distances[0]])
    band_pieces = ordered[:, 4:6]
    slash_pieces = jnp.stack([ordered[:, 0:2], ordered[:, 2:4]])
    tile_keys = []
    tile_values = []
    for head_number in range(local_heads):
        for tile_index in range(VTILES):
            fetched = broadcast(
                jnp.stack([key_heads[:, head_number], value_heads[:, head_number]]),
                "ctx",
                vertical_tiles[head_number, tile_index],
            )
            tile_keys.append(fetched[0])
            tile_values.append(fetched[1])
    all_keys = jnp.concatenate(
        [
            heads_first(band_pieces[:, 0], local_heads, head_dim),
            heads_first(slash_pieces[:, :, 0], local_heads, head_dim),
            jnp.stack(tile_keys).reshape(local_heads, VTILES * shard_length, head_dim),
        ],
        1,
    )
    all_values = jnp.concatenate(
        [
            heads_first(band_pieces[:, 1], local_heads, head_dim),
            heads_first(slash_pieces[:, :, 1], local_heads, head_dim),
            jnp.stack(tile_values).reshape(local_heads, VTILES * shard_length, head_dim),
        ],
        1,
    )
    window = jnp.arange(3 * shard_length, dtype=jnp.int32)
    band_pos = jnp.broadcast_to(
        first_pos - 2 * shard_length + window, (local_heads, 3 * shard_length)
    )
    slash_pos = first_pos - (slash_spans[:, :, None] + 2) * shard_length + window[None, None, :]
    tile_pos = (
        vertical_tiles[:, :, None] * shard_length
        + jnp.arange(shard_length, dtype=jnp.int32)[None, None, :]
    )
    key_pos = jnp.concatenate(
        [band_pos, slash_pos.reshape(local_heads, -1), tile_pos.reshape(local_heads, -1)], 1
    )
    column_kind = jnp.concatenate(
        [
            jnp.full((3 * shard_length,), 0, jnp.int32),
            jnp.full((3 * shard_length,), 1, jnp.int32),
            jnp.full((3 * shard_length,), 2, jnp.int32),
            jnp.full((VTILES * shard_length,), 3, jnp.int32),
        ]
    )
    query_pos = first_pos + jnp.arange(shard_length, dtype=jnp.int32)
    query_heads = (
        query_tensor.reshape(shard_length, local_heads, group_width, head_dim)
        .transpose(1, 2, 0, 3)
        .reshape(local_heads, group_width * shard_length, head_dim)
    )

    def attend_head(packed):
        return attend(
            packed[0],
            packed[1],
            packed[2],
            packed[3],
            query_pos,
            packed[4],
            packed[5],
            column_kind,
            group_width,
        )

    mixed_heads = lax.map(
        attend_head, (query_heads, all_keys, all_values, key_pos, slash_offsets, vertical_tiles)
    )
    attended = (
        mixed_heads.reshape(local_heads, group_width, shard_length, head_dim)
        .transpose(2, 0, 1, 3)
        .reshape(shard_length, -1)
    )
    keep_rows = shard_length // 8
    capacity = kept_rows.shape[1]
    starts = jnp.cumsum(kept_count) - kept_count
    slot_ids = jnp.arange(capacity, dtype=jnp.int32)
    is_live = slot_ids < kept_count[shard_index]
    placed_at = starts[shard_index] + slot_ids
    target_shard = placed_at // keep_rows
    target_slot = placed_at % keep_rows
    offset = target_shard - shard_index
    selected = jnp.take(attended, kept_rows[0], axis=0)
    rounded = lax.psum_scatter(
        lax.dot_general(
            selected,
            lax.all_gather(out_weight, "ctx", axis=0, tiled=True),
            (((1,), (1,)), ((), ())),
            preferred_element_type=jnp.float32,
        ),
        "head",
        scatter_dimension=1,
        tiled=True,
    ).astype(jnp.bfloat16)

    def send_output(parcel, travel):
        return shifted_2(parcel, "ctx", travel)

    projected = move_near(rounded, is_live, offset, target_slot, keep_rows, send_output)
    return (attended, projected)


def solution(mesh):
    placed = (
        P(("groups", "ctx"), "head"),
        P(("groups", "ctx"), "head"),
        P(("groups", "ctx"), "head"),
        P(("groups", "head"), None),
        P(("groups", "head"), None),
        P(("groups", "ctx"), None),
        P("groups"),
        P("ctx", "head"),
    )
    size, cores = mesh.shape["ctx"], mesh.shape["head"]

    def blocks_fit(args):
        heads = args[1].shape[1] // cores // HEAD_SIZE
        length = args[0].shape[0] // size // mesh.shape["groups"]
        power = size & (size - 1) == 0 and heads & (heads - 1) == 0
        whole_tiles = length == VTILE and args[5].shape[1] <= HEAD_SIZE
        pairs = cores == 2 and mesh.shape["groups"] == 2 and args[7].shape[0] // size % 256 == 0
        return power and whole_tiles and pairs and size == heads * cores

    def sharded(body):
        return jax.shard_map(
            body,
            mesh=mesh,
            in_specs=placed,
            out_specs=(P(("groups", "ctx"), "head"), P(("groups", "ctx"), "head")),
            check_vma=False,
        )

    def program(*args):
        if not blocks_fit(args):
            return sharded(local)(*args)
        return sharded(local_blocks)(*args)

    return program
```

```python
import math

import jax
import jax.numpy as jnp
from jax import lax
from jax.experimental import pallas as pl
from jax.experimental.pallas import tpu as pltpu
from jax.sharding import PartitionSpec as P


HEAD_SIZE = 128
SLASH_SPAN = 8
VTILES = 2
LOCAL_BAND_KEYS = 256
SLASH_W = 128
VTILE = 128
PAD_ROWS = 8
MASKED = -1e30


ANY = pl.BlockSpec(memory_space=pl.ANY)
SMEM = pl.BlockSpec(memory_space=pltpu.SMEM)
VMEM = pl.BlockSpec(memory_space=pltpu.VMEM)
GRANT = pltpu.CompilerParams(vmem_limit_bytes=16 << 20)


def xor_pairs(size, k):
    return [(i, i ^ k) for i in range(size)]


def in_vmem(x):
    return pltpu.with_memory_space_constraint(x, pltpu.VMEM)


def in_hbm(x):
    return pltpu.with_memory_space_constraint(x, pltpu.HBM)


def start_all(copies, sems):
    started = [
        pltpu.make_async_copy(source, target, sems.at[number])
        for number, (source, target) in enumerate(copies)
    ]
    for copy in started:
        copy.start()
    return started


def pack_heads(shard_index, query, key, value, kept_rows, heads):
    length = query.shape[0]
    hd = HEAD_SIZE
    group = query.shape[1] // heads // hd
    capacity = kept_rows.shape[1]
    total = (2 + group) * length

    def body(c_ref, q_ref, k_ref, v_ref, kept_ref, *rest):
        out, (kept_buf, sems) = rest[: 2 * heads], rest[2 * heads :]
        slot = c_ref[0] % heads
        copies = [(kept_ref, kept_buf)]
        for j in range(heads):
            head = slot ^ j
            k_from = k_ref.at[:, pl.ds(pl.multiple_of(head * hd, hd), hd)]
            v_from = v_ref.at[:, pl.ds(pl.multiple_of(head * hd, hd), hd)]
            blocks = [k_from, v_from]
            for g in range(group):
                at = pl.multiple_of((head * group + g) * hd, hd)
                blocks.append(q_ref.at[:, pl.ds(at, hd)])
            copies += [
                (block, out[j].at[pl.ds(i * length, length), :]) for i, block in enumerate(blocks)
            ]
            copies += [
                (k_from, out[heads + j].at[:, pl.ds(0, hd)]),
                (v_from, out[heads + j].at[:, pl.ds(hd, hd)]),
            ]
        started = start_all(copies, sems)
        for j in range(heads):
            out[j][total:, :] = jnp.zeros((PAD_ROWS, hd), jnp.bfloat16)
        started[0].wait()
        kept = kept_buf[...].astype(jnp.float32).astype(jnp.bfloat16)
        for j in range(heads):
            out[j][total : total + 1, 0:capacity] = kept
        for copy in started[1:]:
            copy.wait()

    return pl.pallas_call(
        body,
        out_shape=[pltpu.VMEM((total + PAD_ROWS, hd), jnp.bfloat16)] * heads
        + [pltpu.VMEM((length, 2 * hd), jnp.bfloat16)] * heads,
        in_specs=[SMEM] + [ANY] * 4,
        out_specs=[VMEM] * (2 * heads),
        scratch_shapes=[
            pltpu.VMEM((1, capacity), jnp.int32),
            pltpu.SemaphoreType.DMA((1 + (4 + group) * heads,)),
        ],
        compiler_params=GRANT,
        name="pack_heads",
    )(shard_index, in_hbm(query), in_hbm(key), in_hbm(value), in_hbm(kept_rows))


def pack_weight(shard_index, group_index, slash, tiles, counts, weight, length):
    heads = slash.shape[1]
    size = counts.shape[0]
    lanes = HEAD_SIZE
    width = weight.shape[1] // heads
    outs = weight.shape[0]
    sent = [outs] * (heads - 1) + [outs // 2]

    def body(c_ref, g_ref, slash_ref, tile_ref, count_ref, w_ref, *rest):
        out, (mask_ref, table_ref, tile_buf, sems) = rest[:heads], rest[heads:]
        c = c_ref[0]
        slot = c % heads
        first = c - slot
        copies = []
        for j in range(heads):
            at = pl.multiple_of((slot ^ j) * width, HEAD_SIZE)
            row = pl.multiple_of(g_ref[0] * sent[j], sent[j]) if sent[j] < outs else 0
            copies.append((w_ref.at[pl.ds(row, sent[j]), pl.ds(at, width)], out[j]))
        started = start_all(copies, sems)
        difference = lax.broadcasted_iota(jnp.int32, (length, length), 0) - lax.broadcasted_iota(
            jnp.int32, (length, length), 1
        )
        for d in range(size):
            distance = difference + d * length
            allowed = (distance >= 0) & (distance < LOCAL_BAND_KEYS)
            for i in range(slash_ref.shape[0]):
                offset = slash_ref[i, slot]
                allowed |= (distance >= offset) & (distance < offset + SLASH_W)
            tile_buf[d] = jnp.where(allowed, 0.0, MASKED)
        tile_buf[size] = jnp.where(difference >= 0, 0.0, MASKED)
        tile_buf[size + 1] = jnp.zeros((length, length), jnp.float32)
        tile_buf[size + 2] = jnp.full((length, length), MASKED, jnp.float32)
        before = jnp.int32(0)
        for s in range(heads):
            shards = [c ^ k for k in range(heads, size)] + [first + t for t in range(s + 1)]
            for number, k_shard in enumerate(shards):
                back = first + s - k_shard
                entry = back
                for i in range(tile_ref.shape[0]):
                    vertical = size + jnp.where(back == 0, 0, 1)
                    entry = jnp.where(tile_ref[i, slot] == k_shard, vertical, entry)
                entry = jnp.where(back < 0, size + 2, entry)
                mask_ref[s, :, number * length : (number + 1) * length] = tile_buf[entry]
            count = count_ref[first + s]
            table_ref[s, 0:1, :] = jnp.full((1, lanes), count, jnp.int32)
            table_ref[s, 1:2, :] = jnp.full((1, lanes), before, jnp.int32)
            before = before + count
        for copy in started:
            copy.wait()

    return pl.pallas_call(
        body,
        out_shape=[pltpu.VMEM((count, width), jnp.bfloat16) for count in sent]
        + [
            pltpu.VMEM((heads, length, size * length), jnp.float32),
            pltpu.VMEM((heads, 8, lanes), jnp.int32),
        ],
        in_specs=[SMEM] * 5 + [ANY],
        out_specs=[VMEM] * (heads + 2),
        scratch_shapes=[
            pltpu.VMEM((size + 3, length, length), jnp.float32),
            pltpu.SemaphoreType.DMA((heads,)),
        ],
        compiler_params=GRANT,
        name="pack_weight",
    )(shard_index, group_index, in_hbm(slash), in_hbm(tiles), in_hbm(counts), in_hbm(weight))


def attention(shard_index, masks, table, near, far, keep_rows):
    heads = len(near)
    length = far[0].shape[0]
    hd = HEAD_SIZE
    group = (near[0].shape[0] - PAD_ROWS) // length - 2
    width = group * hd
    far_keys = len(far) * length
    keys = far_keys + heads * length
    block_rows = heads * keep_rows
    factor = hd ** (-0.5) * math.log2(math.e)

    def body(c_ref, mask_ref, table_ref, *rest):
        near_refs, rest = rest[:heads], rest[heads:]
        far_refs, rest = rest[: len(far)], rest[len(far) :]
        out_refs, rows_ref = rest[:heads], rest[heads]
        q_all, k_all, v_all, kept_all, mixed_all = rest[heads + 1 :]
        slot = c_ref[0] % heads
        for k in range(len(far)):
            k_all[k * length : (k + 1) * length, :] = far_refs[k][:, 0:hd]
            v_all[k * length : (k + 1) * length, 0:hd] = far_refs[k][:, hd:]
        v_all[:, hd:] = jnp.ones((keys, hd), jnp.bfloat16)
        for k in range(heads):
            to = slot ^ k
            at = pl.ds(pl.multiple_of(far_keys + to * length, length), length)
            k_all[at, :] = near_refs[k][0:length, :]
            v_all[at, 0:hd] = near_refs[k][length : 2 * length, :]
            q_at = pl.multiple_of(to * group * length, length)
            q_all[pl.ds(q_at, group * length), :] = near_refs[k][
                2 * length : (2 + group) * length, :
            ]
            kept_at = pl.ds(pl.multiple_of(to * PAD_ROWS, PAD_ROWS), PAD_ROWS)
            kept_all[kept_at, :] = near_refs[k][(2 + group) * length :, :].astype(jnp.float32)
        rows = jnp.zeros((block_rows, width), jnp.float32)

        def scores_of(step):
            s, part = step
            rows_at = (s * group + part * 2) * length
            return lax.dot_general(
                q_all[rows_at : rows_at + 2 * length, :],
                k_all[0 : far_keys + (s + 1) * length, :],
                (((1,), (1,)), ((), ())),
                preferred_element_type=jnp.float32,
            )

        steps = [(s, part) for s in range(heads) for part in range(group // 2)]
        ready = [scores_of(step) for step in steps[:1]]
        for number, (s, part) in enumerate(steps):
            if number + 1 < len(steps):
                ready.append(scores_of(steps[number + 1]))
            seen = far_keys + (s + 1) * length
            scores = ready.pop(0).reshape(2, length, seen) * factor + mask_ref[s, :, 0:seen][None]
            scores = scores.reshape(2 * length, seen)
            weights = jnp.exp2(scores - jnp.max(scores, axis=1, keepdims=True))
            mixed = jnp.dot(
                weights.astype(jnp.bfloat16), v_all[0:seen, :], preferred_element_type=jnp.float32
            )
            mixed = (mixed[:, :hd] / mixed[:, hd:]).astype(jnp.bfloat16)
            for g in range(2):
                at = (part * 2 + g) * hd
                mixed_all[s * length : (s + 1) * length, at : at + hd] = mixed[
                    g * length : (g + 1) * length
                ]
        for s in range(heads):
            kept = kept_all[s * PAD_ROWS : s * PAD_ROWS + 1, :].astype(jnp.int32)
            token = lax.broadcasted_iota(jnp.int32, (length, hd), 0)
            is_token = (token == kept).astype(jnp.float32).astype(jnp.bfloat16)
            index = lax.broadcasted_iota(jnp.int32, (hd, block_rows), 0)
            place = lax.broadcasted_iota(jnp.int32, (hd, block_rows), 1)
            count, before = table_ref[s, 0:1, 0:block_rows], table_ref[s, 1:2, 0:block_rows]
            is_place = ((place - index == before) & (index < count)).astype(jnp.float32)
            chooser = jnp.dot(
                is_token, is_place.astype(jnp.bfloat16), preferred_element_type=jnp.float32
            ).astype(jnp.bfloat16)
            rows = rows + lax.dot_general(
                chooser,
                mixed_all[s * length : (s + 1) * length, :],
                (((0,), (0,)), ((), ())),
                preferred_element_type=jnp.float32,
            )
        rows_ref[...] = rows.astype(jnp.bfloat16)
        for k in range(heads):
            at = pl.multiple_of((slot ^ k) * length, length)
            out_refs[k][...] = mixed_all[pl.ds(at, length), :]

    return pl.pallas_call(
        body,
        out_shape=[pltpu.VMEM((length, width), jnp.bfloat16)] * heads
        + [pltpu.VMEM((block_rows, width), jnp.bfloat16)],
        in_specs=[SMEM] + [VMEM] * (2 + heads + len(far)),
        out_specs=[VMEM] * (heads + 1),
        scratch_shapes=[
            pltpu.VMEM((heads * group * length, hd), jnp.bfloat16),
            pltpu.VMEM((keys, hd), jnp.bfloat16),
            pltpu.VMEM((keys, 2 * hd), jnp.bfloat16),
            pltpu.VMEM((heads * PAD_ROWS, hd), jnp.float32),
            pltpu.VMEM((heads * length, width), jnp.bfloat16),
        ],
        compiler_params=GRANT,
        name="attention",
    )(shard_index, masks, table, *near, *far)


def project(shard_index, core_index, group_index, own_rows, other_rows, weights):
    heads = len(weights) - 1
    count = own_rows.shape[0]
    outs = weights[0].shape[0]

    def body(c_ref, h_ref, g_ref, own_ref, other_ref, *rest):
        w_refs, (keep_ref, send_ref) = rest[: heads + 1], rest[heads + 1 :]
        slot = c_ref[0] % heads
        keeps_own = c_ref[0] // heads == h_ref[0]
        own, other = own_ref[...], other_ref[...]
        both = jnp.concatenate(
            [jnp.where(keeps_own, own, other), jnp.where(keeps_own, other, own)], 0
        )
        half = outs // 2
        last = (slot ^ (heads - 1)) * outs
        starts = [(slot ^ j) * outs for j in range(heads - 1)]
        starts += [last + g_ref[0] * half, last + (1 - g_ref[0]) * half]
        for w_ref, start in zip(w_refs, starts):
            at = pl.ds(pl.multiple_of(start, HEAD_SIZE), w_ref.shape[0])
            share = lax.dot_general(
                both, w_ref[...], (((1,), (1,)), ((), ())), preferred_element_type=jnp.float32
            )
            keep_ref[:, at] = share[:count]
            send_ref[:, at] = share[count:].astype(jnp.bfloat16)

    return pl.pallas_call(
        body,
        out_shape=[
            pltpu.VMEM((count, heads * outs), jnp.float32),
            pltpu.VMEM((count, heads * outs), jnp.bfloat16),
        ],
        in_specs=[SMEM] * 3 + [VMEM] * (3 + heads),
        out_specs=[VMEM] * 2,
        compiler_params=GRANT,
        name="project",
    )(shard_index, core_index, group_index, own_rows, other_rows, *weights)


def split_rows(shard_index, kept, received, heads):
    keep_rows = kept.shape[0] // heads

    def body(c_ref, a_ref, b_ref, *out):
        slot = c_ref[0] % heads
        for j in range(heads):
            at = pl.multiple_of((slot ^ j) * keep_rows, 8)
            out[j][...] = (
                a_ref[pl.ds(at, keep_rows), :] + b_ref[pl.ds(at, keep_rows), :].astype(jnp.float32)
            ).astype(jnp.bfloat16)

    return pl.pallas_call(
        body,
        out_shape=[pltpu.VMEM((keep_rows, kept.shape[1]), jnp.bfloat16)] * heads,
        in_specs=[SMEM, VMEM, VMEM],
        out_specs=[VMEM] * heads,
        compiler_params=GRANT,
        name="split_rows",
    )(shard_index, kept, received)


def add_shares(shares):
    def body(*rest):
        total = rest[0][...].astype(jnp.float32)
        for share in rest[1:-1]:
            total = total + share[...].astype(jnp.float32)
        rest[-1][...] = total.astype(jnp.bfloat16)

    return pl.pallas_call(
        body,
        out_shape=pltpu.VMEM(shares[0].shape, jnp.bfloat16),
        in_specs=[VMEM] * len(shares),
        out_specs=VMEM,
        compiler_params=GRANT,
        name="add_shares",
    )(*shares)


def join_heads(shard_index, pieces):
    heads = len(pieces)
    length, width = pieces[0].shape

    def body(c_ref, *rest):
        ins, (out_ref, sems) = rest[:heads], rest[heads:]
        slot = c_ref[0] % heads
        copies = []
        for j in range(heads):
            at = pl.multiple_of((slot ^ j) * width, HEAD_SIZE)
            copies.append((ins[j], out_ref.at[:, pl.ds(at, width)]))
        for copy in start_all(copies, sems):
            copy.wait()

    return pl.pallas_call(
        body,
        out_shape=pltpu.HBM((length, heads * width), jnp.bfloat16),
        in_specs=[SMEM] + [VMEM] * heads,
        out_specs=ANY,
        scratch_shapes=[pltpu.SemaphoreType.DMA((heads,))],
        compiler_params=GRANT,
        name="join_heads",
    )(shard_index, *pieces)


def local_blocks(
    query_tensor,
    key_tensor,
    value_tensor,
    slash_offsets,
    vertical_tiles,
    kept_rows,
    kept_count,
    out_weight,
):
    size = lax.axis_size("ctx")
    cores = lax.axis_size("head")
    heads = key_tensor.shape[1] // HEAD_SIZE
    keep_rows = query_tensor.shape[0] // 8
    c = lax.axis_index("ctx").astype(jnp.int32)
    shard_index = c.reshape(1)
    group_index = lax.axis_index("groups").astype(jnp.int32).reshape(1)
    core_index = lax.axis_index("head").astype(jnp.int32).reshape(1)

    def move(x, axis, pairs):
        return in_vmem(lax.ppermute(x, axis, pairs))

    def swap(x, k):
        return move(x, "ctx", xor_pairs(size, k))

    packed = pack_heads(shard_index, query_tensor, key_tensor, value_tensor, kept_rows, heads)
    near = [in_vmem(packed[0])] + [swap(packed[k], k) for k in range(1, heads)]
    far = []
    for k in range(heads, size):
        pairs = [(i, i ^ k) for i in range(size) if i // heads < (i ^ k) // heads]
        far.append(move(packed[heads + k % heads], "ctx", pairs))
    *packed_weight, masks, table = pack_weight(
        shard_index,
        group_index,
        slash_offsets.T,
        vertical_tiles.T,
        kept_count,
        out_weight,
        query_tensor.shape[0],
    )
    weights = [in_vmem(packed_weight[0])]
    weights += [swap(packed_weight[k], k) for k in range(1, heads)]
    weights.append(move(weights[-1], "groups", [(0, 1), (1, 0)]))
    *mixed, rows = attention(shard_index, in_vmem(masks), in_vmem(table), near, far, keep_rows)
    other_rows = move(rows, "ctx", xor_pairs(size, heads))
    returned = [in_vmem(mixed[0])] + [swap(mixed[k], k) for k in range(1, heads)]
    kept, sent = project(shard_index, core_index, group_index, in_vmem(rows), other_rows, weights)
    received = move(sent, "head", [(i, cores - 1 - i) for i in range(cores)])
    shares = split_rows(shard_index, in_vmem(kept), received, heads)
    parts = [in_vmem(shares[0])] + [swap(shares[k], k) for k in range(1, heads)]
    summed = add_shares(parts)
    pairs = []
    for i in range(size):
        for h in range(cores):
            pairs.append((i * cores + h, (heads * h + i % heads) * cores + i // heads))
    projected = in_hbm(lax.ppermute(summed, ("ctx", "head"), pairs))
    return (join_heads(shard_index, returned), projected)


def shifted_2(x, axis, by):
    size = lax.axis_size(axis)
    pairs = [(i, i + by) for i in range(size) if 0 <= i + by < size]
    return lax.ppermute(x, axis, pairs)


def broadcast(x, axis, root):
    mine = lax.axis_index(axis) == root
    return lax.psum(jnp.where(mine, x, jnp.zeros_like(x)), axis)


def attend(
    query_rows,
    key_slab,
    value_slab,
    key_pos,
    query_pos,
    slash_shift_list,
    tile_list,
    column_kind,
    group_width,
):
    scores = jnp.dot(query_rows, key_slab.T, preferred_element_type=jnp.float32) * key_slab.shape[
        -1
    ] ** (-0.5)
    distance = query_pos[:, None] - key_pos[None, :]
    key_tile = jnp.where(key_pos >= 0, key_pos // VTILE, -1)
    vertical = jnp.any(key_tile[:, None] == tile_list[None, :], axis=1)[None, :]
    in_band = (distance >= 0) & (distance < LOCAL_BAND_KEYS) & ~vertical
    first_slash = (
        (distance >= slash_shift_list[0]) & (distance < slash_shift_list[0] + SLASH_W) & ~vertical
    )
    second_slash = (
        (distance >= slash_shift_list[1]) & (distance < slash_shift_list[1] + SLASH_W) & ~vertical
    )
    earlier = in_band | first_slash
    kinds = column_kind[None, :]
    allowed = jnp.where(
        kinds == 0,
        in_band,
        jnp.where(
            kinds == 1,
            first_slash & ~in_band,
            jnp.where(kinds == 2, second_slash & ~earlier, distance >= 0),
        ),
    )
    allowed = jnp.tile(allowed & (key_pos >= 0)[None, :], (group_width, 1))
    masked = jnp.where(allowed, scores, -jnp.inf)
    row_max = jnp.max(masked, axis=1, keepdims=True)
    weights = jnp.where(allowed, jnp.exp(masked - row_max), 0.0)
    row_sum = jnp.sum(weights, axis=1, keepdims=True)
    blended = jnp.dot(weights.astype(jnp.bfloat16), value_slab, preferred_element_type=jnp.float32)
    return (blended / row_sum).astype(jnp.bfloat16)


def heads_first(stacked, local_heads, head_dim):
    reordered = jnp.moveaxis(stacked, -2, 0)
    return reordered.reshape(local_heads, -1, head_dim)


def move_near(row_block, is_live, offset, target_slot, keep_rows, sender):
    slot_grid = jnp.arange(keep_rows, dtype=jnp.int32)[:, None]
    gathered = jnp.zeros((keep_rows, row_block.shape[1]), jnp.float32)
    for travel in range(-3, 4):
        chooser = (
            (slot_grid == target_slot[None, :]) & (offset[None, :] == travel) & is_live[None, :]
        ).astype(jnp.bfloat16)
        parcel = jnp.dot(chooser, row_block, preferred_element_type=jnp.float32).astype(
            jnp.bfloat16
        )
        if travel != 0:
            parcel = sender(parcel, travel)
        gathered = gathered + parcel.astype(jnp.float32)
    return gathered.astype(jnp.bfloat16)


def local(
    query_tensor,
    key_tensor,
    value_tensor,
    slash_offsets,
    vertical_tiles,
    kept_rows,
    kept_count,
    out_weight,
):
    shard_length = query_tensor.shape[0]
    head_dim = HEAD_SIZE
    local_heads = key_tensor.shape[1] // head_dim
    group_width = query_tensor.shape[1] // key_tensor.shape[1]
    shard_index = lax.axis_index("ctx")
    first_pos = shard_index * shard_length
    key_heads = key_tensor.reshape(shard_length, local_heads, head_dim)
    value_heads = value_tensor.reshape(shard_length, local_heads, head_dim)
    slash_spans = slash_offsets // shard_length
    own_pair = jnp.stack([key_heads, value_heads])
    moving = jnp.concatenate([own_pair, own_pair], 0)
    member_spans = jnp.stack(
        [slash_spans[:, 0], slash_spans[:, 0], slash_spans[:, 1], slash_spans[:, 1]]
    )
    for bit_number in range((SLASH_SPAN - 1).bit_length()):
        shifted = shifted_2(moving, "ctx", 1 << bit_number)
        head_flags = (member_spans >> bit_number & 1 == 1)[:, None, :, None]
        moving = jnp.where(head_flags, shifted, moving)
    nearby = jnp.concatenate([moving, own_pair], 0)
    distances = [nearby]
    for _ in range(2):
        nearby = shifted_2(nearby, "ctx", 1)
        distances.append(nearby)
    ordered = jnp.stack([distances[2], distances[1], distances[0]])
    band_pieces = ordered[:, 4:6]
    slash_pieces = jnp.stack([ordered[:, 0:2], ordered[:, 2:4]])
    tile_keys = []
    tile_values = []
    for head_number in range(local_heads):
        for tile_index in range(VTILES):
            fetched = broadcast(
                jnp.stack([key_heads[:, head_number], value_heads[:, head_number]]),
                "ctx",
                vertical_tiles[head_number, tile_index],
            )
            tile_keys.append(fetched[0])
            tile_values.append(fetched[1])
    all_keys = jnp.concatenate(
        [
            heads_first(band_pieces[:, 0], local_heads, head_dim),
            heads_first(slash_pieces[:, :, 0], local_heads, head_dim),
            jnp.stack(tile_keys).reshape(local_heads, VTILES * shard_length, head_dim),
        ],
        1,
    )
    all_values = jnp.concatenate(
        [
            heads_first(band_pieces[:, 1], local_heads, head_dim),
            heads_first(slash_pieces[:, :, 1], local_heads, head_dim),
            jnp.stack(tile_values).reshape(local_heads, VTILES * shard_length, head_dim),
        ],
        1,
    )
    window = jnp.arange(3 * shard_length, dtype=jnp.int32)
    band_pos = jnp.broadcast_to(
        first_pos - 2 * shard_length + window, (local_heads, 3 * shard_length)
    )
    slash_pos = first_pos - (slash_spans[:, :, None] + 2) * shard_length + window[None, None, :]
    tile_pos = (
        vertical_tiles[:, :, None] * shard_length
        + jnp.arange(shard_length, dtype=jnp.int32)[None, None, :]
    )
    key_pos = jnp.concatenate(
        [band_pos, slash_pos.reshape(local_heads, -1), tile_pos.reshape(local_heads, -1)], 1
    )
    column_kind = jnp.concatenate(
        [
            jnp.full((3 * shard_length,), 0, jnp.int32),
            jnp.full((3 * shard_length,), 1, jnp.int32),
            jnp.full((3 * shard_length,), 2, jnp.int32),
            jnp.full((VTILES * shard_length,), 3, jnp.int32),
        ]
    )
    query_pos = first_pos + jnp.arange(shard_length, dtype=jnp.int32)
    query_heads = (
        query_tensor.reshape(shard_length, local_heads, group_width, head_dim)
        .transpose(1, 2, 0, 3)
        .reshape(local_heads, group_width * shard_length, head_dim)
    )

    def attend_head(packed):
        return attend(
            packed[0],
            packed[1],
            packed[2],
            packed[3],
            query_pos,
            packed[4],
            packed[5],
            column_kind,
            group_width,
        )

    mixed_heads = lax.map(
        attend_head, (query_heads, all_keys, all_values, key_pos, slash_offsets, vertical_tiles)
    )
    attended = (
        mixed_heads.reshape(local_heads, group_width, shard_length, head_dim)
        .transpose(2, 0, 1, 3)
        .reshape(shard_length, -1)
    )
    keep_rows = shard_length // 8
    capacity = kept_rows.shape[1]
    starts = jnp.cumsum(kept_count) - kept_count
    slot_ids = jnp.arange(capacity, dtype=jnp.int32)
    is_live = slot_ids < kept_count[shard_index]
    placed_at = starts[shard_index] + slot_ids
    target_shard = placed_at // keep_rows
    target_slot = placed_at % keep_rows
    offset = target_shard - shard_index
    selected = jnp.take(attended, kept_rows[0], axis=0)
    rounded = lax.psum_scatter(
        lax.dot_general(
            selected,
            lax.all_gather(out_weight, "ctx", axis=0, tiled=True),
            (((1,), (1,)), ((), ())),
            preferred_element_type=jnp.float32,
        ),
        "head",
        scatter_dimension=1,
        tiled=True,
    ).astype(jnp.bfloat16)

    def send_output(parcel, travel):
        return shifted_2(parcel, "ctx", travel)

    projected = move_near(rounded, is_live, offset, target_slot, keep_rows, send_output)
    return (attended, projected)


def solution(mesh):
    placed = (
        P(("groups", "ctx"), "head"),
        P(("groups", "ctx"), "head"),
        P(("groups", "ctx"), "head"),
        P(("groups", "head"), None),
        P(("groups", "head"), None),
        P(("groups", "ctx"), None),
        P("groups"),
        P("ctx", "head"),
    )
    size, cores = mesh.shape["ctx"], mesh.shape["head"]

    def blocks_fit(args):
        heads = args[1].shape[1] // cores // HEAD_SIZE
        length = args[0].shape[0] // size // mesh.shape["groups"]
        power = size & (size - 1) == 0 and heads & (heads - 1) == 0
        whole_tiles = length == VTILE and args[5].shape[1] <= HEAD_SIZE
        pairs = cores == 2 and mesh.shape["groups"] == 2 and args[7].shape[0] // size % 256 == 0
        return power and whole_tiles and pairs and size == heads * cores

    def sharded(body):
        return jax.shard_map(
            body,
            mesh=mesh,
            in_specs=placed,
            out_specs=(P(("groups", "ctx"), "head"), P(("groups", "ctx"), "head")),
            check_vma=False,
        )

    def program(*args):
        if not blocks_fit(args):
            return sharded(local)(*args)
        return sharded(local_blocks)(*args)

    return program
```

```python
import math

import jax
import jax.numpy as jnp
from jax import lax
from jax.experimental import pallas as pl
from jax.experimental.pallas import tpu as pltpu
from jax.sharding import PartitionSpec as P


HEAD_SIZE = 128
SLASH_SPAN = 8
VTILES = 2
LOCAL_BAND_KEYS = 256
SLASH_W = 128
VTILE = 128
PAD_ROWS = 8
MASKED = -1e30


ANY = pl.BlockSpec(memory_space=pl.ANY)
SMEM = pl.BlockSpec(memory_space=pltpu.SMEM)
VMEM = pl.BlockSpec(memory_space=pltpu.VMEM)
GRANT = pltpu.CompilerParams(vmem_limit_bytes=16 << 20)


def xor_pairs(size, k):
    return [(i, i ^ k) for i in range(size)]


def in_vmem(x):
    return pltpu.with_memory_space_constraint(x, pltpu.VMEM)


def in_hbm(x):
    return pltpu.with_memory_space_constraint(x, pltpu.HBM)


def start_all(copies, sems):
    started = [
        pltpu.make_async_copy(source, target, sems.at[number])
        for number, (source, target) in enumerate(copies)
    ]
    for copy in started:
        copy.start()
    return started


def pack_heads(shard_index, query, key, value, kept_rows, heads):
    length = query.shape[0]
    hd = HEAD_SIZE
    group = query.shape[1] // heads // hd
    capacity = kept_rows.shape[1]
    total = (2 + group) * length

    def body(c_ref, q_ref, k_ref, v_ref, kept_ref, *rest):
        out, (kept_buf, sems) = rest[: 2 * heads], rest[2 * heads :]
        slot = c_ref[0] % heads
        copies = [(kept_ref, kept_buf)]
        for j in range(heads):
            head = slot ^ j
            k_from = k_ref.at[:, pl.ds(pl.multiple_of(head * hd, hd), hd)]
            v_from = v_ref.at[:, pl.ds(pl.multiple_of(head * hd, hd), hd)]
            blocks = [k_from, v_from]
            for g in range(group):
                at = pl.multiple_of((head * group + g) * hd, hd)
                blocks.append(q_ref.at[:, pl.ds(at, hd)])
            copies += [
                (block, out[j].at[pl.ds(i * length, length), :]) for i, block in enumerate(blocks)
            ]
            copies += [
                (k_from, out[heads + j].at[:, pl.ds(0, hd)]),
                (v_from, out[heads + j].at[:, pl.ds(hd, hd)]),
            ]
        started = start_all(copies, sems)
        for j in range(heads):
            out[j][total:, :] = jnp.zeros((PAD_ROWS, hd), jnp.bfloat16)
        started[0].wait()
        kept = kept_buf[...].astype(jnp.float32).astype(jnp.bfloat16)
        for j in range(heads):
            out[j][total : total + 1, 0:capacity] = kept
        for copy in started[1:]:
            copy.wait()

    return pl.pallas_call(
        body,
        out_shape=[pltpu.VMEM((total + PAD_ROWS, hd), jnp.bfloat16)] * heads
        + [pltpu.VMEM((length, 2 * hd), jnp.bfloat16)] * heads,
        in_specs=[SMEM] + [ANY] * 4,
        out_specs=[VMEM] * (2 * heads),
        scratch_shapes=[
            pltpu.VMEM((1, capacity), jnp.int32),
            pltpu.SemaphoreType.DMA((1 + (4 + group) * heads,)),
        ],
        compiler_params=GRANT,
        name="pack_heads",
    )(shard_index, in_hbm(query), in_hbm(key), in_hbm(value), in_hbm(kept_rows))


def pack_weight(shard_index, group_index, slash, tiles, counts, weight, length):
    heads = slash.shape[1]
    size = counts.shape[0]
    lanes = HEAD_SIZE
    width = weight.shape[1] // heads
    outs = weight.shape[0]
    sent = [outs] * (heads - 1) + [outs // 2]

    def body(c_ref, g_ref, slash_hbm, tile_hbm, count_hbm, w_ref, *rest):
        out, rest = rest[:heads], rest[heads:]
        mask_ref, table_ref, tile_buf, slash_ref, tile_ref, count_ref, sems = rest
        c = c_ref[0]
        slot = c % heads
        first = c - slot
        copies = []
        for j in range(heads):
            at = pl.multiple_of((slot ^ j) * width, HEAD_SIZE)
            row = pl.multiple_of(g_ref[0] * sent[j], sent[j]) if sent[j] < outs else 0
            copies.append((w_ref.at[pl.ds(row, sent[j]), pl.ds(at, width)], out[j]))
        tables = [(slash_hbm, slash_ref), (tile_hbm, tile_ref), (count_hbm, count_ref)]
        started = start_all(tables + copies, sems)
        difference = lax.broadcasted_iota(jnp.int32, (length, length), 0) - lax.broadcasted_iota(
            jnp.int32, (length, length), 1
        )
        for copy in started[: len(tables)]:
            copy.wait()
        for d in range(size):
            distance = difference + d * length
            allowed = (distance >= 0) & (distance < LOCAL_BAND_KEYS)
            for i in range(slash_ref.shape[0]):
                offset = slash_ref[i, slot]
                allowed |= (distance >= offset) & (distance < offset + SLASH_W)
            tile_buf[d] = jnp.where(allowed, 0.0, MASKED)
        tile_buf[size] = jnp.where(difference >= 0, 0.0, MASKED)
        tile_buf[size + 1] = jnp.zeros((length, length), jnp.float32)
        tile_buf[size + 2] = jnp.full((length, length), MASKED, jnp.float32)
        before = jnp.int32(0)
        for s in range(heads):
            shards = [c ^ k for k in range(heads, size)] + [first + t for t in range(s + 1)]
            for number, k_shard in enumerate(shards):
                back = first + s - k_shard
                entry = back
                for i in range(tile_ref.shape[0]):
                    vertical = size + jnp.where(back == 0, 0, 1)
                    entry = jnp.where(tile_ref[i, slot] == k_shard, vertical, entry)
                entry = jnp.where(back < 0, size + 2, entry)
                mask_ref[s, :, number * length : (number + 1) * length] = tile_buf[entry]
            count = count_ref[first + s]
            table_ref[s, 0:1, :] = jnp.full((1, lanes), count, jnp.int32)
            table_ref[s, 1:2, :] = jnp.full((1, lanes), before, jnp.int32)
            before = before + count
        for copy in started[len(tables) :]:
            copy.wait()

    return pl.pallas_call(
        body,
        out_shape=[pltpu.VMEM((count, width), jnp.bfloat16) for count in sent]
        + [
            pltpu.VMEM((heads, length, size * length), jnp.float32),
            pltpu.VMEM((heads, 8, lanes), jnp.int32),
        ],
        in_specs=[SMEM] * 2 + [ANY] * 4,
        out_specs=[VMEM] * (heads + 2),
        scratch_shapes=[
            pltpu.VMEM((size + 3, length, length), jnp.float32),
            pltpu.SMEM(slash.shape, jnp.int32),
            pltpu.SMEM(tiles.shape, jnp.int32),
            pltpu.SMEM(counts.shape, jnp.int32),
            pltpu.SemaphoreType.DMA((heads + 3,)),
        ],
        compiler_params=GRANT,
        name="pack_weight",
    )(shard_index, group_index, in_hbm(slash), in_hbm(tiles), in_hbm(counts), in_hbm(weight))


def attention(shard_index, masks, table, near, far, keep_rows):
    heads = len(near)
    length = far[0].shape[0]
    hd = HEAD_SIZE
    group = (near[0].shape[0] - PAD_ROWS) // length - 2
    width = group * hd
    far_keys = len(far) * length
    keys = far_keys + heads * length
    block_rows = heads * keep_rows
    factor = hd ** (-0.5) * math.log2(math.e)

    def body(c_ref, mask_ref, table_ref, *rest):
        near_refs, rest = rest[:heads], rest[heads:]
        far_refs, rest = rest[: len(far)], rest[len(far) :]
        out_refs, rows_ref = rest[:heads], rest[heads]
        q_all, k_all, v_all, kept_all, mixed_all = rest[heads + 1 :]
        slot = c_ref[0] % heads
        for k in range(len(far)):
            k_all[k * length : (k + 1) * length, :] = far_refs[k][:, 0:hd]
            v_all[k * length : (k + 1) * length, 0:hd] = far_refs[k][:, hd:]
        v_all[:, hd:] = jnp.ones((keys, hd), jnp.bfloat16)
        for k in range(heads):
            to = slot ^ k
            at = pl.ds(pl.multiple_of(far_keys + to * length, length), length)
            k_all[at, :] = near_refs[k][0:length, :]
            v_all[at, 0:hd] = near_refs[k][length : 2 * length, :]
            q_at = pl.multiple_of(to * group * length, length)
            q_all[pl.ds(q_at, group * length), :] = near_refs[k][
                2 * length : (2 + group) * length, :
            ]
            kept_at = pl.ds(pl.multiple_of(to * PAD_ROWS, PAD_ROWS), PAD_ROWS)
            kept_all[kept_at, :] = near_refs[k][(2 + group) * length :, :].astype(jnp.float32)
        rows = jnp.zeros((block_rows, width), jnp.float32)

        def scores_of(step):
            s, part = step
            rows_at = (s * group + part * 2) * length
            return lax.dot_general(
                q_all[rows_at : rows_at + 2 * length, :],
                k_all[0 : far_keys + (s + 1) * length, :],
                (((1,), (1,)), ((), ())),
                preferred_element_type=jnp.float32,
            )

        steps = [(s, part) for s in range(heads) for part in range(group // 2)]
        ready = [scores_of(step) for step in steps[:1]]
        for number, (s, part) in enumerate(steps):
            if number + 1 < len(steps):
                ready.append(scores_of(steps[number + 1]))
            seen = far_keys + (s + 1) * length
            scores = ready.pop(0).reshape(2, length, seen) * factor + mask_ref[s, :, 0:seen][None]
            scores = scores.reshape(2 * length, seen)
            weights = jnp.exp2(scores - jnp.max(scores, axis=1, keepdims=True))
            mixed = jnp.dot(
                weights.astype(jnp.bfloat16), v_all[0:seen, :], preferred_element_type=jnp.float32
            )
            mixed = (mixed[:, :hd] / mixed[:, hd:]).astype(jnp.bfloat16)
            for g in range(2):
                at = (part * 2 + g) * hd
                mixed_all[s * length : (s + 1) * length, at : at + hd] = mixed[
                    g * length : (g + 1) * length
                ]
        for s in range(heads):
            kept = kept_all[s * PAD_ROWS : s * PAD_ROWS + 1, :].astype(jnp.int32)
            token = lax.broadcasted_iota(jnp.int32, (length, hd), 0)
            is_token = (token == kept).astype(jnp.float32).astype(jnp.bfloat16)
            index = lax.broadcasted_iota(jnp.int32, (hd, block_rows), 0)
            place = lax.broadcasted_iota(jnp.int32, (hd, block_rows), 1)
            count, before = table_ref[s, 0:1, 0:block_rows], table_ref[s, 1:2, 0:block_rows]
            is_place = ((place - index == before) & (index < count)).astype(jnp.float32)
            chooser = jnp.dot(
                is_token, is_place.astype(jnp.bfloat16), preferred_element_type=jnp.float32
            ).astype(jnp.bfloat16)
            rows = rows + lax.dot_general(
                chooser,
                mixed_all[s * length : (s + 1) * length, :],
                (((0,), (0,)), ((), ())),
                preferred_element_type=jnp.float32,
            )
        rows_ref[...] = rows.astype(jnp.bfloat16)
        for k in range(heads):
            at = pl.multiple_of((slot ^ k) * length, length)
            out_refs[k][...] = mixed_all[pl.ds(at, length), :]

    return pl.pallas_call(
        body,
        out_shape=[pltpu.VMEM((length, width), jnp.bfloat16)] * heads
        + [pltpu.VMEM((block_rows, width), jnp.bfloat16)],
        in_specs=[SMEM] + [VMEM] * (2 + heads + len(far)),
        out_specs=[VMEM] * (heads + 1),
        scratch_shapes=[
            pltpu.VMEM((heads * group * length, hd), jnp.bfloat16),
            pltpu.VMEM((keys, hd), jnp.bfloat16),
            pltpu.VMEM((keys, 2 * hd), jnp.bfloat16),
            pltpu.VMEM((heads * PAD_ROWS, hd), jnp.float32),
            pltpu.VMEM((heads * length, width), jnp.bfloat16),
        ],
        compiler_params=GRANT,
        name="attention",
    )(shard_index, masks, table, *near, *far)


def project(shard_index, core_index, group_index, own_rows, other_rows, weights):
    heads = len(weights) - 1
    count = own_rows.shape[0]
    outs = weights[0].shape[0]

    def body(c_ref, h_ref, g_ref, own_ref, other_ref, *rest):
        w_refs, (keep_ref, send_ref) = rest[: heads + 1], rest[heads + 1 :]
        slot = c_ref[0] % heads
        keeps_own = c_ref[0] // heads == h_ref[0]
        own, other = own_ref[...], other_ref[...]
        both = jnp.concatenate(
            [jnp.where(keeps_own, own, other), jnp.where(keeps_own, other, own)], 0
        )
        half = outs // 2
        last = (slot ^ (heads - 1)) * outs
        starts = [(slot ^ j) * outs for j in range(heads - 1)]
        starts += [last + g_ref[0] * half, last + (1 - g_ref[0]) * half]
        for w_ref, start in zip(w_refs, starts):
            at = pl.ds(pl.multiple_of(start, HEAD_SIZE), w_ref.shape[0])
            share = lax.dot_general(
                both, w_ref[...], (((1,), (1,)), ((), ())), preferred_element_type=jnp.float32
            )
            keep_ref[:, at] = share[:count]
            send_ref[:, at] = share[count:].astype(jnp.bfloat16)

    return pl.pallas_call(
        body,
        out_shape=[
            pltpu.VMEM((count, heads * outs), jnp.float32),
            pltpu.VMEM((count, heads * outs), jnp.bfloat16),
        ],
        in_specs=[SMEM] * 3 + [VMEM] * (3 + heads),
        out_specs=[VMEM] * 2,
        compiler_params=GRANT,
        name="project",
    )(shard_index, core_index, group_index, own_rows, other_rows, *weights)


def split_rows(shard_index, kept, received, heads):
    keep_rows = kept.shape[0] // heads

    def body(c_ref, a_ref, b_ref, *out):
        slot = c_ref[0] % heads
        for j in range(heads):
            at = pl.multiple_of((slot ^ j) * keep_rows, 8)
            out[j][...] = (
                a_ref[pl.ds(at, keep_rows), :] + b_ref[pl.ds(at, keep_rows), :].astype(jnp.float32)
            ).astype(jnp.bfloat16)

    return pl.pallas_call(
        body,
        out_shape=[pltpu.VMEM((keep_rows, kept.shape[1]), jnp.bfloat16)] * heads,
        in_specs=[SMEM, VMEM, VMEM],
        out_specs=[VMEM] * heads,
        compiler_params=GRANT,
        name="split_rows",
    )(shard_index, kept, received)


def add_shares(shares):
    def body(*rest):
        total = rest[0][...].astype(jnp.float32)
        for share in rest[1:-1]:
            total = total + share[...].astype(jnp.float32)
        rest[-1][...] = total.astype(jnp.bfloat16)

    return pl.pallas_call(
        body,
        out_shape=pltpu.VMEM(shares[0].shape, jnp.bfloat16),
        in_specs=[VMEM] * len(shares),
        out_specs=VMEM,
        compiler_params=GRANT,
        name="add_shares",
    )(*shares)


def join_heads(shard_index, pieces):
    heads = len(pieces)
    length, width = pieces[0].shape

    def body(c_ref, *rest):
        ins, (out_ref, sems) = rest[:heads], rest[heads:]
        slot = c_ref[0] % heads
        copies = []
        for j in range(heads):
            at = pl.multiple_of((slot ^ j) * width, HEAD_SIZE)
            copies.append((ins[j], out_ref.at[:, pl.ds(at, width)]))
        for copy in start_all(copies, sems):
            copy.wait()

    return pl.pallas_call(
        body,
        out_shape=pltpu.HBM((length, heads * width), jnp.bfloat16),
        in_specs=[SMEM] + [VMEM] * heads,
        out_specs=ANY,
        scratch_shapes=[pltpu.SemaphoreType.DMA((heads,))],
        compiler_params=GRANT,
        name="join_heads",
    )(shard_index, *pieces)


def local_blocks(
    query_tensor,
    key_tensor,
    value_tensor,
    slash_offsets,
    vertical_tiles,
    kept_rows,
    kept_count,
    out_weight,
):
    size = lax.axis_size("ctx")
    cores = lax.axis_size("head")
    heads = key_tensor.shape[1] // HEAD_SIZE
    keep_rows = query_tensor.shape[0] // 8
    c = lax.axis_index("ctx").astype(jnp.int32)
    shard_index = c.reshape(1)
    group_index = lax.axis_index("groups").astype(jnp.int32).reshape(1)
    core_index = lax.axis_index("head").astype(jnp.int32).reshape(1)

    def move(x, axis, pairs):
        return in_vmem(lax.ppermute(x, axis, pairs))

    def swap(x, k):
        return move(x, "ctx", xor_pairs(size, k))

    packed = pack_heads(shard_index, query_tensor, key_tensor, value_tensor, kept_rows, heads)
    near = [in_vmem(packed[0])] + [swap(packed[k], k) for k in range(1, heads)]
    far = []
    for k in range(heads, size):
        pairs = [(i, i ^ k) for i in range(size) if i // heads < (i ^ k) // heads]
        far.append(move(packed[heads + k % heads], "ctx", pairs))
    *packed_weight, masks, table = pack_weight(
        shard_index,
        group_index,
        slash_offsets.T,
        vertical_tiles.T,
        kept_count,
        out_weight,
        query_tensor.shape[0],
    )
    weights = [in_vmem(packed_weight[0])]
    weights += [swap(packed_weight[k], k) for k in range(1, heads)]
    weights.append(move(weights[-1], "groups", [(0, 1), (1, 0)]))
    *mixed, rows = attention(shard_index, in_vmem(masks), in_vmem(table), near, far, keep_rows)
    other_rows = move(rows, "ctx", xor_pairs(size, heads))
    returned = [in_vmem(mixed[0])] + [swap(mixed[k], k) for k in range(1, heads)]
    kept, sent = project(shard_index, core_index, group_index, in_vmem(rows), other_rows, weights)
    received = move(sent, "head", [(i, cores - 1 - i) for i in range(cores)])
    shares = split_rows(shard_index, in_vmem(kept), received, heads)
    parts = [in_vmem(shares[0])] + [swap(shares[k], k) for k in range(1, heads)]
    summed = add_shares(parts)
    pairs = []
    for i in range(size):
        for h in range(cores):
            pairs.append((i * cores + h, (heads * h + i % heads) * cores + i // heads))
    projected = in_hbm(lax.ppermute(summed, ("ctx", "head"), pairs))
    return (join_heads(shard_index, returned), projected)


def shifted_2(x, axis, by):
    size = lax.axis_size(axis)
    pairs = [(i, i + by) for i in range(size) if 0 <= i + by < size]
    return lax.ppermute(x, axis, pairs)


def broadcast(x, axis, root):
    mine = lax.axis_index(axis) == root
    return lax.psum(jnp.where(mine, x, jnp.zeros_like(x)), axis)


def attend(
    query_rows,
    key_slab,
    value_slab,
    key_pos,
    query_pos,
    slash_shift_list,
    tile_list,
    column_kind,
    group_width,
):
    scores = jnp.dot(query_rows, key_slab.T, preferred_element_type=jnp.float32) * key_slab.shape[
        -1
    ] ** (-0.5)
    distance = query_pos[:, None] - key_pos[None, :]
    key_tile = jnp.where(key_pos >= 0, key_pos // VTILE, -1)
    vertical = jnp.any(key_tile[:, None] == tile_list[None, :], axis=1)[None, :]
    in_band = (distance >= 0) & (distance < LOCAL_BAND_KEYS) & ~vertical
    first_slash = (
        (distance >= slash_shift_list[0]) & (distance < slash_shift_list[0] + SLASH_W) & ~vertical
    )
    second_slash = (
        (distance >= slash_shift_list[1]) & (distance < slash_shift_list[1] + SLASH_W) & ~vertical
    )
    earlier = in_band | first_slash
    kinds = column_kind[None, :]
    allowed = jnp.where(
        kinds == 0,
        in_band,
        jnp.where(
            kinds == 1,
            first_slash & ~in_band,
            jnp.where(kinds == 2, second_slash & ~earlier, distance >= 0),
        ),
    )
    allowed = jnp.tile(allowed & (key_pos >= 0)[None, :], (group_width, 1))
    masked = jnp.where(allowed, scores, -jnp.inf)
    row_max = jnp.max(masked, axis=1, keepdims=True)
    weights = jnp.where(allowed, jnp.exp(masked - row_max), 0.0)
    row_sum = jnp.sum(weights, axis=1, keepdims=True)
    blended = jnp.dot(weights.astype(jnp.bfloat16), value_slab, preferred_element_type=jnp.float32)
    return (blended / row_sum).astype(jnp.bfloat16)


def heads_first(stacked, local_heads, head_dim):
    reordered = jnp.moveaxis(stacked, -2, 0)
    return reordered.reshape(local_heads, -1, head_dim)


def move_near(row_block, is_live, offset, target_slot, keep_rows, sender):
    slot_grid = jnp.arange(keep_rows, dtype=jnp.int32)[:, None]
    gathered = jnp.zeros((keep_rows, row_block.shape[1]), jnp.float32)
    for travel in range(-3, 4):
        chooser = (
            (slot_grid == target_slot[None, :]) & (offset[None, :] == travel) & is_live[None, :]
        ).astype(jnp.bfloat16)
        parcel = jnp.dot(chooser, row_block, preferred_element_type=jnp.float32).astype(
            jnp.bfloat16
        )
        if travel != 0:
            parcel = sender(parcel, travel)
        gathered = gathered + parcel.astype(jnp.float32)
    return gathered.astype(jnp.bfloat16)


def local(
    query_tensor,
    key_tensor,
    value_tensor,
    slash_offsets,
    vertical_tiles,
    kept_rows,
    kept_count,
    out_weight,
):
    shard_length = query_tensor.shape[0]
    head_dim = HEAD_SIZE
    local_heads = key_tensor.shape[1] // head_dim
    group_width = query_tensor.shape[1] // key_tensor.shape[1]
    shard_index = lax.axis_index("ctx")
    first_pos = shard_index * shard_length
    key_heads = key_tensor.reshape(shard_length, local_heads, head_dim)
    value_heads = value_tensor.reshape(shard_length, local_heads, head_dim)
    slash_spans = slash_offsets // shard_length
    own_pair = jnp.stack([key_heads, value_heads])
    moving = jnp.concatenate([own_pair, own_pair], 0)
    member_spans = jnp.stack(
        [slash_spans[:, 0], slash_spans[:, 0], slash_spans[:, 1], slash_spans[:, 1]]
    )
    for bit_number in range((SLASH_SPAN - 1).bit_length()):
        shifted = shifted_2(moving, "ctx", 1 << bit_number)
        head_flags = (member_spans >> bit_number & 1 == 1)[:, None, :, None]
        moving = jnp.where(head_flags, shifted, moving)
    nearby = jnp.concatenate([moving, own_pair], 0)
    distances = [nearby]
    for _ in range(2):
        nearby = shifted_2(nearby, "ctx", 1)
        distances.append(nearby)
    ordered = jnp.stack([distances[2], distances[1], distances[0]])
    band_pieces = ordered[:, 4:6]
    slash_pieces = jnp.stack([ordered[:, 0:2], ordered[:, 2:4]])
    tile_keys = []
    tile_values = []
    for head_number in range(local_heads):
        for tile_index in range(VTILES):
            fetched = broadcast(
                jnp.stack([key_heads[:, head_number], value_heads[:, head_number]]),
                "ctx",
                vertical_tiles[head_number, tile_index],
            )
            tile_keys.append(fetched[0])
            tile_values.append(fetched[1])
    all_keys = jnp.concatenate(
        [
            heads_first(band_pieces[:, 0], local_heads, head_dim),
            heads_first(slash_pieces[:, :, 0], local_heads, head_dim),
            jnp.stack(tile_keys).reshape(local_heads, VTILES * shard_length, head_dim),
        ],
        1,
    )
    all_values = jnp.concatenate(
        [
            heads_first(band_pieces[:, 1], local_heads, head_dim),
            heads_first(slash_pieces[:, :, 1], local_heads, head_dim),
            jnp.stack(tile_values).reshape(local_heads, VTILES * shard_length, head_dim),
        ],
        1,
    )
    window = jnp.arange(3 * shard_length, dtype=jnp.int32)
    band_pos = jnp.broadcast_to(
        first_pos - 2 * shard_length + window, (local_heads, 3 * shard_length)
    )
    slash_pos = first_pos - (slash_spans[:, :, None] + 2) * shard_length + window[None, None, :]
    tile_pos = (
        vertical_tiles[:, :, None] * shard_length
        + jnp.arange(shard_length, dtype=jnp.int32)[None, None, :]
    )
    key_pos = jnp.concatenate(
        [band_pos, slash_pos.reshape(local_heads, -1), tile_pos.reshape(local_heads, -1)], 1
    )
    column_kind = jnp.concatenate(
        [
            jnp.full((3 * shard_length,), 0, jnp.int32),
            jnp.full((3 * shard_length,), 1, jnp.int32),
            jnp.full((3 * shard_length,), 2, jnp.int32),
            jnp.full((VTILES * shard_length,), 3, jnp.int32),
        ]
    )
    query_pos = first_pos + jnp.arange(shard_length, dtype=jnp.int32)
    query_heads = (
        query_tensor.reshape(shard_length, local_heads, group_width, head_dim)
        .transpose(1, 2, 0, 3)
        .reshape(local_heads, group_width * shard_length, head_dim)
    )

    def attend_head(packed):
        return attend(
            packed[0],
            packed[1],
            packed[2],
            packed[3],
            query_pos,
            packed[4],
            packed[5],
            column_kind,
            group_width,
        )

    mixed_heads = lax.map(
        attend_head, (query_heads, all_keys, all_values, key_pos, slash_offsets, vertical_tiles)
    )
    attended = (
        mixed_heads.reshape(local_heads, group_width, shard_length, head_dim)
        .transpose(2, 0, 1, 3)
        .reshape(shard_length, -1)
    )
    keep_rows = shard_length // 8
    capacity = kept_rows.shape[1]
    starts = jnp.cumsum(kept_count) - kept_count
    slot_ids = jnp.arange(capacity, dtype=jnp.int32)
    is_live = slot_ids < kept_count[shard_index]
    placed_at = starts[shard_index] + slot_ids
    target_shard = placed_at // keep_rows
    target_slot = placed_at % keep_rows
    offset = target_shard - shard_index
    selected = jnp.take(attended, kept_rows[0], axis=0)
    rounded = lax.psum_scatter(
        lax.dot_general(
            selected,
            lax.all_gather(out_weight, "ctx", axis=0, tiled=True),
            (((1,), (1,)), ((), ())),
            preferred_element_type=jnp.float32,
        ),
        "head",
        scatter_dimension=1,
        tiled=True,
    ).astype(jnp.bfloat16)

    def send_output(parcel, travel):
        return shifted_2(parcel, "ctx", travel)

    projected = move_near(rounded, is_live, offset, target_slot, keep_rows, send_output)
    return (attended, projected)


def solution(mesh):
    placed = (
        P(("groups", "ctx"), "head"),
        P(("groups", "ctx"), "head"),
        P(("groups", "ctx"), "head"),
        P(("groups", "head"), None),
        P(("groups", "head"), None),
        P(("groups", "ctx"), None),
        P("groups"),
        P("ctx", "head"),
    )
    size, cores = mesh.shape["ctx"], mesh.shape["head"]

    def blocks_fit(args):
        heads = args[1].shape[1] // cores // HEAD_SIZE
        length = args[0].shape[0] // size // mesh.shape["groups"]
        power = size & (size - 1) == 0 and heads & (heads - 1) == 0
        whole_tiles = length == VTILE and args[5].shape[1] <= HEAD_SIZE
        pairs = cores == 2 and mesh.shape["groups"] == 2 and args[7].shape[0] // size % 256 == 0
        return power and whole_tiles and pairs and size == heads * cores

    def sharded(body):
        return jax.shard_map(
            body,
            mesh=mesh,
            in_specs=placed,
            out_specs=(P(("groups", "ctx"), "head"), P(("groups", "ctx"), "head")),
            check_vma=False,
        )

    def program(*args):
        if not blocks_fit(args):
            return sharded(local)(*args)
        return sharded(local_blocks)(*args)

    return program
```
